32 devices in a mesh: dp: 4 (over y, x), seq: 8 (over z, core).
Axes of the slice: x: 2, y: 2, z: 4, core: 2. Of those that a mesh axis runs over, the one named last changes fastest.
Arguments:
- tokens: bfloat16 [4, 1024, 2048], P('dp', 'seq'), may hold values from -6 to 6
- teacher: bfloat16 [4, 1024, 2048], P('dp', 'seq'), may hold values from -6 to 6
- valid: int32 [4, 1024], P('dp', 'seq'), may hold values from 0 to 1, as said below
- positions: int32 [4, 1024], P('dp', 'seq'), may hold values from 0 to 1023, as said below
- norm_gain: bfloat16 [2048], replicated, may hold values from 0.5 to 1.5
- norm_bias: bfloat16 [2048], replicated, may hold values from -1 to 1
- qkv_weight: bfloat16 [2048, 6144], P('dp'), may hold values from -0.21875 to 0.21875
- qkv_bias: bfloat16 [6144], replicated, may hold values from -1 to 1
- out_weight: bfloat16 [2048, 2048], P(None, 'dp'), may hold values from -0.25 to 0.25
- out_bias: bfloat16 [2048], replicated, may hold values from -1 to 1
- up_weight: bfloat16 [2048, 8192], P('dp'), may hold values from -0.125 to 0.125
- up_bias: bfloat16 [8192], replicated, may hold values from -1 to 1
- down_weight: bfloat16 [8192, 2048], P(None, 'dp'), may hold values from -0.0625 to 0.0625
- down_bias: bfloat16 [2048], replicated, may hold values from -1 to 1
Outputs:
- loss: float32 [], replicated
- tokens_grad: float32 [4, 1024, 2048], P('dp', 'seq')
- norm_gain_grad: float32 [2048], replicated
- norm_bias_grad: float32 [2048], replicated
- qkv_weight_grad: float32 [2048, 6144], P('dp')
- qkv_bias_grad: float32 [6144], replicated
- out_weight_grad: float32 [2048, 2048], P(None, 'dp')
- out_bias_grad: float32 [2048], replicated
- up_weight_grad: float32 [2048, 8192], P('dp')
- up_bias_grad: float32 [8192], replicated
- down_weight_grad: float32 [8192, 2048], P(None, 'dp')
- down_bias_grad: float32 [2048], replicated
The draws below stay inside these ranges and needn't reach their ends.
Inputs may be any that keep to these rules, and one draw needn't show every extreme that they name: `valid`: in each sequence the last 1 to 256 positions are 0 and all others 1. `positions`: in each sequence the ids count up by one from 0 at the first position and fall back to 0 where a packed document starts; the first sequence is one document, every other holds two or more.
All inputs are finite; a program needn't handle non-finite values.
Results may differ from the reference program's by a relative error of at most 0.008.
The reference program's roundings to bfloat16 on the way count: a program that leaves them out, or rounds other values in their place, can miss the bound.
Values may be sent and summed in bfloat16 or wider, within the bound.
No kernel may reach another device: no remote copies, remote signals or barrier semaphores. Data moves between devices by JAX's collectives and lax.ppermute only.
A program may use at most 512 MiB of HBM per device.

```python
import jax
import jax.numpy as jnp
from jax import lax

WIDTH = 2048
HEADS = 32
HEAD_DIM = 64
ROTARY = 32
HIDDEN_UNITS = 8192
TOK_DEV = 128
SEQS = 4
LENGTH = 1024


def draw_valid(key, part):
    padding = jax.random.randint(key, (SEQS,), 1, 2 * TOK_DEV + 1)
    steps = jnp.arange(LENGTH, dtype=jnp.int32)
    return (steps[None, :] < LENGTH - padding[:, None]).astype(jnp.int32)


def draw_positions(key, part):
    forced_key = jax.random.fold_in(key, 11)
    rolls_key = jax.random.fold_in(key, 23)
    forced = jax.random.randint(forced_key, (SEQS,), 1, LENGTH)
    rolls = jax.random.randint(rolls_key, (SEQS, LENGTH), 0, max(4, LENGTH // 8))
    steps = jnp.broadcast_to(jnp.arange(LENGTH, dtype=jnp.int32), (SEQS, LENGTH))
    first_seq = jnp.arange(SEQS, dtype=jnp.int32)[:, None] == 0
    chosen = (rolls == 0) | (steps == forced[:, None])
    breaks = chosen & jnp.logical_not(first_seq) | (steps == 0)
    starts = jnp.where(breaks, steps, 0)
    return steps - lax.cummax(starts, axis=1)


def block_levels(key, extent, cuts, smallest, largest):
    level, own = 1.0, jax.random.fold_in(key, 6)
    for axis_at, blocks in cuts:
        draws = jnp.exp(jax.random.uniform(jax.random.fold_in(own, axis_at), (blocks,), jnp.float32, smallest / len(cuts), largest / len(cuts)))
        level = level * jnp.repeat(draws, extent[axis_at] // blocks).reshape([-1 if axis == axis_at else 1 for axis in range(len(extent))])
    return level


def scatter_about(key, extent, scale, most, shards=(), kind=jnp.bfloat16):
    drawn = scale * jax.random.normal(key, extent, jnp.float32)
    if shards:
        drawn = drawn * block_levels(key, extent, shards, -0.22, 0.18)
    return jnp.clip(drawn, -most, most).astype(kind)


def setup_inputs(seed: int = 0) -> dict:
    arg_keys = jax.random.split(jax.random.key(seed), 15)
    tokens = scatter_about(arg_keys[0], (SEQS, LENGTH, WIDTH), 1.0, 6.0, ((0, 4), (1, 8)))
    teacher = scatter_about(arg_keys[1], (SEQS, LENGTH, WIDTH), 1.0, 6.0, ((0, 4), (1, 8)))
    valid = draw_valid(jax.random.fold_in(arg_keys[14], 71), 0)
    positions = draw_positions(jax.random.fold_in(arg_keys[14], 71), 0)
    norm_gain = jnp.clip(1.0 + 0.1 * jax.random.normal(arg_keys[4], (WIDTH,), jnp.float32), 0.5, 1.5).astype(jnp.bfloat16)
    norm_bias = scatter_about(arg_keys[5], (WIDTH,), 0.2, 1.0)
    qkv_weight = scatter_about(arg_keys[6], (WIDTH, 3 * WIDTH), (2 * WIDTH // 5) ** -0.5, 0.21875, ((0, 4),))
    qkv_bias = scatter_about(arg_keys[7], (3 * WIDTH,), 0.2, 1.0)
    out_weight = scatter_about(arg_keys[8], (WIDTH, WIDTH), (WIDTH // 4) ** -0.5, 0.25, ((1, 4),))
    out_bias = scatter_about(arg_keys[9], (WIDTH,), 0.2, 1.0)
    up_weight = scatter_about(arg_keys[10], (WIDTH, HIDDEN_UNITS), WIDTH ** -0.5, 0.125, ((0, 4),))
    up_bias = scatter_about(arg_keys[11], (HIDDEN_UNITS,), 0.2, 1.0)
    down_weight = scatter_about(arg_keys[12], (HIDDEN_UNITS, WIDTH), HIDDEN_UNITS ** -0.5, 0.0625, ((1, 4),))
    down_bias = scatter_about(arg_keys[13], (WIDTH,), 0.2, 1.0)
    return {"tokens": tokens, "teacher": teacher, "valid": valid, "positions": positions, "norm_gain": norm_gain, "norm_bias": norm_bias, "qkv_weight": qkv_weight, "qkv_bias": qkv_bias, "out_weight": out_weight, "out_bias": out_bias, "up_weight": up_weight, "up_bias": up_bias, "down_weight": down_weight, "down_bias": down_bias}


@jax.custom_vjp
def low(v):
    return lax.optimization_barrier(v.astype(jnp.bfloat16)).astype(jnp.float32)

@jax.custom_vjp
def low_back(v):
    return v

def low_keep(v):
    return (low(v), None)

def low_pass(kept, grad):
    return (grad,)

def back_keep(v):
    return (v, None)

def back_low(kept, grad):
    return (low(grad),)
low.defvjp(low_keep, low_pass)
low_back.defvjp(back_keep, back_low)
norm_eps = 1e-05
rope_base = 10000.0
masked_fill = -1e+30
precise = lax.Precision.HIGHEST

def layer_norm(values, gain, shift):
    centre = values - lax.optimization_barrier(jnp.mean(values, axis=-1, keepdims=True))
    spread = lax.optimization_barrier(jnp.mean(centre * centre, axis=-1, keepdims=True))
    return centre * lax.rsqrt(spread + norm_eps) * gain + shift

def gelu_tanh(values):
    return jax.nn.gelu(values, approximate=True)

def rotate(block, where):
    half = ROTARY // 2
    freqs = rope_base ** (-(jnp.arange(half, dtype=jnp.float32) * 2.0) / ROTARY)
    angles = where.astype(jnp.float32)[:, None] * freqs[None, :]
    cosine = jnp.cos(angles)[:, None, :]
    sine = jnp.sin(angles)[:, None, :]
    first = block[..., :half]
    second = block[..., half:ROTARY]
    return jnp.concatenate([first * cosine - second * sine, second * cosine + first * sine, block[..., ROTARY:]], axis=-1)

def attention(query, keys, values):
    length = query.shape[0]
    block = min(512, length)
    scale = HEAD_DIM ** (-0.5)
    columns = jnp.arange(length, dtype=jnp.int32)

    def one_block(index):
        start = (index * block).astype(jnp.int32)
        rows = lax.dynamic_slice_in_dim(query, start, block, 0)
        raw = jnp.einsum('bhd,khd->hbk', rows, keys, precision=precise) * scale
        scores = low_back(raw)
        allowed = columns[None, None, :] <= (start + jnp.arange(block, dtype=jnp.int32))[None, :, None]
        masked = jnp.where(allowed, scores, masked_fill)
        top = lax.optimization_barrier(jnp.max(masked, axis=-1, keepdims=True))
        expd = jnp.exp(masked - top)
        probs = low(expd / lax.optimization_barrier(jnp.sum(expd, axis=-1, keepdims=True)))
        return jnp.einsum('hbk,khd->bhd', probs, values, precision=precise)
    outs = lax.map(jax.checkpoint(one_block), jnp.arange(length // block, dtype=jnp.int32))
    return outs.reshape(length, query.shape[1] * query.shape[2])

def sequence_error(params, values, target, mask, where):
    gain, shift, w_qkv, b_qkv, w_out, b_out, w_up, b_up, w_down, b_down = params
    length = values.shape[0]
    normed = low(layer_norm(values, gain, shift))
    mixed = low_back(jnp.dot(normed, w_qkv, precision=precise) + b_qkv)
    query = mixed[:, :WIDTH].reshape(length, HEADS, HEAD_DIM)
    keys = mixed[:, WIDTH:2 * WIDTH].reshape(length, HEADS, HEAD_DIM)
    value = mixed[:, 2 * WIDTH:].reshape(length, HEADS, HEAD_DIM)
    query = low_back(low(rotate(query, where)))
    keys = low_back(low(rotate(keys, where)))
    value = low_back(low(value))
    attended = low_back(low(attention(query, keys, value)))
    attn_branch = low_back(jnp.dot(attended, w_out, precision=precise) + b_out)
    hidden = low_back(jnp.dot(normed, w_up, precision=precise) + b_up)
    activated = low(gelu_tanh(hidden))
    mlp_branch = low_back(jnp.dot(activated, w_down, precision=precise) + b_down)
    output = values + attn_branch + mlp_branch
    diff = output - target
    return jnp.sum(mask[:, None] * diff * diff)

def total_error(params, values, target, mask, positions):

    def step(carry, item):
        seq_values, seq_target, seq_mask, seq_where = item
        return (carry + sequence_error(params, seq_values, seq_target, seq_mask, seq_where), None)
    total, _ = lax.scan(step, jnp.zeros((), jnp.float32), (values, target, mask, positions))
    return total

def reference(tokens, teacher, valid, positions, norm_gain, norm_bias, qkv_weight, qkv_bias, out_weight, out_bias, up_weight, up_bias, down_weight, down_bias):
    values = tokens.astype(jnp.float32)
    target = teacher.astype(jnp.float32)
    mask = valid.astype(jnp.float32)
    params = tuple((item.astype(jnp.float32) for item in (norm_gain, norm_bias, qkv_weight, qkv_bias, out_weight, out_bias, up_weight, up_bias, down_weight, down_bias)))
    count = jnp.sum(mask)

    def objective(weights, inputs):
        return total_error(weights, inputs, target, mask, positions)
    squares, pullback = jax.vjp(objective, params, values)
    loss = squares / (2.0 * WIDTH * count)
    upstream_scale = SEQS * LENGTH * 1.0 / (2.0 * count)
    param_grads, value_grad = pullback(upstream_scale)
    return (loss, value_grad, param_grads[0], param_grads[1], param_grads[2], param_grads[3], param_grads[4], param_grads[5], param_grads[6], param_grads[7], param_grads[8], param_grads[9])
```

```python
import jax
import jax.numpy as jnp
from jax import lax
from jax.sharding import PartitionSpec as P

HEADS = 32
HEAD_DIM = 64
ROTARY = 32


norm_eps = 1e-05
rope_base = 10000.0
masked_fill = -1e30


def gelu_tanh(values):
    return jax.nn.gelu(values, approximate=True)


def rotate(block, where):
    half = ROTARY // 2
    freqs = rope_base ** (-(jnp.arange(half, dtype=jnp.float32) * 2.0) / ROTARY)
    angles = where.astype(jnp.float32)[:, None] * freqs[None, :]
    cosine = jnp.cos(angles)[:, None, :]
    sine = jnp.sin(angles)[:, None, :]
    first = block[..., :half]
    second = block[..., half:ROTARY]
    return jnp.concatenate(
        [first * cosine - second * sine, second * cosine + first * sine, block[..., ROTARY:]],
        axis=-1,
    )


def causal_scores(rows, keys, start, scale):
    block = rows.shape[0]
    length = keys.shape[0]
    raw = jnp.einsum("bhd,khd->hbk", rows, keys, preferred_element_type=jnp.float32) * scale
    row_index = start + jnp.arange(block, dtype=jnp.int32)
    col_index = jnp.arange(length, dtype=jnp.int32)
    allowed = col_index[None, None, :] <= row_index[None, :, None]
    return jnp.where(allowed, raw, masked_fill)


def attend(query, keys, values, block):
    length = query.shape[0]
    scale = HEAD_DIM ** (-0.5)

    def one_block(carry, index):
        start = index * block
        rows = lax.dynamic_slice_in_dim(query, start, block, 0)
        scores = causal_scores(rows, keys, start, scale)
        top = jnp.max(scores, axis=-1, keepdims=True)
        expd = jnp.exp(scores - top)
        total = jnp.sum(expd, axis=-1, keepdims=True)
        probs = (expd / total).astype(jnp.bfloat16)
        result = jnp.einsum("hbk,khd->bhd", probs, values, preferred_element_type=jnp.float32)
        return (carry, (result, top[..., 0] + jnp.log(total[..., 0])))

    _, (outs, logsum) = lax.scan(one_block, None, jnp.arange(length // block, dtype=jnp.int32))
    return (outs.reshape(length, query.shape[1] * query.shape[2]), logsum)


def attend_back(query, keys, values, logsum, upstream_all, block):
    length = query.shape[0]
    scale = HEAD_DIM ** (-0.5)

    def one_block(carry, item):
        key_total, value_total = carry
        index, block_logsum = item
        start = index * block
        rows = lax.dynamic_slice_in_dim(query, start, block, 0)
        upstream = lax.dynamic_slice_in_dim(upstream_all, start, block, 0)
        scores = causal_scores(rows, keys, start, scale)
        probs = jnp.exp(scores - block_logsum[..., None])
        probs_low = probs.astype(jnp.bfloat16)
        prob_grad = jnp.einsum("bhd,khd->hbk", upstream, values, preferred_element_type=jnp.float32)
        inner = jnp.sum(probs * prob_grad, axis=-1, keepdims=True)
        score_grad = (probs * (prob_grad - inner)).astype(jnp.bfloat16)
        row_grad = (
            jnp.einsum("hbk,khd->bhd", score_grad, keys, preferred_element_type=jnp.float32) * scale
        )
        key_total = (
            key_total
            + jnp.einsum("hbk,bhd->khd", score_grad, rows, preferred_element_type=jnp.float32)
            * scale
        )
        value_total = value_total + jnp.einsum(
            "hbk,bhd->khd", probs_low, upstream, preferred_element_type=jnp.float32
        )
        return ((key_total, value_total), row_grad)

    zeros = jnp.zeros(keys.shape, jnp.float32)
    indices = jnp.arange(length // block, dtype=jnp.int32)
    (key_grad, value_grad), row_grads = lax.scan(one_block, (zeros, zeros), (indices, logsum))
    return (
        row_grads.reshape(length, -1),
        key_grad.reshape(length, -1),
        value_grad.reshape(length, -1),
    )


def dot(a, b, dims):
    return lax.dot_general(a, b, (dims, ((), ())), preferred_element_type=jnp.float32)


def local(
    tokens,
    teacher,
    valid,
    positions,
    norm_gain,
    norm_bias,
    qkv_weight,
    qkv_bias,
    out_weight,
    out_bias,
    up_weight,
    up_bias,
    down_weight,
    down_bias,
):
    low = jnp.bfloat16
    inputs = tokens[0].astype(jnp.float32)
    target = teacher[0].astype(jnp.float32)
    mask = valid[0].astype(jnp.float32)
    rows_here, width = inputs.shape
    seq_count = lax.axis_size("seq")
    data_count = lax.axis_size("dp")
    part = lax.axis_index("seq")
    length = rows_here * seq_count
    block = min(512, length)
    local_heads = HEADS // seq_count
    head_width = local_heads * HEAD_DIM
    units = up_weight.shape[1] // seq_count
    depth = qkv_weight.shape[0]
    gain = norm_gain.astype(jnp.float32)
    shift = norm_bias.astype(jnp.float32)

    centre = inputs - jnp.mean(inputs, axis=-1, keepdims=True)
    spread = jnp.mean(centre * centre, axis=-1, keepdims=True)
    rstd = lax.rsqrt(spread + norm_eps)
    xhat = centre * rstd
    normed_low = (xhat * gain + shift).astype(low)
    count = lax.psum(jnp.sum(mask), ("dp", "seq"))

    def my_heads(array):
        grouped = array.reshape(array.shape[:-1] + (3, seq_count, head_width))
        mine = lax.dynamic_index_in_dim(grouped, part, array.ndim, keepdims=False)
        return mine.reshape(array.shape[:-1] + (3 * head_width,))

    normed_all = lax.all_gather(normed_low, "seq", axis=0, tiled=True)
    where = lax.all_gather(positions[0], "seq", axis=0, tiled=True)
    w_in = jnp.concatenate(
        [my_heads(qkv_weight), lax.dynamic_slice_in_dim(up_weight, part * units, units, 1)], axis=1
    )
    w_back = jnp.concatenate(
        [
            lax.dynamic_slice_in_dim(out_weight, part * head_width, head_width, 0),
            lax.dynamic_slice_in_dim(down_weight, part * units, units, 0),
        ],
        axis=0,
    )
    w_in = lax.all_gather(w_in, "dp", axis=0, tiled=True)
    w_back = lax.all_gather(w_back, "dp", axis=1, tiled=True)
    b_in = jnp.concatenate(
        [my_heads(qkv_bias), lax.dynamic_slice_in_dim(up_bias, part * units, units, 0)]
    ).astype(jnp.float32)
    three = 3 * head_width

    mixed = dot(normed_all, w_in[:, :three], ((1,), (0,))) + b_in[:three]
    query_pre = mixed[:, :head_width].reshape(length, local_heads, HEAD_DIM)
    keys_pre = mixed[:, head_width : 2 * head_width].reshape(length, local_heads, HEAD_DIM)
    query, query_turn = jax.vjp(lambda part_block: rotate(part_block, where), query_pre)
    keys, keys_turn = jax.vjp(lambda part_block: rotate(part_block, where), keys_pre)
    query, keys = query.astype(low), keys.astype(low)
    values = mixed[:, 2 * head_width :].astype(low).reshape(length, local_heads, HEAD_DIM)
    attended, logsum = attend(query, keys, values, block)
    attended = attended.astype(low)

    hidden = dot(normed_all, w_in[:, three:], ((1,), (0,))) + b_in[three:]
    activated, gelu_back = jax.vjp(gelu_tanh, hidden)
    stacked = jnp.concatenate([attended, activated.astype(low)], axis=1)
    branches = dot(stacked, w_back, ((1,), (0,)))
    branches = lax.psum_scatter(branches, "seq", scatter_dimension=0, tiled=True)
    output = inputs + branches + (out_bias.astype(jnp.float32) + down_bias.astype(jnp.float32))

    weighted = mask[:, None] * (output - target)
    squares = jnp.sum(weighted * (output - target))
    grad_output = length * data_count / count * weighted
    grad_low = grad_output.astype(low)
    branch_bias_grad = jnp.sum(grad_low.astype(jnp.float32), axis=0)
    grad_all = lax.all_gather(grad_low, "seq", axis=0, tiled=True)

    back_grad = dot(stacked, grad_all, ((0,), (0,)))
    back_grad = lax.psum_scatter(back_grad, "dp", scatter_dimension=1, tiled=True).astype(low)
    back_grad = lax.all_gather(back_grad, "seq", axis=0, tiled=False)
    out_grad = back_grad[:, :head_width].reshape(-1, back_grad.shape[2])
    down_grad = back_grad[:, head_width:].reshape(-1, back_grad.shape[2])

    stacked_grad = dot(grad_all, w_back, ((1,), (1,)))
    (hidden_grad,) = gelu_back(stacked_grad[:, head_width:])
    hidden_low = hidden_grad.astype(low)
    head_grad = stacked_grad[:, :head_width].astype(low).reshape(length, local_heads, HEAD_DIM)
    query_grad, key_grad, value_grad = attend_back(query, keys, values, logsum, head_grad, block)

    def turned(turn, grad):
        grad = grad.astype(low).astype(jnp.float32).reshape(length, local_heads, HEAD_DIM)
        return turn(grad)[0].reshape(length, head_width).astype(low)

    mixed_low = jnp.concatenate(
        [turned(query_turn, query_grad), turned(keys_turn, key_grad), value_grad.astype(low)],
        axis=1,
    )
    in_low = jnp.concatenate([mixed_low, hidden_low], axis=1)
    in_grad = dot(normed_all, in_low, ((0,), (0,)))
    in_bias_grad = jnp.sum(in_low.astype(jnp.float32), axis=0)
    in_grad = lax.psum_scatter(in_grad, "dp", scatter_dimension=0, tiled=True).astype(low)
    in_grad = lax.all_gather(in_grad, "seq", axis=0, tiled=False)
    qkv_grad = (
        in_grad[:, :, :three]
        .reshape(seq_count, depth, 3, head_width)
        .transpose(1, 2, 0, 3)
        .reshape(depth, -1)
    )
    up_grad = in_grad[:, :, three:].transpose(1, 0, 2).reshape(depth, -1)

    normed_grad = dot(in_low, w_in, ((1,), (1,)))
    normed_grad = lax.psum_scatter(normed_grad, "seq", scatter_dimension=0, tiled=True)
    gain_grad = jnp.sum(normed_grad * xhat, axis=0)
    shift_grad = jnp.sum(normed_grad, axis=0)
    spread_grad = normed_grad * gain
    input_grad = rstd * (
        spread_grad
        - jnp.mean(spread_grad, axis=-1, keepdims=True)
        - xhat * jnp.mean(spread_grad * xhat, axis=-1, keepdims=True)
    )
    tokens_grad = (grad_output + input_grad)[None]

    slots = jnp.zeros((seq_count, in_bias_grad.shape[0]), jnp.float32)
    slots = lax.dynamic_update_slice_in_dim(slots, in_bias_grad[None], part, 0)
    gain_grad, shift_grad, slots, branch_bias_grad, squares = lax.psum(
        (gain_grad, shift_grad, slots, branch_bias_grad, squares), ("dp", "seq")
    )
    qkv_bias_grad = (
        slots[:, :three].reshape(seq_count, 3, head_width).transpose(1, 0, 2).reshape(-1)
    )
    up_bias_grad = slots[:, three:].reshape(-1)
    loss = squares / (2.0 * width * count)
    return (
        loss,
        tokens_grad,
        gain_grad,
        shift_grad,
        qkv_grad.astype(jnp.float32),
        qkv_bias_grad,
        out_grad.astype(jnp.float32),
        branch_bias_grad,
        up_grad.astype(jnp.float32),
        up_bias_grad,
        down_grad.astype(jnp.float32),
        branch_bias_grad,
    )


def solution(mesh):
    placed = (
        P("dp", "seq", None),
        P("dp", "seq", None),
        P("dp", "seq"),
        P("dp", "seq"),
        P(),
        P(),
        P("dp", None),
        P(),
        P(None, "dp"),
        P(),
        P("dp", None),
        P(),
        P(None, "dp"),
        P(),
    )
    return jax.shard_map(
        local,
        mesh=mesh,
        in_specs=placed,
        out_specs=(
            P(),
            P("dp", "seq", None),
            P(),
            P(),
            P("dp", None),
            P(),
            P(None, "dp"),
            P(),
            P("dp", None),
            P(),
            P(None, "dp"),
            P(),
        ),
        check_vma=False,
    )
```

```python
import functools

import jax
import jax.numpy as jnp
from jax import lax
from jax.experimental import pallas as pl
from jax.experimental.pallas import tpu as pltpu
from jax.sharding import PartitionSpec as P

HEADS = 32
HEAD_DIM = 64
ROTARY = 32


norm_eps = 1e-05
rope_base = 10000.0
masked_fill = -1e30
LANES = 128
RADIX = 64

low = jnp.bfloat16
wide = jnp.float32


def dot(a, b, dims):
    return lax.dot_general(a, b, (dims, ((), ())), preferred_element_type=wide)


def after(array, *earlier):
    return lax.optimization_barrier((array, *earlier))[0]


def swap(array, axis, bit):
    return lax.ppermute(array, axis, [(s, s ^ bit) for s in range(lax.axis_size(axis))])


def gather_dp(shard, pair):
    first, second = pair
    half = shard.shape[0] // 2
    third = [swap(first[:half], "dp", 2), swap(second[half:], "dp", 1)]
    return [shard, first, second, jnp.concatenate(third, axis=0)]


def gather_seq(rows):
    count = lax.axis_size("seq")
    near = jnp.concatenate([rows] + [swap(rows, "seq", k) for k in range(2, count, 2)], axis=0)
    return jnp.concatenate([near, swap(near, "seq", 1)], axis=0)


def scatter_seq(partial):
    count = lax.axis_size("seq")
    half = partial.shape[0] // 2
    rows = half // (count // 2)
    chip = partial[:half] + swap(partial[half:].astype(low), "seq", 1).astype(wide)
    total = chip[:rows]
    for k in range(1, count // 2):
        sent = chip[k * rows : (k + 1) * rows].astype(low)
        total = total + swap(sent, "seq", 2 * k).astype(wide)
    return total


def scatter_dp(blocks, *earlier):
    sent = [block.astype(low) for block in blocks[1:]]
    if earlier:
        sent = lax.optimization_barrier((*sent, *earlier))[: len(sent)]
    total = blocks[0]
    for k in range(1, len(blocks)):
        total = total + swap(sent[k - 1], "dp", k).astype(wide)
    return total.astype(low)


def total_dp(array):
    bit = 1
    while bit < lax.axis_size("dp"):
        array = array + swap(array, "dp", bit)
        bit *= 2
    return array


def normalise(values):
    centre = values - jnp.mean(values, axis=-1, keepdims=True)
    spread = jnp.mean(centre * centre, axis=-1, keepdims=True)
    rstd = lax.rsqrt(spread + norm_eps)
    return centre * rstd, rstd


def enter_kernel(
    owners, owner, tokens, teacher, gain, shift, bias_a, bias_b, place, normed, base, held, kept
):
    inputs = tokens[...].astype(wide)
    xhat, _ = normalise(inputs)
    held[...] = xhat * gain[...].astype(wide) + shift[...].astype(wide)
    biases = bias_a[...].astype(wide) + bias_b[...].astype(wide)
    kept[...] = inputs + biases - teacher[...].astype(wide)
    width = inputs.shape[1]
    depth = width // owners
    for k in range(owners):
        theirs = pl.ds(pl.multiple_of((owner[0] ^ k) * depth, LANES), depth)
        normed[:, k * depth : (k + 1) * depth] = held[:, theirs].astype(low)
        base[:, k * depth : (k + 1) * depth] = kept[:, theirs]
    lane = lax.broadcasted_iota(jnp.int32, (inputs.shape[0], LANES), 1)
    facts = jnp.where(lane < 2, place[...] // RADIX, place[...] % RADIX)
    counts = jnp.where(lane < 2, owner[1] // RADIX, owner[1] % RADIX)
    normed[:, width:] = jnp.where(lane % 2 == 0, facts, counts).astype(wide).astype(low)


def enter(tokens, teacher, gain, shift, bias_a, bias_b, place, owner, counted, owners):
    rows, width = tokens.shape
    whole = pl.BlockSpec(memory_space=pltpu.VMEM)
    return pl.pallas_call(
        functools.partial(enter_kernel, owners),
        in_specs=[pl.BlockSpec(memory_space=pltpu.SMEM)] + [whole] * 7,
        out_specs=[whole] * 2,
        out_shape=[
            jax.ShapeDtypeStruct((rows, width + LANES), low),
            jax.ShapeDtypeStruct((rows, width), wide),
        ],
        scratch_shapes=[pltpu.VMEM((rows, width), wide)] * 2,
        name="enter",
    )(
        jnp.stack([owner, counted]),
        tokens,
        teacher,
        gain[None],
        shift[None],
        bias_a[None],
        bias_b[None],
        place[:, None],
    )


def leave_kernel(
    owners, owner, tokens, gain, summed, grad, bias, token_grad, gain_grad, shift_grad, bias_grad
):
    inputs = tokens[...].astype(wide)
    xhat, rstd = normalise(inputs)
    depth = inputs.shape[1] // owners
    for k in range(owners):
        theirs = pl.ds(pl.multiple_of((owner[0] ^ k) * depth, LANES), depth)
        token_grad[:, theirs] = summed[:, k * depth : (k + 1) * depth]
        bias_grad[:, theirs] = bias[:, k * depth : (k + 1) * depth]
    normed_grad = token_grad[...]
    gain_grad[...] = jnp.sum(normed_grad * xhat, axis=0, keepdims=True)
    shift_grad[...] = jnp.sum(normed_grad, axis=0, keepdims=True)
    scaled = normed_grad * gain[...].astype(wide)
    token_grad[...] = rstd * (
        scaled
        - jnp.mean(scaled, axis=-1, keepdims=True)
        - xhat * jnp.mean(scaled * xhat, axis=-1, keepdims=True)
    )
    for k in range(owners):
        theirs = pl.ds(pl.multiple_of((owner[0] ^ k) * depth, LANES), depth)
        token_grad[:, theirs] += grad[:, k * depth : (k + 1) * depth]


def leave(tokens, gain, summed, grad, bias, owner, owners):
    rows, width = tokens.shape
    whole = pl.BlockSpec(memory_space=pltpu.VMEM)
    line = jax.ShapeDtypeStruct((1, width), wide)
    return pl.pallas_call(
        functools.partial(leave_kernel, owners),
        in_specs=[pl.BlockSpec(memory_space=pltpu.SMEM)] + [whole] * 5,
        out_specs=[whole] * 4,
        out_shape=[jax.ShapeDtypeStruct((rows, width), wide), line, line, line],
        name="leave",
    )(owner[None], tokens, gain[None], summed, grad, bias[None])


def pick_kernel(first, part, a_ref, b_ref, out_ref):
    piece = pl.program_id(0)

    @pl.when(piece < first)
    def _():
        out_ref[...] = a_ref[...]

    @pl.when(piece >= first)
    def _():
        out_ref[...] = b_ref[...]


def pick(a, b, part, block, first, pieces, a_map, b_map, out_map, out_shape):
    return pl.pallas_call(
        functools.partial(pick_kernel, first),
        grid_spec=pltpu.PrefetchScalarGridSpec(
            num_scalar_prefetch=1,
            grid=(pieces,),
            in_specs=[
                pl.BlockSpec(block, lambda p, part: a_map(jnp.minimum(p, first - 1), part[0])),
                pl.BlockSpec(block, lambda p, part: b_map(jnp.maximum(p - first, 0), part[0])),
            ],
            out_specs=pl.BlockSpec(block, lambda p, part: out_map(p)),
        ),
        out_shape=jax.ShapeDtypeStruct(out_shape, a.dtype),
        name="pick",
    )(part[None], a, b)


def gelu_parts(values):
    root = (2.0 / jnp.pi) ** 0.5
    square = values * values
    bent = jnp.tanh(root * (values + 0.044715 * (values * square)))
    factor = 0.5 * (1.0 + bent)
    slope = 0.5 * values * (1.0 - bent * bent) * (root * (1.0 + 3.0 * 0.044715 * square))
    return factor, factor + slope


def turn(values, cosine, sine):
    lane = lax.broadcasted_iota(jnp.int32, values.shape, 1) % HEAD_DIM
    half, width = ROTARY // 2, values.shape[1]
    partner = jnp.where(
        lane < half, pltpu.roll(values, width - half, 1), pltpu.roll(values, half, 1)
    )
    return values * cosine + partner * sine


def project_kernel(count, normed, cosine, sine, bias, *refs):
    weights, (qkv, hidden, stacked) = refs[:count], refs[count:]
    tile = pl.program_id(0)
    depth = weights[0].shape[0]
    total = jnp.dot(normed[:, :depth], weights[0][...], preferred_element_type=wide)
    for k in range(1, count):
        block = normed[:, k * depth : (k + 1) * depth]
        total = total + jnp.dot(block, weights[k][...], preferred_element_type=wide)
    total = total + bias[...]
    repeats = total.shape[1] // LANES

    @pl.when(tile < 2)
    def _():
        turned = turn(
            total,
            jnp.concatenate([cosine[...]] * repeats, axis=1),
            jnp.concatenate([sine[...]] * repeats, axis=1),
        )
        qkv[...] = turned.astype(low)

    @pl.when(tile == 2)
    def _():
        qkv[...] = total.astype(low)

    @pl.when(tile > 2)
    def _():
        hidden[...] = total
        stacked[...] = (total * gelu_parts(total)[0]).astype(low)


def project(normed, cosine, sine, bias, weights, head_width):
    count = len(weights)
    length = normed.shape[0]
    depth, inside = weights[0].shape
    units = inside - 3 * head_width
    table = pl.BlockSpec((length, LANES), lambda t: (0, 0))
    return pl.pallas_call(
        functools.partial(project_kernel, count),
        grid=(inside // head_width,),
        in_specs=[
            pl.BlockSpec(normed.shape, lambda t: (0, 0)),
            table,
            table,
            pl.BlockSpec((1, head_width), lambda t: (0, t)),
        ]
        + [pl.BlockSpec((depth, head_width), lambda t: (0, t))] * count,
        out_specs=[
            pl.BlockSpec((length, head_width), lambda t: (0, jnp.minimum(t, 2))),
            pl.BlockSpec((length, head_width), lambda t: (0, jnp.maximum(t - 3, 0))),
            pl.BlockSpec((length, head_width), lambda t: (0, jnp.maximum(t - 2, 1))),
        ],
        out_shape=[
            jax.ShapeDtypeStruct((length, 3 * head_width), low),
            jax.ShapeDtypeStruct((length, units), wide),
            jax.ShapeDtypeStruct((length, head_width + units), low),
        ],
        cost_estimate=pl.CostEstimate(
            flops=2 * length * count * depth * inside,
            bytes_accessed=2 * (count * depth * inside + normed.size) + 8 * length * inside,
            transcendentals=length * units,
        ),
        name="project",
    )(normed, cosine, sine, bias, *weights)


def slot_of(block, part, chips):
    apart = block ^ part
    return (apart % 2) * chips + apart // 2


def scores_of(rows, keys, start):
    raw = lax.dot_general(rows, keys, (((1,), (1,)), ((), ())), preferred_element_type=wide)
    place = start + lax.broadcasted_iota(jnp.int32, raw.shape, 0)
    kept = lax.broadcasted_iota(jnp.int32, raw.shape, 1) <= place
    return jnp.where(kept, raw * HEAD_DIM ** (-0.5), masked_fill)


def attend_kernel(chips, step, part, qkv, stacked, out, logsum, held, result):
    del stacked
    length, head_width = out.shape
    rows = length // (2 * chips)
    for n in range(2 * chips):
        source = pl.ds(pl.multiple_of(slot_of(n, part[0], chips) * rows, rows), rows)
        held[n * rows : (n + 1) * rows, :] = qkv[source, :]
    lane = lax.broadcasted_iota(jnp.int32, (step, LANES), 1)
    for first in range(0, length, step):
        last = first + step
        sums = jnp.zeros((step, LANES), wide)
        outs = []
        for h in range(head_width // HEAD_DIM):
            a, b = h * HEAD_DIM, (h + 1) * HEAD_DIM
            keys = held[:last, head_width + a : head_width + b]
            values = held[:last, 2 * head_width + a : 2 * head_width + b]
            scores = scores_of(held[first:last, a:b], keys, first)
            top = jnp.max(scores, axis=-1, keepdims=True)
            expd = jnp.exp(scores - top)
            total = jnp.sum(expd, axis=-1, keepdims=True)
            probs = (expd * (1.0 / total)).astype(low)
            outs.append(jnp.dot(probs, values, preferred_element_type=wide))
            sums = jnp.where(lane == h, top + jnp.log(total), sums)
        result[first:last, :] = jnp.concatenate(outs, axis=1).astype(low)
        logsum[first:last, :] = sums
    for n in range(2 * chips):
        target = pl.ds(pl.multiple_of(slot_of(n, part[0], chips) * rows, rows), rows)
        out[target, :] = result[n * rows : (n + 1) * rows, :]


def attend(qkv, stacked, part, chips):
    length, three = qkv.shape
    head_width = three // 3
    heads = head_width // HEAD_DIM
    whole = pl.BlockSpec(memory_space=pltpu.VMEM)
    return pl.pallas_call(
        functools.partial(attend_kernel, chips, min(256, length)),
        grid=(1,),
        in_specs=[
            pl.BlockSpec(memory_space=pltpu.SMEM),
            whole,
            pl.BlockSpec(memory_space=pl.ANY),
        ],
        out_specs=[pl.BlockSpec((length, head_width), lambda n: (0, 0)), whole],
        out_shape=[
            jax.ShapeDtypeStruct(stacked.shape, low),
            jax.ShapeDtypeStruct((length, LANES), wide),
        ],
        scratch_shapes=[pltpu.VMEM((length, three), low), pltpu.VMEM((length, head_width), low)],
        input_output_aliases={2: 0},
        cost_estimate=pl.CostEstimate(
            flops=4 * heads * length * length * LANES,
            bytes_accessed=8 * length * three,
            transcendentals=heads * length * length,
        ),
        name="attend",
    )(part[None], qkv, stacked)


def attend_back_kernel(
    chips, step, part, qkv, grad, logsum, cosine, sine, entered, out, held, given, gone
):
    del entered
    length, head_width = grad.shape
    rows = length // (2 * chips)
    scale = HEAD_DIM ** (-0.5)
    for n in range(2 * chips):
        source = pl.ds(pl.multiple_of(slot_of(n, part[0], chips) * rows, rows), rows)
        held[n * rows : (n + 1) * rows, :] = qkv[source, :]
        given[n * rows : (n + 1) * rows, :] = grad[source, :]
    over_rows = (((0,), (0,)), ((), ()))
    for first in reversed(range(0, length, step)):
        last = first + step
        parts = [[], [], []]
        for h in range(head_width // HEAD_DIM):
            a, b = h * HEAD_DIM, (h + 1) * HEAD_DIM
            query = held[first:last, a:b]
            keys = held[:last, head_width + a : head_width + b]
            values = held[:last, 2 * head_width + a : 2 * head_width + b]
            upstream = given[first:last, a:b]
            probs = jnp.exp(scores_of(query, keys, first) - logsum[first:last, h : h + 1])
            prob_grad = lax.dot_general(
                upstream, values, (((1,), (1,)), ((), ())), preferred_element_type=wide
            )
            inner = jnp.sum(probs * prob_grad, axis=-1, keepdims=True)
            score_grad = (probs * (prob_grad - inner)).astype(low)
            parts[0].append(jnp.dot(score_grad, keys, preferred_element_type=wide) * scale)
            parts[1].append(
                lax.dot_general(score_grad, query, over_rows, preferred_element_type=wide) * scale
            )
            parts[2].append(
                lax.dot_general(
                    probs.astype(low), upstream, over_rows, preferred_element_type=wide
                )
            )
        parts = [jnp.concatenate(part_list, axis=1) for part_list in parts]
        gone[first:last, :head_width] = parts[0]
        for t in (1, 2):
            columns = slice(t * head_width, (t + 1) * head_width)
            if last == length:
                gone[:, columns] = parts[t]
            else:
                gone[:last, columns] += parts[t]
    repeats = head_width // LANES
    for n in range(2 * chips):
        target = pl.ds(pl.multiple_of(slot_of(n, part[0], chips) * rows, rows), rows)
        here = slice(n * rows, (n + 1) * rows)
        ahead = jnp.concatenate([cosine[target, :]] * repeats, axis=1)
        aside = -jnp.concatenate([sine[target, :]] * repeats, axis=1)
        for t in range(3):
            columns = slice(t * head_width, (t + 1) * head_width)
            value = gone[here, columns].astype(low)
            if t < 2:
                value = turn(value.astype(wide), ahead, aside).astype(low)
            out[target, columns] = value


def attend_back(qkv, grad, logsum, cosine, sine, entered, part, chips):
    length, three = qkv.shape
    head_width = three // 3
    heads = head_width // HEAD_DIM
    whole = pl.BlockSpec(memory_space=pltpu.VMEM)
    return pl.pallas_call(
        functools.partial(attend_back_kernel, chips, min(256, length)),
        grid=(1,),
        in_specs=[pl.BlockSpec(memory_space=pltpu.SMEM)]
        + [whole] * 5
        + [pl.BlockSpec(memory_space=pl.ANY)],
        out_specs=pl.BlockSpec((length, three), lambda n: (0, 0)),
        out_shape=jax.ShapeDtypeStruct(entered.shape, low),
        scratch_shapes=[
            pltpu.VMEM((length, three), low),
            pltpu.VMEM((length, head_width), low),
            pltpu.VMEM((length, three), wide),
        ],
        input_output_aliases={6: 0},
        cost_estimate=pl.CostEstimate(
            flops=10 * heads * length * length * LANES,
            bytes_accessed=8 * length * three,
            transcendentals=heads * length * length,
        ),
        name="attend_back",
    )(part[None], qkv, grad, logsum, cosine, sine, entered)


def reject_kernel(count, hidden, *refs):
    grads, weights = refs[:count], refs[count : 2 * count]
    head_grad, entered = refs[2 * count :]
    over = (((1,), (1,)), ((), ()))
    total = lax.dot_general(grads[0][...], weights[0][...], over, preferred_element_type=wide)
    for k in range(1, count):
        total = total + lax.dot_general(
            grads[k][...], weights[k][...], over, preferred_element_type=wide
        )

    @pl.when(pl.program_id(0) == 0)
    def _():
        head_grad[...] = total.astype(low)

    @pl.when(pl.program_id(0) > 0)
    def _():
        entered[...] = (total * gelu_parts(hidden[...])[1]).astype(low)


def reject(grads, weights, hidden, head_width):
    count = len(grads)
    length, depth = grads[0].shape
    behind = weights[0].shape[0]
    inside = behind + 2 * head_width
    return pl.pallas_call(
        functools.partial(reject_kernel, count),
        grid=(behind // head_width,),
        in_specs=[pl.BlockSpec((length, head_width), lambda t: (0, jnp.maximum(t - 1, 0)))]
        + [pl.BlockSpec((length, depth), lambda t: (0, 0))] * count
        + [pl.BlockSpec((head_width, depth), lambda t: (t, 0))] * count,
        out_specs=[
            pl.BlockSpec((length, head_width), lambda t: (0, 0)),
            pl.BlockSpec((length, head_width), lambda t: (0, jnp.maximum(t + 2, 3))),
        ],
        out_shape=[
            jax.ShapeDtypeStruct((length, head_width), low),
            jax.ShapeDtypeStruct((length, inside), low),
        ],
        cost_estimate=pl.CostEstimate(
            flops=2 * length * count * depth * behind,
            bytes_accessed=2 * count * depth * (behind + length) + 8 * length * behind,
            transcendentals=length * behind,
        ),
        name="reject",
    )(hidden, *grads, *weights)


def widen_kernel(*refs):
    refs[-1][...] = refs[0][0].astype(wide)


def widen(gathered, shape, block_shape, grid, source, target, into=None):
    in_specs = [pl.BlockSpec((1, *block_shape), lambda j, p: (j, *source(p)))]
    operands = [gathered]
    if into is not None:
        in_specs.append(pl.BlockSpec(memory_space=pl.ANY))
        operands.append(into)
    moved = 6 * grid[0] * grid[1] * block_shape[0] * block_shape[1]
    return pl.pallas_call(
        widen_kernel,
        grid=grid,
        in_specs=in_specs,
        out_specs=pl.BlockSpec(block_shape, target),
        out_shape=jax.ShapeDtypeStruct(shape, wide),
        input_output_aliases={} if into is None else {1: 0},
        cost_estimate=pl.CostEstimate(flops=0, bytes_accessed=moved, transcendentals=0),
        name="widen",
    )(*operands)


def local(
    tokens,
    teacher,
    valid,
    positions,
    norm_gain,
    norm_bias,
    qkv_weight,
    qkv_bias,
    out_weight,
    out_bias,
    up_weight,
    up_bias,
    down_weight,
    down_bias,
):
    rows_here, width = tokens.shape[1:]
    seq_count = lax.axis_size("seq")
    data_count = lax.axis_size("dp")
    part = lax.axis_index("seq")
    owner = lax.axis_index("dp")
    length = rows_here * seq_count
    chips = seq_count // 2
    head_width = HEADS // seq_count * HEAD_DIM
    three = 3 * head_width
    units = up_weight.shape[1] // seq_count
    inside = three + units
    depth = qkv_weight.shape[0]
    chunks = units // head_width
    mask = valid[0].astype(wide)

    counted = total_dp(jnp.sum(valid[0]).reshape(1, 1))
    normed_low, base = enter(
        tokens[0],
        teacher[0],
        norm_gain,
        norm_bias,
        out_bias,
        down_bias,
        positions[0],
        owner,
        counted[0, 0],
        data_count,
    )

    w_in = pick(
        qkv_weight,
        up_weight,
        part,
        (depth, head_width),
        3,
        3 + chunks,
        lambda p, part: (0, p * seq_count + part),
        lambda p, part: (0, part * chunks + p),
        lambda p: (0, p),
        (depth, inside),
    )
    w_back = pick(
        out_weight,
        down_weight,
        after(part, normed_low),
        (head_width, depth),
        1,
        1 + chunks,
        lambda p, part: (part, 0),
        lambda p, part: (part * chunks + p, 0),
        lambda p: (p, 0),
        (head_width + units, depth),
    )
    in_sent = after(w_in, counted)
    if data_count == 4:
        in_pair = (swap(in_sent, "dp", 1), swap(in_sent, "dp", 2))
        *in_pair, back_sent = lax.optimization_barrier((*in_pair, w_back))
        back_pair = (swap(back_sent, "dp", 1), swap(back_sent, "dp", 2))
        w_in = gather_dp(w_in, in_pair)
        w_back = gather_dp(w_back, back_pair)
    else:
        w_in = [w_in] + [swap(in_sent, "dp", k) for k in range(1, data_count)]
        w_back = [w_back] + [swap(w_back, "dp", k) for k in range(1, data_count)]
    normed_all = gather_seq(normed_low)
    facts = normed_all[:, width : width + 4].astype(jnp.int32)
    where = facts[:, 0] * RADIX + facts[:, 2]
    count = jnp.sum((facts[:, 1] * RADIX + facts[:, 3])[::rows_here]).astype(wide)

    half = ROTARY // 2
    lane = jnp.arange(LANES, dtype=jnp.int32) % HEAD_DIM
    freqs = rope_base ** (-((lane % half).astype(wide) * 2.0) / ROTARY)
    angles = where.astype(wide)[:, None] * jnp.where(lane < ROTARY, freqs, 0.0)[None, :]
    cosine = jnp.cos(angles)
    sine = jnp.sin(angles) * jnp.where(lane < half, -1.0, 1.0)[None, :]

    b_in = jnp.concatenate(
        [
            lax.dynamic_slice_in_dim(qkv_bias, t * width + part * head_width, head_width, 0)
            for t in range(3)
        ]
        + [lax.dynamic_slice_in_dim(up_bias, part * units, units, 0)]
    ).astype(wide)[None]

    def piece(k):
        return normed_all[:, k * depth : (k + 1) * depth]

    qkv, hidden, stacked = project(normed_all, cosine, sine, b_in, w_in, head_width)
    stacked, logsum = attend(qkv, stacked, part, chips)

    if data_count == 4:
        groups = [[0], [1, 2], [3]]
    else:
        groups = [[k] for k in range(data_count)]
    scale = length * data_count / count
    squares = jnp.zeros((), wide)
    grad_output, grad_all = [], []
    for group in groups:
        branches = jnp.concatenate([dot(stacked, w_back[k], ((1,), (0,))) for k in group], axis=1)
        error = base[:, group[0] * depth : (group[-1] + 1) * depth] + scatter_seq(branches)
        weighted = mask[:, None] * error
        squares = squares + jnp.sum(weighted * error)
        grad_output.append(scale * weighted)
        gathered = gather_seq((scale * weighted).astype(low))
        grad_all += [gathered[:, n * depth : (n + 1) * depth] for n in range(len(group))]
    grad_output = jnp.concatenate(grad_output, axis=1)
    branch_bias_grad = jnp.concatenate([jnp.sum(item.astype(wide), axis=0) for item in grad_all])

    def owned(left, right):
        return dot(left, right, ((0,), (0,)))

    cut = units // 4

    def of_stacked(first, last):
        return [owned(stacked[:, first:last], grad) for grad in grad_all]

    down_a = scatter_dp(of_stacked(head_width, head_width + cut))
    down_b = scatter_dp(of_stacked(head_width + cut, head_width + units), down_a)

    head_grad, in_low = reject(grad_all, w_back, hidden, head_width)
    hidden_low = in_low[:, three:]
    up_grad = scatter_dp([owned(piece(k), hidden_low) for k in range(data_count)], down_b)

    head_grad = after(head_grad, down_b)
    in_low = attend_back(qkv, head_grad, logsum, cosine, sine, in_low, part, chips)
    in_low = after(in_low, up_grad)
    mixed_low = in_low[:, :three]
    qkv_grad = scatter_dp([owned(piece(k), mixed_low) for k in range(data_count)], up_grad)
    out_grad = scatter_dp(of_stacked(0, head_width), qkv_grad)

    normed_grad = jnp.concatenate(
        [dot(in_low, w_in[k], ((1,), (1,))) for k in range(data_count)], axis=1
    )
    token_grad, gain_grad, shift_grad, branch_bias_grad = leave(
        tokens[0],
        norm_gain,
        scatter_seq(normed_grad),
        grad_output,
        branch_bias_grad,
        owner,
        data_count,
    )

    in_bias = jnp.sum(in_low.astype(wide), axis=0)
    small = jnp.concatenate(
        [in_bias, gain_grad[0], shift_grad[0], squares[None], branch_bias_grad[0]]
    )
    small = total_dp(small[None])[0]
    branch_bias_grad = small[-width:]
    small = small[:-width]
    lines = -(-small.size // depth)
    lines += -lines % 8
    high = jnp.pad(small, (0, lines * depth - small.size)).reshape(lines, depth)
    first = lax.reduce_precision(high, 8, 7)
    beside = jnp.concatenate([first.astype(low), (high - first).astype(low)])

    def gather(array):
        return lax.all_gather(array, "seq", axis=0, tiled=False)

    down_a, down_b = gather(down_a), gather(down_b)
    all_units = seq_count * units
    down_weight_grad = widen(
        down_a,
        (all_units, depth),
        (cut, depth),
        (seq_count, 1),
        lambda p: (p, 0),
        lambda j, p: (4 * j, 0),
    )
    down_weight_grad = widen(
        down_b,
        (all_units, depth),
        (cut, depth),
        (seq_count, 3),
        lambda p: (p, 0),
        lambda j, p: (4 * j + 1 + p, 0),
        down_weight_grad,
    )
    up_all = gather(after(up_grad, down_a))
    qkv_all = gather(after(qkv_grad, down_weight_grad))
    up_weight_grad = widen(
        up_all,
        (depth, all_units),
        (depth, units),
        (seq_count, 1),
        lambda p: (0, 0),
        lambda j, p: (0, j),
    )
    qkv_weight_grad = widen(
        qkv_all,
        (depth, 3 * width),
        (depth, head_width),
        (seq_count, 3),
        lambda p: (0, p),
        lambda j, p: (0, p * seq_count + j),
    )
    beside = after(jnp.concatenate([out_grad, beside], axis=0), up_weight_grad)
    out_all = gather(beside)
    out_weight_grad = widen(
        out_all,
        (width, depth),
        (head_width, depth),
        (seq_count, 1),
        lambda p: (0, 0),
        lambda j, p: (j, 0),
    )
    slots = out_all[:, head_width:].astype(wide)
    slots = (slots[:, :lines] + slots[:, lines:]).reshape(seq_count, -1)
    norm_grads = jnp.sum(slots[:, inside : inside + 2 * width + 1], axis=0)
    qkv_bias_grad = slots[:, :three].reshape(seq_count, 3, head_width).transpose(1, 0, 2)
    up_bias_grad = slots[:, three:inside].reshape(-1)
    loss = norm_grads[-1] / (2.0 * width * count)
    return (
        loss,
        token_grad[None],
        norm_grads[:width],
        norm_grads[width : 2 * width],
        qkv_weight_grad,
        qkv_bias_grad.reshape(-1),
        out_weight_grad,
        branch_bias_grad,
        up_weight_grad,
        up_bias_grad,
        down_weight_grad,
        branch_bias_grad,
    )


def solution(mesh):
    placed = (
        P("dp", "seq", None),
        P("dp", "seq", None),
        P("dp", "seq"),
        P("dp", "seq"),
        P(),
        P(),
        P("dp", None),
        P(),
        P(None, "dp"),
        P(),
        P("dp", None),
        P(),
        P(None, "dp"),
        P(),
    )
    return jax.shard_map(
        local,
        mesh=mesh,
        in_specs=placed,
        out_specs=(
            P(),
            P("dp", "seq", None),
            P(),
            P(),
            P("dp", None),
            P(),
            P(None, "dp"),
            P(),
            P("dp", None),
            P(),
            P(None, "dp"),
            P(),
        ),
        check_vma=False,
    )
```

```python
import functools

import jax
import jax.numpy as jnp
from jax import lax
from jax.experimental import pallas as pl
from jax.experimental.pallas import tpu as pltpu
from jax.sharding import PartitionSpec as P

HEADS = 32
HEAD_DIM = 64
ROTARY = 32


norm_eps = 1e-05
rope_base = 10000.0
masked_fill = -1e30
LANES = 128
RADIX = 64
DIGIT = 16
SPARE = 16
ROWS = 64

low = jnp.bfloat16
wide = jnp.float32


def dot(a, b, dims):
    return lax.dot_general(a, b, (dims, ((), ())), preferred_element_type=wide)


def after(array, *earlier):
    return lax.optimization_barrier((array, *earlier))[0]


def swap(array, axis, bit):
    return lax.ppermute(array, axis, [(s, s ^ bit) for s in range(lax.axis_size(axis))])


def gather_seq(rows):
    return lax.all_gather(rows, "seq", axis=0, tiled=True)


def between(array, pairs):
    return lax.ppermute(
        array, "seq", [(2 * a + core, 2 * b + core) for a, b in pairs for core in range(2)]
    )


def scatter_chips(blocks):
    chips = len(blocks)
    if chips != 4:
        total = blocks[0]
        for k in range(1, chips):
            total = total + swap(blocks[k].astype(low), "seq", 2 * k).astype(wide)
        return total
    chip = lax.axis_index("seq") // 2
    far = between(blocks[3].astype(low), [(0, 1), (3, 2)])
    passed = (blocks[2] + far.astype(wide)).astype(low)
    upward = between(passed, [(0, 1), (1, 2)])
    downward = between(passed, [(3, 2), (2, 1)])
    upward = jnp.where(chip == 1, blocks[3], blocks[1]) + upward.astype(wide)
    downward = jnp.where(chip == 2, blocks[3], blocks[1]) + downward.astype(wide)
    upward = between(upward.astype(low), [(0, 1), (1, 2), (2, 3)])
    downward = between(downward.astype(low), [(3, 2), (2, 1), (1, 0)])
    return blocks[0] + upward.astype(wide) + downward.astype(wide)


def scatter_blocks(kept, sent):
    chips = lax.axis_size("seq") // 2
    rows = kept.shape[0] // chips
    chip = kept + swap(sent, "seq", 1).astype(wide)
    return scatter_chips([chip[k * rows : (k + 1) * rows] for k in range(chips)])


def scatter_seq(partial):
    return lax.psum_scatter(partial, "seq", scatter_dimension=0, tiled=True).astype(wide)


def total_dp(array):
    bit = 1
    while bit < lax.axis_size("dp"):
        array = array + swap(array, "dp", bit)
        bit *= 2
    return array


def normalise(values):
    centre = values - jnp.mean(values, axis=-1, keepdims=True)
    spread = jnp.mean(centre * centre, axis=-1, keepdims=True)
    rstd = lax.rsqrt(spread + norm_eps)
    return centre * rstd, rstd


def enter_kernel(
    owners, owner, tokens, teacher, gain, shift, bias_a, bias_b, place, normed, base, held, kept
):
    inputs = tokens[...].astype(wide)
    xhat, _ = normalise(inputs)
    held[...] = xhat * gain[...].astype(wide)[None] + shift[...].astype(wide)[None]
    biases = (bias_a[...].astype(wide) + bias_b[...].astype(wide))[None]
    kept[...] = inputs + biases - teacher[...].astype(wide)
    width = inputs.shape[1]
    depth = width // owners
    for k in range(owners):
        theirs = pl.ds(pl.multiple_of((owner[0] ^ k) * depth, LANES), depth)
        normed[:, k * depth : (k + 1) * depth] = held[:, theirs].astype(low)
        base[:, k * depth : (k + 1) * depth] = kept[:, theirs]
    lane = lax.broadcasted_iota(jnp.int32, (inputs.shape[0], LANES), 1)
    row = lax.broadcasted_iota(jnp.int32, (inputs.shape[0], inputs.shape[0]), 0)
    column = lax.broadcasted_iota(jnp.int32, row.shape, 1)
    ids = jnp.sum(
        jnp.where(row == column, place[...].astype(wide), 0.0), axis=1, keepdims=True
    ).astype(jnp.int32)
    facts = jnp.where(lane == 0, ids // RADIX, ids % RADIX)
    normed[:, width:] = facts.astype(wide).astype(low)


def enter(tokens, teacher, gain, shift, bias_a, bias_b, place, owner, owners):
    rows, width = tokens.shape
    whole = pl.BlockSpec(memory_space=pltpu.VMEM)
    return pl.pallas_call(
        functools.partial(enter_kernel, owners),
        in_specs=[pl.BlockSpec(memory_space=pltpu.SMEM)] + [whole] * 7,
        out_specs=[whole] * 2,
        out_shape=[
            jax.ShapeDtypeStruct((rows, width + LANES), low),
            jax.ShapeDtypeStruct((rows, width), wide),
        ],
        scratch_shapes=[pltpu.VMEM((rows, width), wide)] * 2,
        name="enter",
    )(
        owner[None],
        tokens,
        teacher,
        gain,
        shift,
        bias_a,
        bias_b,
        place,
    )


def leave_kernel(
    owners, owner, tokens, gain, summed, grad, bias, token_grad, gain_grad, shift_grad, bias_grad
):
    inputs = tokens[...].astype(wide)
    xhat, rstd = normalise(inputs)
    depth = inputs.shape[1] // owners
    for k in range(owners):
        theirs = pl.ds(pl.multiple_of((owner[0] ^ k) * depth, LANES), depth)
        token_grad[:, theirs] = summed[:, k * depth : (k + 1) * depth]
        bias_grad[:, theirs] = bias[:, k * depth : (k + 1) * depth]
    normed_grad = token_grad[...]
    gain_grad[...] = jnp.sum(normed_grad * xhat, axis=0, keepdims=True)
    shift_grad[...] = jnp.sum(normed_grad, axis=0, keepdims=True)
    scaled = normed_grad * gain[...].astype(wide)[None]
    token_grad[...] = rstd * (
        scaled
        - jnp.mean(scaled, axis=-1, keepdims=True)
        - xhat * jnp.mean(scaled * xhat, axis=-1, keepdims=True)
    )
    for k in range(owners):
        theirs = pl.ds(pl.multiple_of((owner[0] ^ k) * depth, LANES), depth)
        token_grad[:, theirs] += grad[:, k * depth : (k + 1) * depth]


def leave(tokens, gain, summed, grad, bias, owner, owners):
    rows, width = tokens.shape
    whole = pl.BlockSpec(memory_space=pltpu.VMEM)
    line = jax.ShapeDtypeStruct((1, width), wide)
    return pl.pallas_call(
        functools.partial(leave_kernel, owners),
        in_specs=[pl.BlockSpec(memory_space=pltpu.SMEM)] + [whole] * 5,
        out_specs=[whole] * 4,
        out_shape=[jax.ShapeDtypeStruct((rows, width), wide), line, line, line],
        name="leave",
    )(owner[None], tokens, gain, summed, grad, bias[None])


def pick_kernel(moves, part, counted, a, b, *refs):
    outs, arrived = refs[:2], refs[2]
    copies = []
    for which, source, half, target in moves:
        copies.append(
            pltpu.make_async_copy(
                (a, b)[which].at[source(part[0])],
                outs[half].at[target],
                arrived.at[len(copies)],
            )
        )
    for copy in copies:
        copy.start()
    tall = outs[0].shape[0]
    more = outs[1].shape[0] - tall
    if more:
        count = jnp.sum(counted[...].astype(wide), axis=1, keepdims=True)
        outs[1][tall:, :] = jnp.broadcast_to(count, (more, outs[1].shape[1])).astype(low)
    for copy in copies:
        copy.wait()


def pick(arrays, part, counted, moves, shapes):
    moved = 4 * sum(shape[0] * shape[1] for shape in shapes)
    return pl.pallas_call(
        functools.partial(pick_kernel, moves),
        in_specs=[
            pl.BlockSpec(memory_space=pltpu.SMEM),
            pl.BlockSpec(memory_space=pltpu.VMEM),
        ]
        + [pl.BlockSpec(memory_space=pl.ANY)] * 2,
        out_specs=[pl.BlockSpec(memory_space=pltpu.VMEM)] * 2,
        out_shape=[jax.ShapeDtypeStruct(shape, low) for shape in shapes],
        scratch_shapes=[pltpu.SemaphoreType.DMA((len(moves),))],
        cost_estimate=pl.CostEstimate(flops=0, bytes_accessed=moved, transcendentals=0),
        name="pick",
    )(part, counted, *arrays)


def gelu_parts(values):
    root = (2.0 / jnp.pi) ** 0.5
    square = values * values
    bent = jnp.tanh(root * (values + 0.044715 * (values * square)))
    factor = 0.5 * (1.0 + bent)
    slope = 0.5 * values * (1.0 - bent * bent) * (root * (1.0 + 3.0 * 0.044715 * square))
    return factor, factor + slope


def turn(values, cosine, sine):
    lane = lax.broadcasted_iota(jnp.int32, values.shape, 1) % HEAD_DIM
    half, width = ROTARY // 2, values.shape[1]
    partner = jnp.where(
        lane < half, pltpu.roll(values, width - half, 1), pltpu.roll(values, half, 1)
    )
    return values * cosine + partner * sine


def begin_kernel(count, normed, bias, *refs):
    weights, out = refs[:count], refs[count]
    tall = normed.shape[1] // count
    total = bias[...] + jnp.dot(normed[:, :tall], weights[0][...], preferred_element_type=wide)
    for k in range(1, count):
        block = normed[:, k * tall : (k + 1) * tall]
        total = total + jnp.dot(block, weights[k][...], preferred_element_type=wide)
    out[...] = total


def begin(normed, bias, weights, tall, head_width):
    count = len(weights)
    length = normed.shape[0]
    inside = weights[0].shape[1]
    return pl.pallas_call(
        functools.partial(begin_kernel, count),
        grid=(inside // head_width,),
        in_specs=[
            pl.BlockSpec((length, count * tall), lambda t: (0, 0)),
            pl.BlockSpec((1, head_width), lambda t: (0, t)),
        ]
        + [pl.BlockSpec((tall, head_width), lambda t: (0, t))] * count,
        out_specs=pl.BlockSpec((length, head_width), lambda t: (0, t)),
        out_shape=jax.ShapeDtypeStruct((length, inside), wide),
        cost_estimate=pl.CostEstimate(
            flops=2 * length * count * tall * inside,
            bytes_accessed=2 * (count * tall * inside + normed.size) + 4 * length * inside,
            transcendentals=0,
        ),
        name="begin",
    )(normed, bias, *weights)


def project_kernel(normed, other, cosine, sine, begun, weights, others, qkv, hidden, stacked):
    tile = pl.program_id(0)
    total = begun[...] + jnp.dot(normed[...], weights[...], preferred_element_type=wide)
    total = total + jnp.dot(other[...], others[...], preferred_element_type=wide)
    repeats = total.shape[1] // LANES

    @pl.when(tile < 2)
    def _():
        turned = turn(
            total,
            jnp.concatenate([cosine[...]] * repeats, axis=1),
            jnp.concatenate([sine[...]] * repeats, axis=1),
        )
        qkv[...] = turned.astype(low)

    @pl.when(tile == 2)
    def _():
        qkv[...] = total.astype(low)

    @pl.when(tile > 2)
    def _():
        hidden[...] = total
        stacked[...] = (total * gelu_parts(total)[0]).astype(low)


def project(normed, cosine, sine, begun, halves, tall, head_width):
    length = normed.shape[0]
    inside = begun.shape[1]
    units = inside - 3 * head_width
    first = 2 * (normed.shape[1] // (2 * tall)) - 2
    table = pl.BlockSpec((length, LANES), lambda t: (0, 0))
    weights, others = halves
    return pl.pallas_call(
        project_kernel,
        grid=(inside // head_width,),
        in_specs=[
            pl.BlockSpec((length, tall), lambda t: (0, first)),
            pl.BlockSpec((length, tall), lambda t: (0, first + 1)),
            table,
            table,
            pl.BlockSpec((length, head_width), lambda t: (0, t)),
            pl.BlockSpec((tall, head_width), lambda t: (0, t)),
            pl.BlockSpec((tall, head_width), lambda t: (0, t)),
        ],
        out_specs=[
            pl.BlockSpec((length, head_width), lambda t: (0, jnp.minimum(t, 2))),
            pl.BlockSpec((length, head_width), lambda t: (0, jnp.maximum(t - 3, 0))),
            pl.BlockSpec((length, head_width), lambda t: (0, jnp.maximum(t - 2, 1))),
        ],
        out_shape=[
            jax.ShapeDtypeStruct((length, 3 * head_width), low),
            jax.ShapeDtypeStruct((length, units), wide),
            jax.ShapeDtypeStruct((length, head_width + units), low),
        ],
        cost_estimate=pl.CostEstimate(
            flops=4 * length * tall * inside,
            bytes_accessed=4 * tall * (inside + length) + 12 * length * inside,
            transcendentals=length * units,
        ),
        name="project",
    )(normed, normed, cosine, sine, begun, weights, others)


def emit_kernel(owners, counts, stacked, *refs):
    counted, refs = refs[:counts], refs[counts:]
    weights, out = refs[: 2 * owners], refs[-1]
    middle = weights[0].shape[0]
    for k in range(owners):

        @pl.when(pl.program_id(0) // 2 == k)
        def _(k=k):
            total = jnp.dot(
                stacked[:, :middle], weights[2 * k][...], preferred_element_type=wide
            ) + jnp.dot(stacked[:, middle:], weights[2 * k + 1][...], preferred_element_type=wide)
            out[...] = total.astype(low)

    if not counted:
        return

    @pl.when(pl.program_id(0) == 2 * owners)
    def _():
        count = counted[0][...].astype(wide)
        for ref in counted[1:]:
            count = count + ref[...].astype(wide)
        count = count[:1].astype(jnp.int32)
        lane = lax.broadcasted_iota(jnp.int32, count.shape, 1)
        digits = jnp.where(lane == 0, count, count // DIGIT)
        digits = jnp.where(lane == 2, count // (DIGIT * DIGIT), digits) % DIGIT
        out[:, :LANES] = jnp.broadcast_to(digits.astype(wide), (out.shape[0], LANES)).astype(low)


def emit(stacked, weights, counted, first, all_owners, into=None):
    owners = len(weights)
    length, behind = stacked.shape
    middle, depth = weights[0][0].shape
    size = depth // 2
    steps = 2 * owners + (first + owners == all_owners)

    def at(k):
        return pl.BlockSpec((middle, size), lambda t: (0, jnp.clip(t - 2 * k, 0, 1)))

    row = size // SPARE
    operands = [stacked, *counted, *[item for pair in weights for item in pair]]
    in_specs = [pl.BlockSpec((length, behind), lambda t: (0, 0))]
    in_specs += [pl.BlockSpec((SPARE, LANES), lambda t: (row, 0))] * len(counted)
    in_specs += [at(k) for k in range(owners) for _ in range(2)]
    aliases = {}
    if into is not None:
        aliases = {len(operands): 0}
        operands.append(into)
        in_specs.append(pl.BlockSpec(memory_space=pl.ANY))
    return pl.pallas_call(
        functools.partial(emit_kernel, owners, len(counted)),
        grid=(steps,),
        in_specs=in_specs,
        out_specs=pl.BlockSpec((length, size), lambda t: (0, 2 * first + t)),
        out_shape=jax.ShapeDtypeStruct((length, all_owners * depth + LANES), low),
        input_output_aliases=aliases,
        cost_estimate=pl.CostEstimate(
            flops=2 * length * behind * owners * depth,
            bytes_accessed=2 * behind * (length + owners * depth) + 2 * length * steps * size,
            transcendentals=0,
        ),
        name="emit",
    )(*operands)


def scores_of(rows, keys, start):
    raw = lax.dot_general(rows, keys, (((1,), (1,)), ((), ())), preferred_element_type=wide)
    place = start + lax.broadcasted_iota(jnp.int32, raw.shape, 0)
    kept = lax.broadcasted_iota(jnp.int32, raw.shape, 1) <= place
    return jnp.where(kept, raw * HEAD_DIM ** (-0.5), masked_fill)


def attend_kernel(step, qkv, stacked, out, logsum):
    del stacked
    length, head_width = out.shape
    lane = lax.broadcasted_iota(jnp.int32, (step, LANES), 1)
    for first in range(0, length, step):
        last = first + step
        sums = jnp.zeros((step, LANES), wide)
        outs = []
        for h in range(head_width // HEAD_DIM):
            a, b = h * HEAD_DIM, (h + 1) * HEAD_DIM
            keys = qkv[:last, head_width + a : head_width + b]
            values = qkv[:last, 2 * head_width + a : 2 * head_width + b]
            scores = scores_of(qkv[first:last, a:b], keys, first)
            top = jnp.max(scores, axis=-1, keepdims=True)
            expd = jnp.exp(scores - top)
            total = jnp.sum(expd, axis=-1, keepdims=True)
            probs = (expd * (1.0 / total)).astype(low)
            outs.append(jnp.dot(probs, values, preferred_element_type=wide))
            sums = jnp.where(lane == h, top + jnp.log(total), sums)
        out[first:last, :] = jnp.concatenate(outs, axis=1).astype(low)
        logsum[first:last, :] = sums


def attend(qkv, stacked):
    length, three = qkv.shape
    head_width = three // 3
    heads = head_width // HEAD_DIM
    whole = pl.BlockSpec(memory_space=pltpu.VMEM)
    return pl.pallas_call(
        functools.partial(attend_kernel, min(256, length)),
        grid=(1,),
        in_specs=[whole, pl.BlockSpec(memory_space=pl.ANY)],
        out_specs=[pl.BlockSpec((length, head_width), lambda n: (0, 0)), whole],
        out_shape=[
            jax.ShapeDtypeStruct(stacked.shape, low),
            jax.ShapeDtypeStruct((length, LANES), wide),
        ],
        input_output_aliases={1: 0},
        cost_estimate=pl.CostEstimate(
            flops=4 * heads * length * length * LANES,
            bytes_accessed=8 * length * three,
            transcendentals=heads * length * length,
        ),
        name="attend",
    )(qkv, stacked)


def attend_back_kernel(step, qkv, grad, logsum, cosine, sine, entered, out, gone):
    del entered
    length, head_width = grad.shape
    scale = HEAD_DIM ** (-0.5)
    over_rows = (((0,), (0,)), ((), ()))
    for first in reversed(range(0, length, step)):
        last = first + step
        parts = [[], [], []]
        for h in range(head_width // HEAD_DIM):
            a, b = h * HEAD_DIM, (h + 1) * HEAD_DIM
            query = qkv[first:last, a:b]
            keys = qkv[:last, head_width + a : head_width + b]
            values = qkv[:last, 2 * head_width + a : 2 * head_width + b]
            upstream = grad[first:last, a:b]
            probs = jnp.exp(scores_of(query, keys, first) - logsum[first:last, h : h + 1])
            prob_grad = lax.dot_general(
                upstream, values, (((1,), (1,)), ((), ())), preferred_element_type=wide
            )
            inner = jnp.sum(probs * prob_grad, axis=-1, keepdims=True)
            score_grad = (probs * (prob_grad - inner)).astype(low)
            parts[0].append(jnp.dot(score_grad, keys, preferred_element_type=wide) * scale)
            parts[1].append(
                lax.dot_general(score_grad, query, over_rows, preferred_element_type=wide) * scale
            )
            parts[2].append(
                lax.dot_general(
                    probs.astype(low), upstream, over_rows, preferred_element_type=wide
                )
            )
        parts = [jnp.concatenate(part_list, axis=1) for part_list in parts]
        gone[first:last, :head_width] = parts[0]
        for t in (1, 2):
            columns = slice(t * head_width, (t + 1) * head_width)
            if last == length:
                gone[:, columns] = parts[t]
            else:
                gone[:last, columns] += parts[t]
    repeats = head_width // LANES
    for first in range(0, length, step):
        here = slice(first, first + step)
        ahead = jnp.concatenate([cosine[here, :]] * repeats, axis=1)
        aside = -jnp.concatenate([sine[here, :]] * repeats, axis=1)
        for t in range(3):
            columns = slice(t * head_width, (t + 1) * head_width)
            value = gone[here, columns].astype(low)
            if t < 2:
                value = turn(value.astype(wide), ahead, aside).astype(low)
            out[here, columns] = value


def attend_back(qkv, grad, logsum, cosine, sine, entered):
    length, three = qkv.shape
    head_width = three // 3
    heads = head_width // HEAD_DIM
    whole = pl.BlockSpec(memory_space=pltpu.VMEM)
    return pl.pallas_call(
        functools.partial(attend_back_kernel, min(256, length)),
        grid=(1,),
        in_specs=[whole] * 5 + [pl.BlockSpec(memory_space=pl.ANY)],
        out_specs=pl.BlockSpec((length, three), lambda n: (0, 0)),
        out_shape=jax.ShapeDtypeStruct(entered.shape, low),
        scratch_shapes=[
            pltpu.VMEM((length, three), wide),
        ],
        input_output_aliases={5: 0},
        cost_estimate=pl.CostEstimate(
            flops=10 * heads * length * length * LANES,
            bytes_accessed=8 * length * three,
            transcendentals=heads * length * length,
        ),
        name="attend_back",
    )(qkv, grad, logsum, cosine, sine, entered)


def reject_kernel(count, hidden, grads, *refs):
    weights, (head_grad, entered) = refs[:count], refs[count:]
    depth = weights[0].shape[1]
    over = (((1,), (1,)), ((), ()))
    total = lax.dot_general(grads[:, :depth], weights[0][...], over, preferred_element_type=wide)
    for k in range(1, count):
        total = total + lax.dot_general(
            grads[:, k * depth : (k + 1) * depth],
            weights[k][...],
            over,
            preferred_element_type=wide,
        )

    @pl.when(pl.program_id(0) == 0)
    def _():
        head_grad[...] = total.astype(low)

    @pl.when(pl.program_id(0) > 0)
    def _():
        entered[...] = (total * gelu_parts(hidden[...])[1]).astype(low)


def reject(grads, weights, hidden, head_width):
    count = len(weights)
    length = grads.shape[0]
    behind, depth = weights[0].shape
    inside = behind + 2 * head_width
    return pl.pallas_call(
        functools.partial(reject_kernel, count),
        grid=(behind // head_width,),
        in_specs=[pl.BlockSpec((length, head_width), lambda t: (0, jnp.maximum(t - 1, 0)))]
        + [pl.BlockSpec((length, count * depth), lambda t: (0, 0))]
        + [pl.BlockSpec((head_width, depth), lambda t: (t, 0))] * count,
        out_specs=[
            pl.BlockSpec((length, head_width), lambda t: (0, 0)),
            pl.BlockSpec((length, head_width), lambda t: (0, jnp.maximum(t + 2, 3))),
        ],
        out_shape=[
            jax.ShapeDtypeStruct((length, head_width), low),
            jax.ShapeDtypeStruct((length, inside), low),
        ],
        cost_estimate=pl.CostEstimate(
            flops=2 * length * count * depth * behind,
            bytes_accessed=2 * count * depth * (behind + length) + 8 * length * behind,
            transcendentals=length * behind,
        ),
        name="reject",
    )(hidden, grads, *weights)


def answer_kernel(count, chips, part, entered, *refs):
    weights, (kept, sent, held) = refs[:count], refs[count:]
    rows = kept.shape[0] // chips
    over = (((1,), (1,)), ((), ()))
    for n in range(count):

        @pl.when(pl.program_id(0) == n)
        def _(n=n):
            held[...] = lax.dot_general(
                entered[...], weights[n][...], over, preferred_element_type=wide
            )

    for k in range(chips):
        here = slice(k * rows, (k + 1) * rows)
        for core, out in enumerate((kept, sent)):
            block = part[0] ^ (2 * k + core)
            source = pl.ds(pl.multiple_of(block * rows, rows), rows)
            out[here, :] = held[source, :].astype(out.dtype)


def answer(entered, pieces, part, chips, tall):
    count = len(pieces)
    length, inside = entered.shape
    half = length // 2
    return pl.pallas_call(
        functools.partial(answer_kernel, count, chips),
        grid=(count,),
        in_specs=[
            pl.BlockSpec(memory_space=pltpu.SMEM),
            pl.BlockSpec((length, inside), lambda t: (0, 0)),
        ]
        + [pl.BlockSpec((tall, inside), lambda t: (0, 0))] * count,
        out_specs=[pl.BlockSpec((half, tall), lambda t: (0, t))] * 2,
        out_shape=[
            jax.ShapeDtypeStruct((half, count * tall), wide),
            jax.ShapeDtypeStruct((half, count * tall), low),
        ],
        scratch_shapes=[pltpu.VMEM((length, tall), wide)],
        cost_estimate=pl.CostEstimate(
            flops=2 * length * inside * count * tall,
            bytes_accessed=2 * inside * (length + count * tall) + 3 * length * count * tall,
            transcendentals=0,
        ),
        name="answer",
    )(part[None], entered, *pieces)


def widen_rows_kernel(head_width, a, b, down, out):
    cut = a.shape[1]
    out[...] = b[0, :head_width].astype(wide)
    down[:cut] = b[0, head_width:].astype(wide)
    down[cut:] = a[0].astype(wide)


def widen_rows(all_a, all_b, head_width, width):
    count, cut, depth = all_a.shape
    assert head_width + cut == all_b.shape[1]
    moved = 6 * count * depth * (head_width + 2 * cut)
    return pl.pallas_call(
        functools.partial(widen_rows_kernel, head_width),
        grid=(count,),
        in_specs=[
            pl.BlockSpec((1, cut, depth), lambda j: (j, 0, 0)),
            pl.BlockSpec((1, head_width + cut, depth), lambda j: (j, 0, 0)),
        ],
        out_specs=[
            pl.BlockSpec((2 * cut, depth), lambda j: (j, 0)),
            pl.BlockSpec((head_width, depth), lambda j: (j, 0)),
        ],
        out_shape=[
            jax.ShapeDtypeStruct((count * 2 * cut, depth), wide),
            jax.ShapeDtypeStruct((width, depth), wide),
        ],
        cost_estimate=pl.CostEstimate(flops=0, bytes_accessed=moved, transcendentals=0),
        name="widen_rows",
    )(all_a, all_b)


def widen_columns_kernel(groups, gathered, out):
    count, _, columns = gathered.shape
    size = columns // groups
    for j in range(count):
        for g in range(groups):
            at = (g * count + j) * size
            out[:, at : at + size] = gathered[j, :, g * size : (g + 1) * size].astype(wide)


def widen_columns(gathered, rows, groups):
    count, _, columns = gathered.shape
    tall = min(64, rows)
    moved = 6 * count * rows * columns
    return pl.pallas_call(
        functools.partial(widen_columns_kernel, groups),
        grid=(rows // tall,),
        in_specs=[pl.BlockSpec((count, tall, columns), lambda r: (0, r, 0))],
        out_specs=pl.BlockSpec((tall, count * columns), lambda r: (r, 0)),
        out_shape=jax.ShapeDtypeStruct((rows, count * columns), wide),
        cost_estimate=pl.CostEstimate(flops=0, bytes_accessed=moved, transcendentals=0),
        name="widen_columns",
    )(gathered)


def local(
    tokens,
    teacher,
    valid,
    positions,
    norm_gain,
    norm_bias,
    qkv_weight,
    qkv_bias,
    out_weight,
    out_bias,
    up_weight,
    up_bias,
    down_weight,
    down_bias,
):
    rows_here, width = tokens.shape[1:]
    seq_count = lax.axis_size("seq")
    data_count = lax.axis_size("dp")
    part = lax.axis_index("seq")
    owner = lax.axis_index("dp")
    length = rows_here * seq_count
    head_width = HEADS // seq_count * HEAD_DIM
    three = 3 * head_width
    units = up_weight.shape[1] // seq_count
    inside = three + units
    depth = qkv_weight.shape[0]
    mask = valid[0].astype(wide)

    tall = depth // 2
    behind = head_width + units

    def span(start, size, unit):
        return pl.ds(start if isinstance(start, int) else pl.multiple_of(start, unit), size)

    def block_at(row, rows, column, columns):
        return span(row, rows, ROWS), span(column, columns, LANES)

    moves = []
    for half in range(2):
        for t in range(3):
            moves.append(
                (
                    0,
                    lambda part, t=t, half=half: block_at(
                        half * tall, tall, t * width + part * head_width, head_width
                    ),
                    half,
                    block_at(0, tall, t * head_width, head_width),
                )
            )
        moves.append(
            (
                1,
                lambda part, half=half: block_at(half * tall, tall, part * units, units),
                half,
                block_at(0, tall, three, units),
            )
        )
    w_in = pick(
        (qkv_weight, up_weight),
        part[None],
        valid,
        moves,
        [(tall, inside), (tall + SPARE, inside)],
    )
    normed_low, base = enter(
        tokens[0],
        teacher[0],
        norm_gain,
        norm_bias,
        out_bias,
        down_bias,
        positions,
        after(owner, *w_in),
        data_count,
    )

    rest = behind // 2 - head_width
    moves = [
        (
            0,
            lambda part: block_at(part * head_width, head_width, 0, depth),
            0,
            block_at(0, head_width, 0, depth),
        ),
        (
            1,
            lambda part: block_at(part * units, rest, 0, depth),
            0,
            block_at(head_width, rest, 0, depth),
        ),
        (
            1,
            lambda part: block_at(part * units + rest, units - rest, 0, depth),
            1,
            block_at(0, units - rest, 0, depth),
        ),
    ]
    w_back = pick(
        (out_weight, down_weight),
        after(part[None], normed_low),
        valid,
        moves,
        [(behind // 2, depth)] * 2,
    )
    if data_count == 4:
        sides = [tuple(swap(item, "dp", k) for item in w_in) for k in (1, 2)]
        last_in = swap(sides[0][0], "dp", 2), swap(sides[1][1], "dp", 1)
        first_in = [w_in, *sides]
        w_back = lax.optimization_barrier((*w_back, *last_in))[:2]
        back_sides = [tuple(swap(item, "dp", k) for item in w_back) for k in (1, 2)]
    else:
        w_in = [w_in] + [tuple(swap(item, "dp", k) for item in w_in) for k in range(1, data_count)]
        w_back = [w_back] + [
            tuple(swap(item, "dp", k) for item in w_back) for k in range(1, data_count)
        ]
        first_in, last_in = w_in[:-1], w_in[-1]
    normed_all = gather_seq(normed_low)
    facts = normed_all[:, width : width + 2].astype(jnp.int32)
    where = facts[:, 0] * RADIX + facts[:, 1]

    half = ROTARY // 2
    lane = jnp.arange(LANES, dtype=jnp.int32) % HEAD_DIM
    freqs = rope_base ** (-((lane % half).astype(wide) * 2.0) / ROTARY)
    angles = where.astype(wide)[:, None] * jnp.where(lane < ROTARY, freqs, 0.0)[None, :]
    cosine = jnp.cos(angles)
    sine = jnp.sin(angles) * jnp.where(lane < half, -1.0, 1.0)[None, :]

    b_in = jnp.concatenate(
        [
            lax.dynamic_slice_in_dim(qkv_bias, t * width + part * head_width, head_width, 0)
            for t in range(3)
        ]
        + [lax.dynamic_slice_in_dim(up_bias, part * units, units, 0)]
    ).astype(wide)[None]

    def piece(array, k):
        return array[:, k * depth : (k + 1) * depth]

    flat_in = [item for pair in first_in for item in pair]
    begun = begin(normed_all, b_in, flat_in, tall, head_width)
    begun, cosine, sine = lax.optimization_barrier((begun, cosine, sine))
    qkv, hidden, stacked = project(normed_all, cosine, sine, begun, last_in, tall, head_width)
    stacked, logsum = attend(qkv, stacked)

    counted = [item[1] for item in (*first_in, last_in)]
    if data_count == 4:
        back_sides = [tuple(after(item, qkv) for item in pair) for pair in back_sides]
        w_back = [w_back, *back_sides]
        w_back.append((swap(back_sides[0][0], "dp", 2), swap(back_sides[1][1], "dp", 1)))
    branches = emit(stacked, w_back[:-1], [], 0, data_count)
    branches = emit(stacked, w_back[-1:], counted, data_count - 1, data_count, branches)
    branches = scatter_seq(branches)
    digits = branches[0, width : width + 3]
    count = digits[0] + DIGIT * digits[1] + DIGIT * DIGIT * digits[2]
    error = base + branches[:, :width]
    weighted = mask[:, None] * error
    squares = jnp.sum(weighted * error)
    grad_output = length * data_count / count * weighted
    grad_all = gather_seq(grad_output.astype(low))
    branch_bias_grad = jnp.sum(grad_all.astype(wide), axis=0)
    w_back = [jnp.concatenate(pair, axis=0) for pair in w_back]

    def owned(left, right):
        return dot(left, right, ((0,), (0,)))

    def gather(array):
        return lax.all_gather(array, "seq", axis=0, tiled=False)

    cut = units // 2

    def of_stacked(first, last):
        return [owned(stacked[:, first:last], piece(grad_all, k)) for k in range(data_count)]

    def of_normed(right):
        return [owned(piece(normed_all, k), right) for k in range(data_count)]

    def prepare(pieces):
        return pieces[0], [item.astype(low) for item in pieces[1:]]

    def send(sent, *meanwhile):
        got = [swap(item, "dp", k + 1) for k, item in enumerate(sent)]
        held = lax.optimization_barrier((*got, *jax.tree.leaves(meanwhile)))
        return held[: len(got)], jax.tree.unflatten(jax.tree.structure(meanwhile), held[len(got) :])

    def total(own, got):
        for item in got:
            own = own + item.astype(wide)
        return own.astype(low)

    own_a, sent_a = prepare(of_stacked(head_width + cut, head_width + units))
    own_b, sent_b = prepare(of_stacked(0, head_width + cut))
    head_grad, in_low = reject(grad_all, w_back, hidden, head_width)
    got, ((own_b, sent_b), head_grad, in_low) = send(
        sent_a, (own_b, sent_b), head_grad, in_low
    )
    down_a = total(own_a, got)
    all_a = gather(down_a)
    own_up, sent_up = prepare(of_normed(in_low[:, three:]))
    got, ((own_up, sent_up), head_grad) = send(sent_b, (own_up, sent_up), head_grad)
    down_b = total(own_b, got)
    all_b = gather(down_b)
    head_grad = after(head_grad, down_b)
    in_low = attend_back(qkv, head_grad, logsum, cosine, sine, in_low)
    own_qkv, sent_qkv = prepare(of_normed(in_low[:, :three]))
    kept, sent = answer(in_low, [*flat_in, *last_in], part, seq_count // 2, tall)
    got, ((own_qkv, sent_qkv), kept, sent, all_a) = send(
        sent_up, (own_qkv, sent_qkv), kept, sent, all_a
    )
    up_grad = total(own_up, got)
    all_up = gather(up_grad)
    summed = scatter_blocks(kept, sent)
    got, (summed, all_b) = send(sent_qkv, summed, all_b)
    qkv_grad = total(own_qkv, got)
    token_grad, gain_grad, shift_grad, branch_bias_grad = leave(
        tokens[0],
        norm_gain,
        summed,
        grad_output,
        branch_bias_grad,
        owner,
        data_count,
    )

    in_bias = jnp.sum(in_low.astype(wide), axis=0)
    small = jnp.concatenate(
        [in_bias, gain_grad[0], shift_grad[0], squares[None], branch_bias_grad[0]]
    )
    small = total_dp(small[None])[0]
    branch_bias_grad = small[-width:]
    small = small[:-width]
    lines = -(-small.size // three)
    lines += -lines % 8
    high = jnp.pad(small, (0, lines * three - small.size)).reshape(lines, three)
    first = lax.reduce_precision(high, 8, 7)
    beside = jnp.concatenate([qkv_grad, first.astype(low), (high - first).astype(low)])

    down_weight_grad, out_weight_grad = widen_rows(all_a, all_b, head_width, width)
    all_qkv = gather(after(beside, all_up))
    up_weight_grad = widen_columns(all_up, depth, 1)
    all_qkv = after(all_qkv, down_weight_grad, up_weight_grad)
    qkv_weight_grad = widen_columns(all_qkv, depth, 3)
    slots = all_qkv[:, depth:].astype(wide)
    slots = (slots[:, :lines] + slots[:, lines:]).reshape(seq_count, -1)
    norm_grads = jnp.sum(slots[:, inside : inside + 2 * width + 1], axis=0)
    qkv_bias_grad = slots[:, :three].reshape(seq_count, 3, head_width).transpose(1, 0, 2)
    up_bias_grad = slots[:, three:inside].reshape(-1)
    loss = norm_grads[-1] / (2.0 * width * count)
    return (
        loss,
        token_grad[None],
        norm_grads[:width],
        norm_grads[width : 2 * width],
        qkv_weight_grad,
        qkv_bias_grad.reshape(-1),
        out_weight_grad,
        branch_bias_grad,
        up_weight_grad,
        up_bias_grad,
        down_weight_grad,
        branch_bias_grad,
    )


def solution(mesh):
    placed = (
        P("dp", "seq", None),
        P("dp", "seq", None),
        P("dp", "seq"),
        P("dp", "seq"),
        P(),
        P(),
        P("dp", None),
        P(),
        P(None, "dp"),
        P(),
        P("dp", None),
        P(),
        P(None, "dp"),
        P(),
    )
    return jax.shard_map(
        local,
        mesh=mesh,
        in_specs=placed,
        out_specs=(
            P(),
            P("dp", "seq", None),
            P(),
            P(),
            P("dp", None),
            P(),
            P(None, "dp"),
            P(),
            P("dp", None),
            P(),
            P(None, "dp"),
            P(),
        ),
        check_vma=False,
    )
```

```python
import functools

import jax
import jax.numpy as jnp
from jax import lax
from jax.experimental import pallas as pl
from jax.experimental.pallas import tpu as pltpu
from jax.sharding import PartitionSpec as P

HEADS = 32
HEAD_DIM = 64
ROTARY = 32


norm_eps = 1e-05
rope_base = 10000.0
masked_fill = -1e30
LANES = 128
RADIX = 64
DIGIT = 16
SPARE = 16
ROWS = 64

low = jnp.bfloat16
wide = jnp.float32


def dot(a, b, dims):
    return lax.dot_general(a, b, (dims, ((), ())), preferred_element_type=wide)


def after(array, *earlier):
    return lax.optimization_barrier((array, *earlier))[0]


def swap(array, axis, bit):
    return lax.ppermute(array, axis, [(s, s ^ bit) for s in range(lax.axis_size(axis))])


def gather_seq(rows):
    return lax.all_gather(rows, "seq", axis=0, tiled=True)


def between(array, pairs):
    return lax.ppermute(
        array, "seq", [(2 * a + core, 2 * b + core) for a, b in pairs for core in range(2)]
    )


def scatter_chips(blocks):
    chips = len(blocks)
    if chips != 4:
        total = blocks[0]
        for k in range(1, chips):
            total = total + swap(blocks[k].astype(low), "seq", 2 * k).astype(wide)
        return total
    chip = lax.axis_index("seq") // 2
    far = between(blocks[3].astype(low), [(0, 1), (3, 2)])
    passed = (blocks[2] + far.astype(wide)).astype(low)
    upward = between(passed, [(0, 1), (1, 2)])
    downward = between(passed, [(3, 2), (2, 1)])
    upward = jnp.where(chip == 1, blocks[3], blocks[1]) + upward.astype(wide)
    downward = jnp.where(chip == 2, blocks[3], blocks[1]) + downward.astype(wide)
    upward = between(upward.astype(low), [(0, 1), (1, 2), (2, 3)])
    downward = between(downward.astype(low), [(3, 2), (2, 1), (1, 0)])
    return blocks[0] + upward.astype(wide) + downward.astype(wide)


def scatter_blocks(kept, sent):
    chips = lax.axis_size("seq") // 2
    rows = kept.shape[0] // chips
    chip = kept + swap(sent, "seq", 1).astype(wide)
    return scatter_chips([chip[k * rows : (k + 1) * rows] for k in range(chips)])


def scatter_seq(partial):
    return lax.psum_scatter(partial, "seq", scatter_dimension=0, tiled=True)


def total_dp(array):
    items = [array] + [swap(array, "dp", k) for k in range(1, lax.axis_size("dp"))]
    while len(items) > 1:
        items = [a + b for a, b in zip(items[::2], items[1::2])]
    return items[0]


def normalise(values):
    centre = values - jnp.mean(values, axis=-1, keepdims=True)
    spread = jnp.mean(centre * centre, axis=-1, keepdims=True)
    rstd = lax.rsqrt(spread + norm_eps)
    return centre * rstd, rstd


def enter_kernel(
    owners, owner, tokens, teacher, gain, shift, bias_a, bias_b, place, normed, base, held, kept
):
    inputs = tokens[...].astype(wide)
    xhat, _ = normalise(inputs)
    held[...] = xhat * gain[...].astype(wide)[None] + shift[...].astype(wide)[None]
    biases = (bias_a[...].astype(wide) + bias_b[...].astype(wide))[None]
    kept[...] = inputs + biases - teacher[...].astype(wide)
    width = inputs.shape[1]
    depth = width // owners
    for k in range(owners):
        theirs = pl.ds(pl.multiple_of((owner[0] ^ k) * depth, LANES), depth)
        normed[:, k * depth : (k + 1) * depth] = held[:, theirs].astype(low)
        base[:, k * depth : (k + 1) * depth] = kept[:, theirs]
    lane = lax.broadcasted_iota(jnp.int32, (inputs.shape[0], LANES), 1)
    ids = column_of(place[...]).astype(jnp.int32)
    facts = jnp.where(lane == 0, ids // RADIX, ids % RADIX)
    normed[:, width:] = facts.astype(wide).astype(low)


def enter(tokens, teacher, gain, shift, bias_a, bias_b, place, owner, owners):
    rows, width = tokens.shape
    whole = pl.BlockSpec(memory_space=pltpu.VMEM)
    return pl.pallas_call(
        functools.partial(enter_kernel, owners),
        in_specs=[pl.BlockSpec(memory_space=pltpu.SMEM)] + [whole] * 7,
        out_specs=[whole] * 2,
        out_shape=[
            jax.ShapeDtypeStruct((rows, width + LANES), low),
            jax.ShapeDtypeStruct((rows, width), wide),
        ],
        scratch_shapes=[pltpu.VMEM((rows, width), wide)] * 2,
        name="enter",
    )(
        owner[None],
        tokens,
        teacher,
        gain,
        shift,
        bias_a,
        bias_b,
        place,
    )


def column_of(row):
    size = row.shape[1]
    here = lax.broadcasted_iota(jnp.int32, (size, size), 0)
    there = lax.broadcasted_iota(jnp.int32, (size, size), 1)
    return jnp.sum(jnp.where(here == there, row.astype(wide), 0.0), axis=1, keepdims=True)


def grade_kernel(scale, branches, base, valid, grad, grad_low, sums):
    width = base.shape[1]
    lane = lax.broadcasted_iota(jnp.int32, (1, LANES), 1)
    weight = jnp.where(lane == 1, float(DIGIT), jnp.where(lane == 2, float(DIGIT * DIGIT), 1.0))
    digits = jnp.where(lane < 3, branches[:1, width:].astype(wide) * weight, 0.0)
    count = jnp.sum(digits, axis=1, keepdims=True)
    error = base[...] + branches[:, :width].astype(wide)
    weighted = column_of(valid[...]) * error
    squares = jnp.sum(jnp.sum(weighted * error, axis=0, keepdims=True), axis=1, keepdims=True)
    result = scale / count * weighted
    grad[...] = result
    grad_low[...] = result.astype(low)
    line = lax.broadcasted_iota(jnp.int32, sums.shape, 0)
    sums[...] = jnp.where(line == 0, squares, count)


def grade(branches, base, valid, scale):
    whole = pl.BlockSpec(memory_space=pltpu.VMEM)
    return pl.pallas_call(
        functools.partial(grade_kernel, scale),
        in_specs=[whole] * 3,
        out_specs=[whole] * 3,
        out_shape=[
            jax.ShapeDtypeStruct(base.shape, wide),
            jax.ShapeDtypeStruct(base.shape, low),
            jax.ShapeDtypeStruct((8, LANES), wide),
        ],
        cost_estimate=pl.CostEstimate(
            flops=4 * base.size, bytes_accessed=12 * base.size, transcendentals=0
        ),
        name="grade",
    )(branches, base, valid)


def leave_kernel(
    owners, owner, tokens, gain, summed, grad, bias, token_grad, gain_grad, shift_grad, bias_grad
):
    inputs = tokens[...].astype(wide)
    xhat, rstd = normalise(inputs)
    depth = inputs.shape[1] // owners
    for k in range(owners):
        theirs = pl.ds(pl.multiple_of((owner[0] ^ k) * depth, LANES), depth)
        token_grad[:, theirs] = summed[:, k * depth : (k + 1) * depth]
        bias_grad[:, theirs] = bias[:, k * depth : (k + 1) * depth]
    normed_grad = token_grad[...]
    gain_grad[...] = jnp.sum(normed_grad * xhat, axis=0, keepdims=True)
    shift_grad[...] = jnp.sum(normed_grad, axis=0, keepdims=True)
    scaled = normed_grad * gain[...].astype(wide)[None]
    token_grad[...] = rstd * (
        scaled
        - jnp.mean(scaled, axis=-1, keepdims=True)
        - xhat * jnp.mean(scaled * xhat, axis=-1, keepdims=True)
    )
    for k in range(owners):
        theirs = pl.ds(pl.multiple_of((owner[0] ^ k) * depth, LANES), depth)
        token_grad[:, theirs] += grad[:, k * depth : (k + 1) * depth]


def leave(tokens, gain, summed, grad, bias, owner, owners):
    rows, width = tokens.shape
    whole = pl.BlockSpec(memory_space=pltpu.VMEM)
    line = jax.ShapeDtypeStruct((1, width), wide)
    return pl.pallas_call(
        functools.partial(leave_kernel, owners),
        in_specs=[pl.BlockSpec(memory_space=pltpu.SMEM)] + [whole] * 5,
        out_specs=[whole] * 4,
        out_shape=[jax.ShapeDtypeStruct((rows, width), wide), line, line, line],
        name="leave",
    )(owner[None], tokens, gain, summed, grad, bias[None])


def pick_kernel(moves, part, counted, a, b, *refs):
    outs, arrived = refs[:2], refs[2]
    copies = []
    for which, source, half, target in moves:
        copies.append(
            pltpu.make_async_copy(
                (a, b)[which].at[source(part[0])],
                outs[half].at[target],
                arrived.at[len(copies)],
            )
        )
    for copy in copies:
        copy.start()
    tall = outs[0].shape[0]
    more = outs[1].shape[0] - tall
    if more:
        count = jnp.sum(counted[...].astype(wide), axis=1, keepdims=True)
        outs[1][tall:, :] = jnp.broadcast_to(count, (more, outs[1].shape[1])).astype(low)
    for copy in copies:
        copy.wait()


def pick(arrays, part, counted, moves, shapes):
    moved = 4 * sum(shape[0] * shape[1] for shape in shapes)
    return pl.pallas_call(
        functools.partial(pick_kernel, moves),
        in_specs=[
            pl.BlockSpec(memory_space=pltpu.SMEM),
            pl.BlockSpec(memory_space=pltpu.VMEM),
        ]
        + [pl.BlockSpec(memory_space=pl.ANY)] * 2,
        out_specs=[pl.BlockSpec(memory_space=pltpu.VMEM)] * 2,
        out_shape=[jax.ShapeDtypeStruct(shape, low) for shape in shapes],
        scratch_shapes=[pltpu.SemaphoreType.DMA((len(moves),))],
        cost_estimate=pl.CostEstimate(flops=0, bytes_accessed=moved, transcendentals=0),
        name="pick",
    )(part, counted, *arrays)


def gelu_parts(values):
    root = (2.0 / jnp.pi) ** 0.5
    square = values * values
    bent = jnp.tanh(root * (values + 0.044715 * (values * square)))
    factor = 0.5 * (1.0 + bent)
    slope = 0.5 * values * (1.0 - bent * bent) * (root * (1.0 + 3.0 * 0.044715 * square))
    return factor, factor + slope


def turn(values, cosine, sine):
    lane = lax.broadcasted_iota(jnp.int32, values.shape, 1) % HEAD_DIM
    half, width = ROTARY // 2, values.shape[1]
    partner = jnp.where(
        lane < half, pltpu.roll(values, width - half, 1), pltpu.roll(values, half, 1)
    )
    return values * cosine + partner * sine


def project_kernel(count, normed, cosine, sine, bias, *refs):
    weights, (qkv, hidden, stacked) = refs[:count], refs[count:]
    tile = pl.program_id(0)
    tall = normed.shape[1] // count
    total = bias[...]
    for k in range(count):
        block = normed[:, k * tall : (k + 1) * tall]
        total = total + jnp.dot(block, weights[k][...], preferred_element_type=wide)
    repeats = total.shape[1] // LANES

    @pl.when(tile < 2)
    def _():
        turned = turn(
            total,
            jnp.concatenate([cosine[...]] * repeats, axis=1),
            jnp.concatenate([sine[...]] * repeats, axis=1),
        )
        qkv[...] = turned.astype(low)

    @pl.when(tile == 2)
    def _():
        qkv[...] = total.astype(low)

    @pl.when(tile > 2)
    def _():
        hidden[...] = total
        stacked[...] = (total * gelu_parts(total)[0]).astype(low)


def project(normed, cosine, sine, bias, weights, tall, head_width):
    count = len(weights)
    length = normed.shape[0]
    inside = weights[0].shape[1]
    units = inside - 3 * head_width
    table = pl.BlockSpec((length, LANES), lambda t: (0, 0))
    return pl.pallas_call(
        functools.partial(project_kernel, count),
        grid=(inside // head_width,),
        in_specs=[
            pl.BlockSpec((length, count * tall), lambda t: (0, 0)),
            table,
            table,
            pl.BlockSpec((1, head_width), lambda t: (0, t)),
        ]
        + [pl.BlockSpec((tall, head_width), lambda t: (0, t))] * count,
        out_specs=[
            pl.BlockSpec((length, head_width), lambda t: (0, jnp.minimum(t, 2))),
            pl.BlockSpec((length, head_width), lambda t: (0, jnp.maximum(t - 3, 0))),
            pl.BlockSpec((length, head_width), lambda t: (0, jnp.maximum(t - 2, 1))),
        ],
        out_shape=[
            jax.ShapeDtypeStruct((length, 3 * head_width), low),
            jax.ShapeDtypeStruct((length, units), wide),
            jax.ShapeDtypeStruct((length, head_width + units), low),
        ],
        cost_estimate=pl.CostEstimate(
            flops=2 * length * count * tall * inside,
            bytes_accessed=2 * count * tall * (inside + length) + 8 * length * inside,
            transcendentals=length * units,
        ),
        name="project",
    )(normed, cosine, sine, bias, *weights)


def emit_kernel(owners, counts, stacked, *refs):
    counted, refs = refs[:counts], refs[counts:]
    weights, out = refs[: 2 * owners], refs[-1]
    middle = weights[0].shape[0]
    for k in range(owners):

        @pl.when(pl.program_id(0) // 2 == k)
        def _(k=k):
            total = jnp.dot(
                stacked[:, :middle], weights[2 * k][...], preferred_element_type=wide
            ) + jnp.dot(stacked[:, middle:], weights[2 * k + 1][...], preferred_element_type=wide)
            out[...] = total.astype(low)

    if not counted:
        return

    @pl.when(pl.program_id(0) == 2 * owners)
    def _():
        count = counted[0][...].astype(wide)
        for ref in counted[1:]:
            count = count + ref[...].astype(wide)
        count = count[:1].astype(jnp.int32)
        lane = lax.broadcasted_iota(jnp.int32, count.shape, 1)
        digits = jnp.where(lane == 0, count, count // DIGIT)
        digits = jnp.where(lane == 2, count // (DIGIT * DIGIT), digits) % DIGIT
        out[:, :LANES] = jnp.broadcast_to(digits.astype(wide), (out.shape[0], LANES)).astype(low)


def emit(stacked, weights, counted, first, all_owners, into=None):
    owners = len(weights)
    length, behind = stacked.shape
    middle, depth = weights[0][0].shape
    size = depth // 2
    steps = 2 * owners + (first + owners == all_owners)

    def at(k):
        return pl.BlockSpec((middle, size), lambda t: (0, jnp.clip(t - 2 * k, 0, 1)))

    row = size // SPARE
    operands = [stacked, *counted, *[item for pair in weights for item in pair]]
    in_specs = [pl.BlockSpec((length, behind), lambda t: (0, 0))]
    in_specs += [pl.BlockSpec((SPARE, LANES), lambda t: (row, 0))] * len(counted)
    in_specs += [at(k) for k in range(owners) for _ in range(2)]
    aliases = {}
    if into is not None:
        aliases = {len(operands): 0}
        operands.append(into)
        in_specs.append(pl.BlockSpec(memory_space=pl.ANY))
    return pl.pallas_call(
        functools.partial(emit_kernel, owners, len(counted)),
        grid=(steps,),
        in_specs=in_specs,
        out_specs=pl.BlockSpec((length, size), lambda t: (0, 2 * first + t)),
        out_shape=jax.ShapeDtypeStruct((length, all_owners * depth + LANES), low),
        input_output_aliases=aliases,
        cost_estimate=pl.CostEstimate(
            flops=2 * length * behind * owners * depth,
            bytes_accessed=2 * behind * (length + owners * depth) + 2 * length * steps * size,
            transcendentals=0,
        ),
        name="emit",
    )(*operands)


def scores_of(rows, keys, start):
    raw = lax.dot_general(rows, keys, (((1,), (1,)), ((), ())), preferred_element_type=wide)
    place = start + lax.broadcasted_iota(jnp.int32, raw.shape, 0)
    kept = lax.broadcasted_iota(jnp.int32, raw.shape, 1) <= place
    return jnp.where(kept, raw * HEAD_DIM ** (-0.5), masked_fill)


def attend_kernel(step, qkv, stacked, out, logsum):
    del stacked
    length, head_width = out.shape
    lane = lax.broadcasted_iota(jnp.int32, (step, LANES), 1)
    for first in range(0, length, step):
        last = first + step
        sums = jnp.zeros((step, LANES), wide)
        outs = []
        for h in range(head_width // HEAD_DIM):
            a, b = h * HEAD_DIM, (h + 1) * HEAD_DIM
            keys = qkv[:last, head_width + a : head_width + b]
            values = qkv[:last, 2 * head_width + a : 2 * head_width + b]
            scores = scores_of(qkv[first:last, a:b], keys, first)
            top = jnp.max(scores, axis=-1, keepdims=True)
            expd = jnp.exp(scores - top)
            total = jnp.sum(expd, axis=-1, keepdims=True)
            probs = (expd * (1.0 / total)).astype(low)
            outs.append(jnp.dot(probs, values, preferred_element_type=wide))
            sums = jnp.where(lane == h, top + jnp.log(total), sums)
        out[first:last, :] = jnp.concatenate(outs, axis=1).astype(low)
        logsum[first:last, :] = sums


def attend(qkv, stacked):
    length, three = qkv.shape
    head_width = three // 3
    heads = head_width // HEAD_DIM
    whole = pl.BlockSpec(memory_space=pltpu.VMEM)
    return pl.pallas_call(
        functools.partial(attend_kernel, min(256, length)),
        grid=(1,),
        in_specs=[whole, pl.BlockSpec(memory_space=pl.ANY)],
        out_specs=[pl.BlockSpec((length, head_width), lambda n: (0, 0)), whole],
        out_shape=[
            jax.ShapeDtypeStruct(stacked.shape, low),
            jax.ShapeDtypeStruct((length, LANES), wide),
        ],
        input_output_aliases={1: 0},
        cost_estimate=pl.CostEstimate(
            flops=4 * heads * length * length * LANES,
            bytes_accessed=8 * length * three,
            transcendentals=heads * length * length,
        ),
        name="attend",
    )(qkv, stacked)


def attend_back_kernel(step, qkv, grad, logsum, cosine, sine, entered, out, gone):
    del entered
    length, head_width = grad.shape
    scale = HEAD_DIM ** (-0.5)
    over_rows = (((0,), (0,)), ((), ()))
    for first in reversed(range(0, length, step)):
        last = first + step
        parts = [[], [], []]
        for h in range(head_width // HEAD_DIM):
            a, b = h * HEAD_DIM, (h + 1) * HEAD_DIM
            query = qkv[first:last, a:b]
            keys = qkv[:last, head_width + a : head_width + b]
            values = qkv[:last, 2 * head_width + a : 2 * head_width + b]
            upstream = grad[first:last, a:b]
            probs = jnp.exp(scores_of(query, keys, first) - logsum[first:last, h : h + 1])
            prob_grad = lax.dot_general(
                upstream, values, (((1,), (1,)), ((), ())), preferred_element_type=wide
            )
            inner = jnp.sum(probs * prob_grad, axis=-1, keepdims=True)
            score_grad = (probs * (prob_grad - inner)).astype(low)
            parts[0].append(jnp.dot(score_grad, keys, preferred_element_type=wide) * scale)
            parts[1].append(
                lax.dot_general(score_grad, query, over_rows, preferred_element_type=wide) * scale
            )
            parts[2].append(
                lax.dot_general(
                    probs.astype(low), upstream, over_rows, preferred_element_type=wide
                )
            )
        parts = [jnp.concatenate(part_list, axis=1) for part_list in parts]
        gone[first:last, :head_width] = parts[0]
        for t in (1, 2):
            columns = slice(t * head_width, (t + 1) * head_width)
            if last == length:
                gone[:, columns] = parts[t]
            else:
                gone[:last, columns] += parts[t]
    repeats = head_width // LANES
    for first in range(0, length, step):
        here = slice(first, first + step)
        ahead = jnp.concatenate([cosine[here, :]] * repeats, axis=1)
        aside = -jnp.concatenate([sine[here, :]] * repeats, axis=1)
        for t in range(3):
            columns = slice(t * head_width, (t + 1) * head_width)
            value = gone[here, columns].astype(low)
            if t < 2:
                value = turn(value.astype(wide), ahead, aside).astype(low)
            out[here, columns] = value


def attend_back(qkv, grad, logsum, cosine, sine, entered):
    length, three = qkv.shape
    head_width = three // 3
    heads = head_width // HEAD_DIM
    whole = pl.BlockSpec(memory_space=pltpu.VMEM)
    return pl.pallas_call(
        functools.partial(attend_back_kernel, min(256, length)),
        grid=(1,),
        in_specs=[whole] * 5 + [pl.BlockSpec(memory_space=pl.ANY)],
        out_specs=pl.BlockSpec((length, three), lambda n: (0, 0)),
        out_shape=jax.ShapeDtypeStruct(entered.shape, low),
        scratch_shapes=[
            pltpu.VMEM((length, three), wide),
        ],
        input_output_aliases={5: 0},
        cost_estimate=pl.CostEstimate(
            flops=10 * heads * length * length * LANES,
            bytes_accessed=8 * length * three,
            transcendentals=heads * length * length,
        ),
        name="attend_back",
    )(qkv, grad, logsum, cosine, sine, entered)


def reject_kernel(count, hidden, grads, *refs):
    weights, (head_grad, entered) = refs[:count], refs[count:]
    depth = weights[0].shape[1]
    over = (((1,), (1,)), ((), ()))
    total = lax.dot_general(grads[:, :depth], weights[0][...], over, preferred_element_type=wide)
    for k in range(1, count):
        total = total + lax.dot_general(
            grads[:, k * depth : (k + 1) * depth],
            weights[k][...],
            over,
            preferred_element_type=wide,
        )

    @pl.when(pl.program_id(0) == 0)
    def _():
        head_grad[...] = total.astype(low)

    @pl.when(pl.program_id(0) > 0)
    def _():
        entered[...] = (total * gelu_parts(hidden[...])[1]).astype(low)


def reject(grads, weights, hidden, head_width):
    count = len(weights)
    length = grads.shape[0]
    behind, depth = weights[0].shape
    inside = behind + 2 * head_width
    return pl.pallas_call(
        functools.partial(reject_kernel, count),
        grid=(behind // head_width,),
        in_specs=[pl.BlockSpec((length, head_width), lambda t: (0, jnp.maximum(t - 1, 0)))]
        + [pl.BlockSpec((length, count * depth), lambda t: (0, 0))]
        + [pl.BlockSpec((head_width, depth), lambda t: (t, 0))] * count,
        out_specs=[
            pl.BlockSpec((length, head_width), lambda t: (0, 0)),
            pl.BlockSpec((length, head_width), lambda t: (0, jnp.maximum(t + 2, 3))),
        ],
        out_shape=[
            jax.ShapeDtypeStruct((length, head_width), low),
            jax.ShapeDtypeStruct((length, inside), low),
        ],
        cost_estimate=pl.CostEstimate(
            flops=2 * length * count * depth * behind,
            bytes_accessed=2 * count * depth * (behind + length) + 8 * length * behind,
            transcendentals=length * behind,
        ),
        name="reject",
    )(hidden, grads, *weights)


def answer_kernel(count, chips, part, entered, *refs):
    weights, (kept, sent, held) = refs[:count], refs[count:]
    rows = kept.shape[0] // chips
    over = (((1,), (1,)), ((), ()))
    for n in range(count):

        @pl.when(pl.program_id(0) == n)
        def _(n=n):
            held[...] = lax.dot_general(
                entered[...], weights[n][...], over, preferred_element_type=wide
            )

    for k in range(chips):
        here = slice(k * rows, (k + 1) * rows)
        for core, out in enumerate((kept, sent)):
            block = part[0] ^ (2 * k + core)
            source = pl.ds(pl.multiple_of(block * rows, rows), rows)
            out[here, :] = held[source, :].astype(out.dtype)


def answer(entered, pieces, part, chips, tall):
    count = len(pieces)
    length, inside = entered.shape
    half = length // 2
    return pl.pallas_call(
        functools.partial(answer_kernel, count, chips),
        grid=(count,),
        in_specs=[
            pl.BlockSpec(memory_space=pltpu.SMEM),
            pl.BlockSpec((length, inside), lambda t: (0, 0)),
        ]
        + [pl.BlockSpec((tall, inside), lambda t: (0, 0))] * count,
        out_specs=[pl.BlockSpec((half, tall), lambda t: (0, t))] * 2,
        out_shape=[
            jax.ShapeDtypeStruct((half, count * tall), wide),
            jax.ShapeDtypeStruct((half, count * tall), low),
        ],
        scratch_shapes=[pltpu.VMEM((length, tall), wide)],
        cost_estimate=pl.CostEstimate(
            flops=2 * length * inside * count * tall,
            bytes_accessed=2 * inside * (length + count * tall) + 3 * length * count * tall,
            transcendentals=0,
        ),
        name="answer",
    )(part[None], entered, *pieces)


def widen_rows_kernel(head_width, a, b, down, out):
    cut = b.shape[1] - head_width
    out[...] = b[0, :head_width].astype(wide)
    down[:cut] = b[0, head_width:].astype(wide)
    down[cut:] = a[0].astype(wide)


def widen_rows(all_a, all_b, head_width, width):
    count, rest, depth = all_a.shape
    tall = all_b.shape[1]
    units = rest + tall - head_width
    return pl.pallas_call(
        functools.partial(widen_rows_kernel, head_width),
        grid=(count,),
        in_specs=[
            pl.BlockSpec((1, rest, depth), lambda j: (j, 0, 0)),
            pl.BlockSpec((1, tall, depth), lambda j: (j, 0, 0)),
        ],
        out_specs=[
            pl.BlockSpec((units, depth), lambda j: (j, 0)),
            pl.BlockSpec((head_width, depth), lambda j: (j, 0)),
        ],
        out_shape=[
            jax.ShapeDtypeStruct((count * units, depth), wide),
            jax.ShapeDtypeStruct((width, depth), wide),
        ],
        cost_estimate=pl.CostEstimate(
            flops=0, bytes_accessed=6 * count * depth * (rest + tall), transcendentals=0
        ),
        name="widen_rows",
    )(all_a, all_b)


def widen_columns_kernel(groups, gathered, out):
    count, _, columns = gathered.shape
    size = columns // groups
    for j in range(count):
        for g in range(groups):
            at = (g * count + j) * size
            out[:, at : at + size] = gathered[j, :, g * size : (g + 1) * size].astype(wide)


def widen_columns(gathered, rows, groups):
    count, _, columns = gathered.shape
    tall = min(64, rows)
    moved = 6 * count * rows * columns
    return pl.pallas_call(
        functools.partial(widen_columns_kernel, groups),
        grid=(rows // tall,),
        in_specs=[pl.BlockSpec((count, tall, columns), lambda r: (0, r, 0))],
        out_specs=pl.BlockSpec((tall, count * columns), lambda r: (r, 0)),
        out_shape=jax.ShapeDtypeStruct((rows, count * columns), wide),
        cost_estimate=pl.CostEstimate(flops=0, bytes_accessed=moved, transcendentals=0),
        name="widen_columns",
    )(gathered)


def local(
    tokens,
    teacher,
    valid,
    positions,
    norm_gain,
    norm_bias,
    qkv_weight,
    qkv_bias,
    out_weight,
    out_bias,
    up_weight,
    up_bias,
    down_weight,
    down_bias,
):
    rows_here, width = tokens.shape[1:]
    seq_count = lax.axis_size("seq")
    data_count = lax.axis_size("dp")
    part = lax.axis_index("seq")
    owner = lax.axis_index("dp")
    length = rows_here * seq_count
    head_width = HEADS // seq_count * HEAD_DIM
    three = 3 * head_width
    units = up_weight.shape[1] // seq_count
    inside = three + units
    depth = qkv_weight.shape[0]

    tall = depth // 2
    behind = head_width + units

    def span(start, size, unit):
        return pl.ds(start if isinstance(start, int) else pl.multiple_of(start, unit), size)

    def block_at(row, rows, column, columns):
        return span(row, rows, ROWS), span(column, columns, LANES)

    moves = []
    for half in range(2):
        for t in range(3):
            moves.append(
                (
                    0,
                    lambda part, t=t, half=half: block_at(
                        half * tall, tall, t * width + part * head_width, head_width
                    ),
                    half,
                    block_at(0, tall, t * head_width, head_width),
                )
            )
        moves.append(
            (
                1,
                lambda part, half=half: block_at(half * tall, tall, part * units, units),
                half,
                block_at(0, tall, three, units),
            )
        )
    w_in = pick(
        (qkv_weight, up_weight),
        part[None],
        valid,
        moves,
        [(tall, inside), (tall + SPARE, inside)],
    )
    normed_low, base = enter(
        tokens[0],
        teacher[0],
        norm_gain,
        norm_bias,
        out_bias,
        down_bias,
        positions,
        after(owner, *w_in),
        data_count,
    )

    rest = behind // 2 - head_width
    moves = [
        (
            0,
            lambda part: block_at(part * head_width, head_width, 0, depth),
            0,
            block_at(0, head_width, 0, depth),
        ),
        (
            1,
            lambda part: block_at(part * units, rest, 0, depth),
            0,
            block_at(head_width, rest, 0, depth),
        ),
        (
            1,
            lambda part: block_at(part * units + rest, units - rest, 0, depth),
            1,
            block_at(0, units - rest, 0, depth),
        ),
    ]
    w_back = pick(
        (out_weight, down_weight),
        after(part[None], normed_low),
        valid,
        moves,
        [(behind // 2, depth)] * 2,
    )
    if data_count == 4:
        sides = [tuple(swap(item, "dp", k) for item in w_in) for k in (1, 2)]
        last_in = swap(sides[0][0], "dp", 2), swap(sides[1][1], "dp", 1)
        first_in = [w_in, *sides]
        w_back = lax.optimization_barrier((*w_back, *last_in))[:2]
        back_sides = [tuple(swap(item, "dp", k) for item in w_back) for k in (1, 2)]
    else:
        w_in = [w_in] + [tuple(swap(item, "dp", k) for item in w_in) for k in range(1, data_count)]
        w_back = [w_back] + [
            tuple(swap(item, "dp", k) for item in w_back) for k in range(1, data_count)
        ]
        first_in, last_in = w_in[:-1], w_in[-1]
    normed_all = gather_seq(normed_low)
    facts = normed_all[:, width : width + 2].astype(jnp.int32)
    where = facts[:, 0] * RADIX + facts[:, 1]

    half = ROTARY // 2
    lane = jnp.arange(LANES, dtype=jnp.int32) % HEAD_DIM
    freqs = rope_base ** (-((lane % half).astype(wide) * 2.0) / ROTARY)
    angles = where.astype(wide)[:, None] * jnp.where(lane < ROTARY, freqs, 0.0)[None, :]
    cosine = jnp.cos(angles)
    sine = jnp.sin(angles) * jnp.where(lane < half, -1.0, 1.0)[None, :]

    b_in = jnp.concatenate(
        [
            lax.dynamic_slice_in_dim(qkv_bias, t * width + part * head_width, head_width, 0)
            for t in range(3)
        ]
        + [lax.dynamic_slice_in_dim(up_bias, part * units, units, 0)]
    ).astype(wide)[None]

    def piece(array, k):
        return array[:, k * depth : (k + 1) * depth]

    flat_in = [item for pair in (*first_in, last_in) for item in pair]
    qkv, hidden, stacked = project(normed_all, cosine, sine, b_in, flat_in, tall, head_width)
    stacked, logsum = attend(qkv, stacked)

    counted = [item[1] for item in (*first_in, last_in)]
    if data_count == 4:
        back_sides = [tuple(after(item, stacked) for item in pair) for pair in back_sides]
        w_back = [w_back, *back_sides]
        w_back.append((swap(back_sides[0][0], "dp", 2), swap(back_sides[1][1], "dp", 1)))
    branches = emit(stacked, w_back[:-1], [], 0, data_count)
    branches = emit(stacked, w_back[-1:], counted, data_count - 1, data_count, branches)
    w_back = [jnp.concatenate(pair, axis=0) for pair in w_back]
    branches, *w_back = lax.optimization_barrier((scatter_seq(branches), *w_back))
    grad_output, grad_low, sums = grade(branches, base, valid, float(length * data_count))
    squares, count = sums[0, 0], sums[1, 0]
    grad_all = gather_seq(grad_low)
    branch_bias_grad = jnp.sum(grad_all.astype(wide), axis=0)

    def owned(left, right):
        return dot(left, right, ((0,), (0,)))

    def gather(array):
        return lax.all_gather(array, "seq", axis=0, tiled=False)

    cut = units * 5 // 8

    def of_stacked(first, last):
        return [owned(stacked[:, first:last], piece(grad_all, k)) for k in range(data_count)]

    def of_normed(right):
        return [owned(piece(normed_all, k), right) for k in range(data_count)]

    def prepare(pieces):
        return pieces[0], [item.astype(low) for item in pieces[1:]]

    def send(sent, *meanwhile):
        got = [swap(item, "dp", k + 1) for k, item in enumerate(sent)]
        held = lax.optimization_barrier((*got, *jax.tree.leaves(meanwhile)))
        return held[: len(got)], jax.tree.unflatten(jax.tree.structure(meanwhile), held[len(got) :])

    def total(own, got):
        for item in got:
            own = own + item.astype(wide)
        return own.astype(low)

    own_a, sent_a = prepare(of_stacked(head_width + cut, head_width + units))
    own_b, sent_b = prepare(of_stacked(0, head_width + cut))
    got, ((own_b, sent_b),) = send(sent_a, (own_b, sent_b))
    down_a = total(own_a, got)
    all_a = gather(down_a)
    head_grad, in_low = reject(after(grad_all, down_a), w_back, hidden, head_width)
    in_low = attend_back(qkv, head_grad, logsum, cosine, sine, in_low)
    got, (in_low,) = send(sent_b, in_low)
    down_b = total(own_b, got)
    all_b = gather(down_b)
    in_low = after(in_low, down_b)
    own_up, sent_up = prepare(of_normed(in_low[:, three:]))
    own_qkv, sent_qkv = prepare(of_normed(after(in_low[:, :three], *sent_up)))
    kept, sent = answer(in_low, flat_in, part, seq_count // 2, tall)
    got, ((own_qkv, sent_qkv), kept, all_a) = send(sent_up, (own_qkv, sent_qkv), kept, all_a)
    up_grad = total(own_up, got)
    all_up = gather(up_grad)
    summed = scatter_blocks(kept, sent)
    got, (summed, all_b) = send(sent_qkv, summed, all_b)
    qkv_grad = total(own_qkv, got)
    token_grad, gain_grad, shift_grad, branch_bias_grad = leave(
        tokens[0],
        norm_gain,
        summed,
        grad_output,
        branch_bias_grad,
        owner,
        data_count,
    )

    in_bias = jnp.sum(in_low.astype(wide), axis=0)
    small = jnp.concatenate(
        [in_bias, gain_grad[0], shift_grad[0], squares[None], branch_bias_grad[0]]
    )
    small = total_dp(small[None])[0]
    branch_bias_grad = small[-width:]
    small = small[:-width]
    lines = -(-small.size // three)
    lines += -lines % 8
    high = jnp.pad(small, (0, lines * three - small.size)).reshape(lines, three)
    first = lax.reduce_precision(high, 8, 7)
    beside = jnp.concatenate([qkv_grad, first.astype(low), (high - first).astype(low)])

    down_weight_grad, out_weight_grad = widen_rows(all_a, all_b, head_width, width)
    all_qkv = gather(after(beside, all_up))
    up_weight_grad = widen_columns(all_up, depth, 1)
    all_qkv = after(all_qkv, down_weight_grad, up_weight_grad)
    qkv_weight_grad = widen_columns(all_qkv, depth, 3)
    slots = all_qkv[:, depth:].astype(wide)
    slots = (slots[:, :lines] + slots[:, lines:]).reshape(seq_count, -1)
    norm_grads = jnp.sum(slots[:, inside : inside + 2 * width + 1], axis=0)
    qkv_bias_grad = slots[:, :three].reshape(seq_count, 3, head_width).transpose(1, 0, 2)
    up_bias_grad = slots[:, three:inside].reshape(-1)
    loss = norm_grads[-1] / (2.0 * width * count)
    return (
        loss,
        token_grad[None],
        norm_grads[:width],
        norm_grads[width : 2 * width],
        qkv_weight_grad,
        qkv_bias_grad.reshape(-1),
        out_weight_grad,
        branch_bias_grad,
        up_weight_grad,
        up_bias_grad,
        down_weight_grad,
        branch_bias_grad,
    )


def solution(mesh):
    placed = (
        P("dp", "seq", None),
        P("dp", "seq", None),
        P("dp", "seq"),
        P("dp", "seq"),
        P(),
        P(),
        P("dp", None),
        P(),
        P(None, "dp"),
        P(),
        P("dp", None),
        P(),
        P(None, "dp"),
        P(),
    )
    return jax.shard_map(
        local,
        mesh=mesh,
        in_specs=placed,
        out_specs=(
            P(),
            P("dp", "seq", None),
            P(),
            P(),
            P("dp", None),
            P(),
            P(None, "dp"),
            P(),
            P("dp", None),
            P(),
            P(None, "dp"),
            P(),
        ),
        check_vma=False,
    )
```

```python
import functools

import jax
import jax.numpy as jnp
from jax import lax
from jax.experimental import pallas as pl
from jax.experimental.pallas import tpu as pltpu
from jax.sharding import PartitionSpec as P

HEADS = 32
HEAD_DIM = 64
ROTARY = 32


norm_eps = 1e-05
rope_base = 10000.0
masked_fill = -1e30
LANES = 128
RADIX = 64
DIGIT = 16
SPARE = 16
ROWS = 64

low = jnp.bfloat16
wide = jnp.float32


def dot(a, b, dims):
    return lax.dot_general(a, b, (dims, ((), ())), preferred_element_type=wide)


def after(array, *earlier):
    return lax.optimization_barrier((array, *earlier))[0]


def swap(array, axis, bit):
    return lax.ppermute(array, axis, [(s, s ^ bit) for s in range(lax.axis_size(axis))])


def gather_seq(rows):
    return lax.all_gather(rows, "seq", axis=0, tiled=True)


def between(array, pairs):
    return lax.ppermute(
        array, "seq", [(2 * a + core, 2 * b + core) for a, b in pairs for core in range(2)]
    )


def scatter_chips(blocks):
    chips = len(blocks)
    if chips != 4:
        total = blocks[0]
        for k in range(1, chips):
            total = total + swap(blocks[k].astype(low), "seq", 2 * k).astype(wide)
        return total
    chip = lax.axis_index("seq") // 2
    far = between(blocks[3].astype(low), [(0, 1), (3, 2)])
    passed = (blocks[2] + far.astype(wide)).astype(low)
    upward = between(passed, [(0, 1), (1, 2)])
    downward = between(passed, [(3, 2), (2, 1)])
    upward = jnp.where(chip == 1, blocks[3], blocks[1]) + upward.astype(wide)
    downward = jnp.where(chip == 2, blocks[3], blocks[1]) + downward.astype(wide)
    upward = between(upward.astype(low), [(0, 1), (1, 2), (2, 3)])
    downward = between(downward.astype(low), [(3, 2), (2, 1), (1, 0)])
    return blocks[0] + upward.astype(wide) + downward.astype(wide)


def scatter_blocks(kept, sent):
    chips = lax.axis_size("seq") // 2
    rows = kept.shape[0] // chips
    chip = kept + swap(sent, "seq", 1).astype(wide)
    return scatter_chips([chip[k * rows : (k + 1) * rows] for k in range(chips)])


def scatter_seq(partial):
    return lax.psum_scatter(partial, "seq", scatter_dimension=0, tiled=True)


def total_dp(array):
    items = [array] + [swap(array, "dp", k) for k in range(1, lax.axis_size("dp"))]
    while len(items) > 1:
        items = [a + b for a, b in zip(items[::2], items[1::2])]
    return items[0]


def normalise(values):
    centre = values - jnp.mean(values, axis=-1, keepdims=True)
    spread = jnp.mean(centre * centre, axis=-1, keepdims=True)
    rstd = lax.rsqrt(spread + norm_eps)
    return centre * rstd, rstd


def enter_kernel(
    owners, owner, tokens, teacher, gain, shift, bias_a, bias_b, place, normed, base, held, kept
):
    inputs = tokens[...].astype(wide)
    xhat, _ = normalise(inputs)
    held[...] = xhat * gain[...].astype(wide)[None] + shift[...].astype(wide)[None]
    biases = (bias_a[...].astype(wide) + bias_b[...].astype(wide))[None]
    kept[...] = inputs + biases - teacher[...].astype(wide)
    width = inputs.shape[1]
    depth = width // owners
    for k in range(owners):
        theirs = pl.ds(pl.multiple_of((owner[0] ^ k) * depth, LANES), depth)
        normed[:, k * depth : (k + 1) * depth] = held[:, theirs].astype(low)
        base[:, k * depth : (k + 1) * depth] = kept[:, theirs]
    lane = lax.broadcasted_iota(jnp.int32, (inputs.shape[0], LANES), 1)
    ids = column_of(place[...]).astype(jnp.int32)
    facts = jnp.where(lane == 0, ids // RADIX, ids % RADIX)
    normed[:, width:] = facts.astype(wide).astype(low)


def enter(tokens, teacher, gain, shift, bias_a, bias_b, place, owner, owners):
    rows, width = tokens.shape
    whole = pl.BlockSpec(memory_space=pltpu.VMEM)
    return pl.pallas_call(
        functools.partial(enter_kernel, owners),
        in_specs=[pl.BlockSpec(memory_space=pltpu.SMEM)] + [whole] * 7,
        out_specs=[whole] * 2,
        out_shape=[
            jax.ShapeDtypeStruct((rows, width + LANES), low),
            jax.ShapeDtypeStruct((rows, width), wide),
        ],
        scratch_shapes=[pltpu.VMEM((rows, width), wide)] * 2,
        name="enter",
    )(
        owner[None],
        tokens,
        teacher,
        gain,
        shift,
        bias_a,
        bias_b,
        place,
    )


def column_of(row):
    size = row.shape[1]
    here = lax.broadcasted_iota(jnp.int32, (size, size), 0)
    there = lax.broadcasted_iota(jnp.int32, (size, size), 1)
    return jnp.sum(jnp.where(here == there, row.astype(wide), 0.0), axis=1, keepdims=True)


def grade_kernel(scale, branches, base, valid, grad, grad_low, sums):
    width = base.shape[1]
    lane = lax.broadcasted_iota(jnp.int32, (1, LANES), 1)
    weight = jnp.where(lane == 1, float(DIGIT), jnp.where(lane == 2, float(DIGIT * DIGIT), 1.0))
    digits = jnp.where(lane < 3, branches[:1, width:].astype(wide) * weight, 0.0)
    count = jnp.sum(digits, axis=1, keepdims=True)
    error = base[...] + branches[:, :width].astype(wide)
    weighted = column_of(valid[...]) * error
    squares = jnp.sum(jnp.sum(weighted * error, axis=0, keepdims=True), axis=1, keepdims=True)
    result = scale / count * weighted
    grad[...] = result
    grad_low[...] = result.astype(low)
    line = lax.broadcasted_iota(jnp.int32, sums.shape, 0)
    sums[...] = jnp.where(line == 0, squares, count)


def grade(branches, base, valid, scale):
    whole = pl.BlockSpec(memory_space=pltpu.VMEM)
    return pl.pallas_call(
        functools.partial(grade_kernel, scale),
        in_specs=[whole] * 3,
        out_specs=[whole] * 3,
        out_shape=[
            jax.ShapeDtypeStruct(base.shape, wide),
            jax.ShapeDtypeStruct(base.shape, low),
            jax.ShapeDtypeStruct((8, LANES), wide),
        ],
        cost_estimate=pl.CostEstimate(
            flops=4 * base.size, bytes_accessed=12 * base.size, transcendentals=0
        ),
        name="grade",
    )(branches, base, valid)


def leave_kernel(
    owners, owner, tokens, gain, summed, grad, bias, token_grad, gain_grad, shift_grad, bias_grad
):
    inputs = tokens[...].astype(wide)
    xhat, rstd = normalise(inputs)
    depth = inputs.shape[1] // owners
    for k in range(owners):
        theirs = pl.ds(pl.multiple_of((owner[0] ^ k) * depth, LANES), depth)
        token_grad[:, theirs] = summed[:, k * depth : (k + 1) * depth]
        bias_grad[:, theirs] = bias[:, k * depth : (k + 1) * depth]
    normed_grad = token_grad[...]
    gain_grad[...] = jnp.sum(normed_grad * xhat, axis=0, keepdims=True)
    shift_grad[...] = jnp.sum(normed_grad, axis=0, keepdims=True)
    scaled = normed_grad * gain[...].astype(wide)[None]
    token_grad[...] = rstd * (
        scaled
        - jnp.mean(scaled, axis=-1, keepdims=True)
        - xhat * jnp.mean(scaled * xhat, axis=-1, keepdims=True)
    )
    for k in range(owners):
        theirs = pl.ds(pl.multiple_of((owner[0] ^ k) * depth, LANES), depth)
        token_grad[:, theirs] += grad[:, k * depth : (k + 1) * depth]


def leave(tokens, gain, summed, grad, bias, owner, owners):
    rows, width = tokens.shape
    whole = pl.BlockSpec(memory_space=pltpu.VMEM)
    line = jax.ShapeDtypeStruct((1, width), wide)
    return pl.pallas_call(
        functools.partial(leave_kernel, owners),
        in_specs=[pl.BlockSpec(memory_space=pltpu.SMEM)] + [whole] * 5,
        out_specs=[whole] * 4,
        out_shape=[jax.ShapeDtypeStruct((rows, width), wide), line, line, line],
        name="leave",
    )(owner[None], tokens, gain, summed, grad, bias[None])


def pick_kernel(moves, part, counted, a, b, *refs):
    outs, arrived = refs[:2], refs[2]
    copies = []
    for which, source, half, target in moves:
        copies.append(
            pltpu.make_async_copy(
                (a, b)[which].at[source(part[0])],
                outs[half].at[target],
                arrived.at[len(copies)],
            )
        )
    for copy in copies:
        copy.start()
    tall = outs[0].shape[0]
    more = outs[1].shape[0] - tall
    if more:
        count = jnp.sum(counted[...].astype(wide), axis=1, keepdims=True)
        outs[1][tall:, :] = jnp.broadcast_to(count, (more, outs[1].shape[1])).astype(low)
    for copy in copies:
        copy.wait()


def pick(arrays, part, counted, moves, shapes):
    moved = 4 * sum(shape[0] * shape[1] for shape in shapes)
    return pl.pallas_call(
        functools.partial(pick_kernel, moves),
        in_specs=[
            pl.BlockSpec(memory_space=pltpu.SMEM),
            pl.BlockSpec(memory_space=pltpu.VMEM),
        ]
        + [pl.BlockSpec(memory_space=pl.ANY)] * 2,
        out_specs=[pl.BlockSpec(memory_space=pltpu.VMEM)] * 2,
        out_shape=[jax.ShapeDtypeStruct(shape, low) for shape in shapes],
        scratch_shapes=[pltpu.SemaphoreType.DMA((len(moves),))],
        cost_estimate=pl.CostEstimate(flops=0, bytes_accessed=moved, transcendentals=0),
        name="pick",
    )(part, counted, *arrays)


def gelu_parts(values):
    root = (2.0 / jnp.pi) ** 0.5
    square = values * values
    bent = jnp.tanh(root * (values + 0.044715 * (values * square)))
    factor = 0.5 * (1.0 + bent)
    slope = 0.5 * values * (1.0 - bent * bent) * (root * (1.0 + 3.0 * 0.044715 * square))
    return factor, factor + slope


def turn(values, cosine, sine):
    lane = lax.broadcasted_iota(jnp.int32, values.shape, 1) % HEAD_DIM
    half, width = ROTARY // 2, values.shape[1]
    partner = jnp.where(
        lane < half, pltpu.roll(values, width - half, 1), pltpu.roll(values, half, 1)
    )
    return values * cosine + partner * sine


def project_kernel(count, normed, cosine, sine, bias, *refs):
    weights, (qkv, hidden, stacked) = refs[:count], refs[count:]
    tile = pl.program_id(0)
    tall = normed.shape[1] // count
    total = bias[...]
    for k in range(count):
        block = normed[:, k * tall : (k + 1) * tall]
        total = total + jnp.dot(block, weights[k][...], preferred_element_type=wide)
    repeats = total.shape[1] // LANES

    @pl.when(tile < 2)
    def _():
        turned = turn(
            total,
            jnp.concatenate([cosine[...]] * repeats, axis=1),
            jnp.concatenate([sine[...]] * repeats, axis=1),
        )
        qkv[...] = turned.astype(low)

    @pl.when(tile == 2)
    def _():
        qkv[...] = total.astype(low)

    @pl.when(tile > 2)
    def _():
        hidden[...] = total
        stacked[...] = (total * gelu_parts(total)[0]).astype(low)


def project(normed, cosine, sine, bias, weights, tall, head_width):
    count = len(weights)
    length = normed.shape[0]
    inside = weights[0].shape[1]
    units = inside - 3 * head_width
    table = pl.BlockSpec((length, LANES), lambda t: (0, 0))
    return pl.pallas_call(
        functools.partial(project_kernel, count),
        grid=(inside // head_width,),
        in_specs=[
            pl.BlockSpec((length, count * tall), lambda t: (0, 0)),
            table,
            table,
            pl.BlockSpec((1, head_width), lambda t: (0, t)),
        ]
        + [pl.BlockSpec((tall, head_width), lambda t: (0, t))] * count,
        out_specs=[
            pl.BlockSpec((length, head_width), lambda t: (0, jnp.minimum(t, 2))),
            pl.BlockSpec((length, head_width), lambda t: (0, jnp.maximum(t - 3, 0))),
            pl.BlockSpec((length, head_width), lambda t: (0, jnp.maximum(t - 2, 1))),
        ],
        out_shape=[
            jax.ShapeDtypeStruct((length, 3 * head_width), low),
            jax.ShapeDtypeStruct((length, units), wide),
            jax.ShapeDtypeStruct((length, head_width + units), low),
        ],
        cost_estimate=pl.CostEstimate(
            flops=2 * length * count * tall * inside,
            bytes_accessed=2 * count * tall * (inside + length) + 8 * length * inside,
            transcendentals=length * units,
        ),
        name="project",
    )(normed, cosine, sine, bias, *weights)


def emit_kernel(owners, counts, stacked, *refs):
    counted, refs = refs[:counts], refs[counts:]
    weights, (out, slots, arrived) = refs[: 2 * owners], refs[-3:]
    middle, size = slots.shape[2:]
    step = pl.program_id(0)

    def fetch(n):
        columns = pl.ds(n % 2 * size, size)
        return [
            pltpu.make_async_copy(
                weights[n // 2 * 2 + half].at[:, columns],
                slots.at[n % 2, half],
                arrived.at[n % 2, half],
            )
            for half in range(2)
        ]

    @pl.when(step == 0)
    def _():
        for copy in fetch(0):
            copy.start()

    for n in range(2 * owners):

        @pl.when(step == n)
        def _(n=n):
            if n + 1 < 2 * owners:
                for copy in fetch(n + 1):
                    copy.start()
            for copy in fetch(n):
                copy.wait()

    @pl.when(step < 2 * owners)
    def _():
        slot = lax.rem(step, 2)
        total = jnp.dot(stacked[:, :middle], slots[slot, 0], preferred_element_type=wide)
        total = total + jnp.dot(stacked[:, middle:], slots[slot, 1], preferred_element_type=wide)
        out[...] = total.astype(low)

    if not counted:
        return

    @pl.when(step == 2 * owners)
    def _():
        count = counted[0][...].astype(wide)
        for ref in counted[1:]:
            count = count + ref[...].astype(wide)
        count = count[:1].astype(jnp.int32)
        lane = lax.broadcasted_iota(jnp.int32, count.shape, 1)
        digits = jnp.where(lane == 0, count, count // DIGIT)
        digits = jnp.where(lane == 2, count // (DIGIT * DIGIT), digits) % DIGIT
        out[:, :LANES] = jnp.broadcast_to(digits.astype(wide), (out.shape[0], LANES)).astype(low)


def emit(stacked, weights, counted, first, all_owners, into=None):
    owners = len(weights)
    length, behind = stacked.shape
    middle, depth = weights[0][0].shape
    size = depth // 2
    steps = 2 * owners + (first + owners == all_owners)

    row = size // SPARE
    operands = [stacked, *counted, *[item for pair in weights for item in pair]]
    in_specs = [pl.BlockSpec((length, behind), lambda t: (0, 0))]
    in_specs += [pl.BlockSpec((SPARE, LANES), lambda t: (row, 0))] * len(counted)
    in_specs += [pl.BlockSpec(memory_space=pl.ANY)] * (2 * owners)
    aliases = {}
    if into is not None:
        aliases = {len(operands): 0}
        operands.append(into)
        in_specs.append(pl.BlockSpec(memory_space=pl.ANY))
    return pl.pallas_call(
        functools.partial(emit_kernel, owners, len(counted)),
        grid=(steps,),
        in_specs=in_specs,
        out_specs=pl.BlockSpec((length, size), lambda t: (0, 2 * first + t)),
        out_shape=jax.ShapeDtypeStruct((length, all_owners * depth + LANES), low),
        input_output_aliases=aliases,
        scratch_shapes=[
            pltpu.VMEM((2, 2, middle, size), low),
            pltpu.SemaphoreType.DMA((2, 2)),
        ],
        cost_estimate=pl.CostEstimate(
            flops=2 * length * behind * owners * depth,
            bytes_accessed=2 * behind * (length + owners * depth) + 2 * length * steps * size,
            transcendentals=0,
        ),
        name="emit",
    )(*operands)


def scores_of(rows, keys, start):
    raw = lax.dot_general(rows, keys, (((1,), (1,)), ((), ())), preferred_element_type=wide)
    place = start + lax.broadcasted_iota(jnp.int32, raw.shape, 0)
    kept = lax.broadcasted_iota(jnp.int32, raw.shape, 1) <= place
    return jnp.where(kept, raw * HEAD_DIM ** (-0.5), masked_fill)


def by_blocks(length, head_width, step, body):
    pairs = head_width // LANES
    blocks = length // 2 // step
    for half in range(2):

        def one(n, carry, half=half):
            row = pl.multiple_of(half * (length // 2) + lax.rem(n, blocks) * step, step)
            body(row, pl.multiple_of(lax.div(n, blocks) * LANES, LANES), (half + 1) * length // 2)
            return carry

        lax.fori_loop(0, pairs * blocks, one, 0)


def attend_kernel(step, qkv, stacked, out, logsum):
    del stacked
    length, head_width = out.shape
    lane = lax.broadcasted_iota(jnp.int32, (step, LANES), 1)

    def body(row, at, last):
        rows = pl.ds(row, step)
        queries = qkv[rows, pl.ds(at, LANES)]
        keys = qkv[:last, pl.ds(head_width + at, LANES)]
        values = qkv[:last, pl.ds(2 * head_width + at, LANES)]
        sums = logsum[rows, :]
        outs = []
        for n, h in enumerate((slice(0, HEAD_DIM), slice(HEAD_DIM, LANES))):
            scores = scores_of(queries[:, h], keys[:, h], row)
            top = jnp.max(scores, axis=-1, keepdims=True)
            expd = jnp.exp(scores - top)
            total = jnp.sum(expd, axis=-1, keepdims=True)
            probs = (expd * (1.0 / total)).astype(low)
            outs.append(jnp.dot(probs, values[:, h], preferred_element_type=wide))
            sums = jnp.where(lane == at // HEAD_DIM + n, top + jnp.log(total), sums)
        out[rows, pl.ds(at, LANES)] = jnp.concatenate(outs, axis=1).astype(low)
        logsum[rows, :] = sums

    logsum[...] = jnp.zeros(logsum.shape, wide)
    by_blocks(length, head_width, step, body)


def attend(qkv, stacked):
    length, three = qkv.shape
    head_width = three // 3
    heads = head_width // HEAD_DIM
    whole = pl.BlockSpec(memory_space=pltpu.VMEM)
    return pl.pallas_call(
        functools.partial(attend_kernel, 256),
        grid=(1,),
        in_specs=[whole, pl.BlockSpec(memory_space=pl.ANY)],
        out_specs=[pl.BlockSpec((length, head_width), lambda n: (0, 0)), whole],
        out_shape=[
            jax.ShapeDtypeStruct(stacked.shape, low),
            jax.ShapeDtypeStruct((length, LANES), wide),
        ],
        input_output_aliases={1: 0},
        cost_estimate=pl.CostEstimate(
            flops=4 * heads * length * length * LANES,
            bytes_accessed=8 * length * three,
            transcendentals=heads * length * length,
        ),
        name="attend",
    )(qkv, stacked)


def attend_back_kernel(step, qkv, grad, logsum, cosine, sine, entered, out, gone):
    del entered
    length, head_width = grad.shape
    scale = HEAD_DIM ** (-0.5)
    over_rows = (((0,), (0,)), ((), ()))
    lane = lax.broadcasted_iota(jnp.int32, (step, LANES), 1)

    def body(row, at, last):
        rows = pl.ds(row, step)
        spots = [pl.ds(t * head_width + at, LANES) for t in range(3)]
        queries, keys, values = qkv[rows, spots[0]], qkv[:last, spots[1]], qkv[:last, spots[2]]
        upstreams = grad[rows, spots[0]]
        parts = [[], [], []]
        for n, h in enumerate((slice(0, HEAD_DIM), slice(HEAD_DIM, LANES))):
            sums = jnp.where(lane == at // HEAD_DIM + n, logsum[rows, :], 0.0)
            sums = jnp.sum(sums, axis=1, keepdims=True)
            probs = jnp.exp(scores_of(queries[:, h], keys[:, h], row) - sums)
            prob_grad = lax.dot_general(
                upstreams[:, h],
                values[:, h],
                (((1,), (1,)), ((), ())),
                preferred_element_type=wide,
            )
            inner = jnp.sum(probs * prob_grad, axis=-1, keepdims=True)
            score_grad = (probs * (prob_grad - inner)).astype(low)
            parts[0].append(jnp.dot(score_grad, keys[:, h], preferred_element_type=wide))
            parts[1].append(
                lax.dot_general(score_grad, queries[:, h], over_rows, preferred_element_type=wide)
            )
            parts[2].append(
                lax.dot_general(
                    probs.astype(low), upstreams[:, h], over_rows, preferred_element_type=wide
                )
            )
        parts = [jnp.concatenate(part, axis=1) for part in parts]
        gone[rows, spots[0]] = parts[0] * scale
        gone[:last, spots[1]] += parts[1] * scale
        gone[:last, spots[2]] += parts[2]

    gone[:, head_width:] = jnp.zeros((length, 2 * head_width), wide)
    by_blocks(length, head_width, step, body)

    def turn_back(n, carry):
        rows = pl.ds(pl.multiple_of(lax.rem(n, length // step) * step, step), step)
        at = pl.multiple_of(lax.div(n, length // step) * LANES, LANES)
        value = gone[rows, pl.ds(at, LANES)].astype(low).astype(wide)
        out[rows, pl.ds(at, LANES)] = turn(value, cosine[rows, :], -sine[rows, :]).astype(low)
        return carry

    lax.fori_loop(0, length // step * (2 * head_width // LANES), turn_back, 0)
    out[:, 2 * head_width :] = gone[:, 2 * head_width :].astype(low)


def attend_back(qkv, grad, logsum, cosine, sine, entered):
    length, three = qkv.shape
    head_width = three // 3
    heads = head_width // HEAD_DIM
    whole = pl.BlockSpec(memory_space=pltpu.VMEM)
    return pl.pallas_call(
        functools.partial(attend_back_kernel, 128),
        grid=(1,),
        in_specs=[whole] * 5 + [pl.BlockSpec(memory_space=pl.ANY)],
        out_specs=pl.BlockSpec((length, three), lambda n: (0, 0)),
        out_shape=jax.ShapeDtypeStruct(entered.shape, low),
        scratch_shapes=[
            pltpu.VMEM((length, three), wide),
        ],
        input_output_aliases={5: 0},
        cost_estimate=pl.CostEstimate(
            flops=10 * heads * length * length * LANES,
            bytes_accessed=8 * length * three,
            transcendentals=heads * length * length,
        ),
        name="attend_back",
    )(qkv, grad, logsum, cosine, sine, entered)


def reject_kernel(count, hidden, grads, *refs):
    weights, (head_grad, entered) = refs[:count], refs[count:]
    depth = weights[0].shape[1]
    over = (((1,), (1,)), ((), ()))
    total = lax.dot_general(grads[:, :depth], weights[0][...], over, preferred_element_type=wide)
    for k in range(1, count):
        total = total + lax.dot_general(
            grads[:, k * depth : (k + 1) * depth],
            weights[k][...],
            over,
            preferred_element_type=wide,
        )

    @pl.when(pl.program_id(0) == 0)
    def _():
        head_grad[...] = total.astype(low)

    @pl.when(pl.program_id(0) > 0)
    def _():
        entered[...] = (total * gelu_parts(hidden[...])[1]).astype(low)


def reject(grads, weights, hidden, head_width):
    count = len(weights)
    length = grads.shape[0]
    behind, depth = weights[0].shape
    inside = behind + 2 * head_width
    return pl.pallas_call(
        functools.partial(reject_kernel, count),
        grid=(behind // head_width,),
        in_specs=[pl.BlockSpec((length, head_width), lambda t: (0, jnp.maximum(t - 1, 0)))]
        + [pl.BlockSpec((length, count * depth), lambda t: (0, 0))]
        + [pl.BlockSpec((head_width, depth), lambda t: (t, 0))] * count,
        out_specs=[
            pl.BlockSpec((length, head_width), lambda t: (0, 0)),
            pl.BlockSpec((length, head_width), lambda t: (0, jnp.maximum(t + 2, 3))),
        ],
        out_shape=[
            jax.ShapeDtypeStruct((length, head_width), low),
            jax.ShapeDtypeStruct((length, inside), low),
        ],
        cost_estimate=pl.CostEstimate(
            flops=2 * length * count * depth * behind,
            bytes_accessed=2 * count * depth * (behind + length) + 8 * length * behind,
            transcendentals=length * behind,
        ),
        name="reject",
    )(hidden, grads, *weights)


def sort_blocks(held, part, chips, kept, sent):
    rows = kept.shape[0] // chips
    for k in range(chips):
        here = slice(k * rows, (k + 1) * rows)
        for core, out in enumerate((kept, sent)):
            block = part ^ (2 * k + core)
            source = pl.ds(pl.multiple_of(block * rows, rows), rows)
            out[here, :] = held[source, :].astype(out.dtype)


def outer_kernel(left, right, *outs):
    total = lax.dot_general(
        left[...], right[...], (((0,), (0,)), ((), ())), preferred_element_type=wide
    )
    for n, out in enumerate(outs):

        @pl.when(pl.program_id(0) == n)
        def _(out=out):
            out[...] = total.astype(out.dtype)


def outer(left, right, count, left_size, right_size):
    length = left.shape[0]
    left_step = int(left.shape[1] >= count * left_size)
    flops = 2 * length * count * left_size * right_size
    kinds = [wide] + [low] * (count - 1)
    results = pl.pallas_call(
        outer_kernel,
        grid=(count,),
        in_specs=[
            pl.BlockSpec((length, left_size), lambda k: (0, k * left_step)),
            pl.BlockSpec((length, right_size), lambda k: (0, k * (1 - left_step))),
        ],
        out_specs=[pl.BlockSpec((left_size, right_size), lambda k: (0, 0))] * count,
        out_shape=[jax.ShapeDtypeStruct((left_size, right_size), kind) for kind in kinds],
        cost_estimate=pl.CostEstimate(
            flops=flops, bytes_accessed=flops // length, transcendentals=0
        ),
        name="outer",
    )(left, right)
    return results[0], list(results[1:])


def answer_kernel(count, chips, part, entered, *refs):
    weights, (kept, sent, held, slots, arrived) = refs[:count], refs[count:]
    tall = slots.shape[1]
    step = pl.program_id(0)

    def fetch(n):
        return pltpu.make_async_copy(
            weights[n].at[pl.ds(0, tall)], slots.at[n % 2], arrived.at[n % 2]
        )

    @pl.when(step == 0)
    def _():
        fetch(0).start()

    for n in range(count):

        @pl.when(step == n)
        def _(n=n):
            if n + 1 < count:
                fetch(n + 1).start()
            fetch(n).wait()

    held[...] = lax.dot_general(
        entered[...],
        slots[lax.rem(step, 2)],
        (((1,), (1,)), ((), ())),
        preferred_element_type=wide,
    )
    sort_blocks(held, part[0], chips, kept, sent)


def answer(entered, pieces, part, chips, tall):
    count = len(pieces)
    length, inside = entered.shape
    half = length // 2
    return pl.pallas_call(
        functools.partial(answer_kernel, count, chips),
        grid=(count,),
        in_specs=[
            pl.BlockSpec(memory_space=pltpu.SMEM),
            pl.BlockSpec((length, inside), lambda t: (0, 0)),
        ]
        + [pl.BlockSpec(memory_space=pl.ANY)] * count,
        out_specs=[pl.BlockSpec((half, tall), lambda t: (0, t))] * 2,
        out_shape=[
            jax.ShapeDtypeStruct((half, count * tall), wide),
            jax.ShapeDtypeStruct((half, count * tall), low),
        ],
        scratch_shapes=[
            pltpu.VMEM((length, tall), wide),
            pltpu.VMEM((2, tall, inside), low),
            pltpu.SemaphoreType.DMA((2,)),
        ],
        cost_estimate=pl.CostEstimate(
            flops=2 * length * inside * count * tall,
            bytes_accessed=2 * inside * (length + count * tall) + 3 * length * count * tall,
            transcendentals=0,
        ),
        name="answer",
    )(part[None], entered, *pieces)


def widen_rows_kernel(head_width, a, b, down, out):
    cut = b.shape[1] - head_width
    out[...] = b[0, :head_width].astype(wide)
    down[:cut] = b[0, head_width:].astype(wide)
    down[cut:] = a[0].astype(wide)


def widen_rows(all_a, all_b, head_width, width):
    count, rest, depth = all_a.shape
    tall = all_b.shape[1]
    units = rest + tall - head_width
    return pl.pallas_call(
        functools.partial(widen_rows_kernel, head_width),
        grid=(count,),
        in_specs=[
            pl.BlockSpec((1, rest, depth), lambda j: (j, 0, 0)),
            pl.BlockSpec((1, tall, depth), lambda j: (j, 0, 0)),
        ],
        out_specs=[
            pl.BlockSpec((units, depth), lambda j: (j, 0)),
            pl.BlockSpec((head_width, depth), lambda j: (j, 0)),
        ],
        out_shape=[
            jax.ShapeDtypeStruct((count * units, depth), wide),
            jax.ShapeDtypeStruct((width, depth), wide),
        ],
        cost_estimate=pl.CostEstimate(
            flops=0, bytes_accessed=6 * count * depth * (rest + tall), transcendentals=0
        ),
        name="widen_rows",
    )(all_a, all_b)


def widen_columns_kernel(groups, gathered, out):
    count, _, columns = gathered.shape
    size = columns // groups
    for j in range(count):
        for g in range(groups):
            at = (g * count + j) * size
            out[:, at : at + size] = gathered[j, :, g * size : (g + 1) * size].astype(wide)


def widen_columns(gathered, rows, groups):
    count, _, columns = gathered.shape
    tall = min(64, rows)
    moved = 6 * count * rows * columns
    return pl.pallas_call(
        functools.partial(widen_columns_kernel, groups),
        grid=(rows // tall,),
        in_specs=[pl.BlockSpec((count, tall, columns), lambda r: (0, r, 0))],
        out_specs=pl.BlockSpec((tall, count * columns), lambda r: (r, 0)),
        out_shape=jax.ShapeDtypeStruct((rows, count * columns), wide),
        cost_estimate=pl.CostEstimate(flops=0, bytes_accessed=moved, transcendentals=0),
        name="widen_columns",
    )(gathered)


def local(
    tokens,
    teacher,
    valid,
    positions,
    norm_gain,
    norm_bias,
    qkv_weight,
    qkv_bias,
    out_weight,
    out_bias,
    up_weight,
    up_bias,
    down_weight,
    down_bias,
):
    rows_here, width = tokens.shape[1:]
    seq_count = lax.axis_size("seq")
    data_count = lax.axis_size("dp")
    part = lax.axis_index("seq")
    owner = lax.axis_index("dp")
    length = rows_here * seq_count
    head_width = HEADS // seq_count * HEAD_DIM
    three = 3 * head_width
    units = up_weight.shape[1] // seq_count
    inside = three + units
    depth = qkv_weight.shape[0]

    tall = depth // 2
    behind = head_width + units

    def span(start, size, unit):
        return pl.ds(start if isinstance(start, int) else pl.multiple_of(start, unit), size)

    def block_at(row, rows, column, columns):
        return span(row, rows, ROWS), span(column, columns, LANES)

    moves = []
    for half in range(2):
        for t in range(3):
            moves.append(
                (
                    0,
                    lambda part, t=t, half=half: block_at(
                        half * tall, tall, t * width + part * head_width, head_width
                    ),
                    half,
                    block_at(0, tall, t * head_width, head_width),
                )
            )
        moves.append(
            (
                1,
                lambda part, half=half: block_at(half * tall, tall, part * units, units),
                half,
                block_at(0, tall, three, units),
            )
        )
    w_in = pick(
        (qkv_weight, up_weight),
        part[None],
        valid,
        moves,
        [(tall, inside), (tall + SPARE, inside)],
    )
    normed_low, base = enter(
        tokens[0],
        teacher[0],
        norm_gain,
        norm_bias,
        out_bias,
        down_bias,
        positions,
        after(owner, *w_in),
        data_count,
    )

    rest = behind // 2 - head_width
    moves = [
        (
            0,
            lambda part: block_at(part * head_width, head_width, 0, depth),
            0,
            block_at(0, head_width, 0, depth),
        ),
        (
            1,
            lambda part: block_at(part * units, rest, 0, depth),
            0,
            block_at(head_width, rest, 0, depth),
        ),
        (
            1,
            lambda part: block_at(part * units + rest, units - rest, 0, depth),
            1,
            block_at(0, units - rest, 0, depth),
        ),
    ]
    w_back = pick(
        (out_weight, down_weight),
        after(part[None], normed_low),
        valid,
        moves,
        [(behind // 2, depth)] * 2,
    )
    if data_count == 4:
        sides = [tuple(swap(item, "dp", k) for item in w_in) for k in (1, 2)]
        last_in = swap(sides[0][0], "dp", 2), swap(sides[1][1], "dp", 1)
        first_in = [w_in, *sides]
        w_back = lax.optimization_barrier((*w_back, *last_in))[:2]
        back_sides = [tuple(swap(item, "dp", k) for item in w_back) for k in (1, 2)]
    else:
        w_in = [w_in] + [tuple(swap(item, "dp", k) for item in w_in) for k in range(1, data_count)]
        w_back = [w_back] + [
            tuple(swap(item, "dp", k) for item in w_back) for k in range(1, data_count)
        ]
        first_in, last_in = w_in[:-1], w_in[-1]
    normed_all = gather_seq(normed_low)
    facts = normed_all[:, width : width + 2].astype(jnp.int32)
    where = facts[:, 0] * RADIX + facts[:, 1]

    half = ROTARY // 2
    lane = jnp.arange(LANES, dtype=jnp.int32) % HEAD_DIM
    freqs = rope_base ** (-((lane % half).astype(wide) * 2.0) / ROTARY)
    angles = where.astype(wide)[:, None] * jnp.where(lane < ROTARY, freqs, 0.0)[None, :]
    cosine = jnp.cos(angles)
    sine = jnp.sin(angles) * jnp.where(lane < half, -1.0, 1.0)[None, :]

    b_in = jnp.concatenate(
        [
            lax.dynamic_slice_in_dim(qkv_bias, t * width + part * head_width, head_width, 0)
            for t in range(3)
        ]
        + [lax.dynamic_slice_in_dim(up_bias, part * units, units, 0)]
    ).astype(wide)[None]

    def piece(array, k):
        return array[:, k * depth : (k + 1) * depth]

    flat_in = [item for pair in (*first_in, last_in) for item in pair]
    qkv, hidden, stacked = project(normed_all, cosine, sine, b_in, flat_in, tall, head_width)
    stacked, logsum = attend(qkv, stacked)

    counted = [item[1] for item in (*first_in, last_in)]
    if data_count == 4:
        back_sides = [tuple(after(item, stacked) for item in pair) for pair in back_sides]
        w_back = [w_back, *back_sides]
        w_back.append((swap(back_sides[0][0], "dp", 2), swap(back_sides[1][1], "dp", 1)))
    branches = emit(stacked, w_back[:-1], [], 0, data_count)
    branches = emit(stacked, w_back[-1:], counted, data_count - 1, data_count, branches)
    w_back = [jnp.concatenate(pair, axis=0) for pair in w_back]
    branches, *w_back = lax.optimization_barrier((scatter_seq(branches), *w_back))
    grad_output, grad_low, sums = grade(branches, base, valid, float(length * data_count))
    squares, count = sums[0, 0], sums[1, 0]
    grad_all = gather_seq(grad_low)
    branch_bias_grad = jnp.sum(grad_all.astype(wide), axis=0)

    def owned(left, right):
        return dot(left, right, ((0,), (0,)))

    def gather(array):
        return lax.all_gather(array, "seq", axis=0, tiled=False)

    cut = units * 5 // 8 // LANES * LANES

    def of_stacked(first, last):
        return [owned(stacked[:, first:last], piece(grad_all, k)) for k in range(data_count)]

    def prepare(pieces):
        return pieces[0], [item.astype(low) for item in pieces[1:]]

    def send(sent, *meanwhile):
        got = [swap(item, "dp", k + 1) for k, item in enumerate(sent)]
        held = lax.optimization_barrier((*got, *jax.tree.leaves(meanwhile)))
        return held[: len(got)], jax.tree.unflatten(jax.tree.structure(meanwhile), held[len(got) :])

    def total(own, got):
        for item in got:
            own = own + item.astype(wide)
        return own.astype(low)

    own_a, sent_a = prepare(of_stacked(head_width + cut, head_width + units))
    own_b, sent_b = outer(stacked, grad_all, data_count, head_width + cut, depth)
    got, ((own_b, sent_b),) = send(sent_a, (own_b, sent_b))
    down_a = total(own_a, got)
    all_a = gather(down_a)
    head_grad, in_low = reject(after(grad_all, down_a), w_back, hidden, head_width)
    own_up, sent_up = outer(normed_all, in_low[:, three:], data_count, depth, units)
    got, (head_grad, in_low, (own_up, sent_up)) = send(
        sent_b, head_grad, in_low, (own_up, sent_up)
    )
    down_b = total(own_b, got)
    all_b = gather(down_b)
    head_grad = after(head_grad, down_b)
    in_low = attend_back(qkv, head_grad, logsum, cosine, sine, in_low)
    own_qkv, sent_qkv = outer(normed_all, after(in_low, *sent_up), data_count, depth, three)
    kept, sent = answer(in_low, flat_in, part, seq_count // 2, tall)
    got, ((own_qkv, sent_qkv), kept, all_a) = send(sent_up, (own_qkv, sent_qkv), kept, all_a)
    up_grad = total(own_up, got)
    all_up = gather(up_grad)
    summed = scatter_blocks(kept, sent)
    got, (summed, all_b) = send(sent_qkv, summed, all_b)
    qkv_grad = total(own_qkv, got)
    token_grad, gain_grad, shift_grad, branch_bias_grad = leave(
        tokens[0],
        norm_gain,
        summed,
        grad_output,
        branch_bias_grad,
        owner,
        data_count,
    )

    in_bias = jnp.sum(in_low.astype(wide), axis=0)
    small = jnp.concatenate(
        [in_bias, gain_grad[0], shift_grad[0], squares[None], branch_bias_grad[0]]
    )
    small = total_dp(small[None])[0]
    branch_bias_grad = small[-width:]
    small = small[:-width]
    lines = -(-small.size // three)
    lines += -lines % 8
    high = jnp.pad(small, (0, lines * three - small.size)).reshape(lines, three)
    first = lax.reduce_precision(high, 8, 7)
    beside = jnp.concatenate([qkv_grad, first.astype(low), (high - first).astype(low)])

    down_weight_grad, out_weight_grad = widen_rows(all_a, all_b, head_width, width)
    all_qkv = gather(after(beside, all_up))
    up_weight_grad = widen_columns(all_up, depth, 1)
    all_qkv = after(all_qkv, down_weight_grad, up_weight_grad)
    qkv_weight_grad = widen_columns(all_qkv, depth, 3)
    slots = all_qkv[:, depth:].astype(wide)
    slots = (slots[:, :lines] + slots[:, lines:]).reshape(seq_count, -1)
    norm_grads = jnp.sum(slots[:, inside : inside + 2 * width + 1], axis=0)
    qkv_bias_grad = slots[:, :three].reshape(seq_count, 3, head_width).transpose(1, 0, 2)
    up_bias_grad = slots[:, three:inside].reshape(-1)
    loss = norm_grads[-1] / (2.0 * width * count)
    return (
        loss,
        token_grad[None],
        norm_grads[:width],
        norm_grads[width : 2 * width],
        qkv_weight_grad,
        qkv_bias_grad.reshape(-1),
        out_weight_grad,
        branch_bias_grad,
        up_weight_grad,
        up_bias_grad,
        down_weight_grad,
        branch_bias_grad,
    )


def solution(mesh):
    placed = (
        P("dp", "seq", None),
        P("dp", "seq", None),
        P("dp", "seq"),
        P("dp", "seq"),
        P(),
        P(),
        P("dp", None),
        P(),
        P(None, "dp"),
        P(),
        P("dp", None),
        P(),
        P(None, "dp"),
        P(),
    )
    return jax.shard_map(
        local,
        mesh=mesh,
        in_specs=placed,
        out_specs=(
            P(),
            P("dp", "seq", None),
            P(),
            P(),
            P("dp", None),
            P(),
            P(None, "dp"),
            P(),
            P("dp", None),
            P(),
            P(None, "dp"),
            P(),
        ),
        check_vma=False,
    )
```

```python
import functools

import jax
import jax.numpy as jnp
from jax import lax
from jax.experimental import pallas as pl
from jax.experimental.pallas import tpu as pltpu
from jax.sharding import PartitionSpec as P

HEADS = 32
HEAD_DIM = 64
ROTARY = 32


norm_eps = 1e-05
rope_base = 10000.0
masked_fill = -1e30
LANES = 128
RADIX = 64
DIGIT = 16
SPARE = 16
ROWS = 64

low = jnp.bfloat16
wide = jnp.float32


def dot(a, b, dims):
    return lax.dot_general(a, b, (dims, ((), ())), preferred_element_type=wide)


def after(array, *earlier):
    return lax.optimization_barrier((array, *earlier))[0]


def swap(array, axis, bit):
    return lax.ppermute(array, axis, [(s, s ^ bit) for s in range(lax.axis_size(axis))])


def gather_seq(rows):
    return lax.all_gather(rows, "seq", axis=0, tiled=True)


def between(array, pairs):
    return lax.ppermute(
        array, "seq", [(2 * a + core, 2 * b + core) for a, b in pairs for core in range(2)]
    )


def scatter_chips(blocks):
    chips = len(blocks)
    if chips != 4:
        total = blocks[0]
        for k in range(1, chips):
            total = total + swap(blocks[k].astype(low), "seq", 2 * k).astype(wide)
        return total
    chip = lax.axis_index("seq") // 2
    far = between(blocks[3].astype(low), [(0, 1), (3, 2)])
    passed = (blocks[2] + far.astype(wide)).astype(low)
    upward = between(passed, [(0, 1), (1, 2)])
    downward = between(passed, [(3, 2), (2, 1)])
    upward = jnp.where(chip == 1, blocks[3], blocks[1]) + upward.astype(wide)
    downward = jnp.where(chip == 2, blocks[3], blocks[1]) + downward.astype(wide)
    upward = between(upward.astype(low), [(0, 1), (1, 2), (2, 3)])
    downward = between(downward.astype(low), [(3, 2), (2, 1), (1, 0)])
    return blocks[0] + upward.astype(wide) + downward.astype(wide)


def scatter_blocks(kept, sent):
    chips = lax.axis_size("seq") // 2
    rows = kept.shape[0] // chips
    chip = kept + swap(sent, "seq", 1).astype(wide)
    return scatter_chips([chip[k * rows : (k + 1) * rows] for k in range(chips)])


def scatter_seq(partial):
    return lax.psum_scatter(partial, "seq", scatter_dimension=0, tiled=True)


def total_dp(array):
    items = [array] + [swap(array, "dp", k) for k in range(1, lax.axis_size("dp"))]
    while len(items) > 1:
        items = [a + b for a, b in zip(items[::2], items[1::2])]
    return items[0]


def normalise(values):
    centre = values - jnp.mean(values, axis=-1, keepdims=True)
    spread = jnp.mean(centre * centre, axis=-1, keepdims=True)
    rstd = lax.rsqrt(spread + norm_eps)
    return centre * rstd, rstd


def enter_kernel(
    owners, owner, tokens, teacher, gain, shift, bias_a, bias_b, place, normed, base, held, kept
):
    inputs = tokens[...].astype(wide)
    xhat, _ = normalise(inputs)
    held[...] = xhat * gain[...].astype(wide)[None] + shift[...].astype(wide)[None]
    biases = (bias_a[...].astype(wide) + bias_b[...].astype(wide))[None]
    kept[...] = inputs + biases - teacher[...].astype(wide)
    width = inputs.shape[1]
    depth = width // owners
    for k in range(owners):
        theirs = pl.ds(pl.multiple_of((owner[0] ^ k) * depth, LANES), depth)
        normed[:, k * depth : (k + 1) * depth] = held[:, theirs].astype(low)
        base[:, k * depth : (k + 1) * depth] = kept[:, theirs]
    lane = lax.broadcasted_iota(jnp.int32, (inputs.shape[0], LANES), 1)
    ids = column_of(place[...]).astype(jnp.int32)
    facts = jnp.where(lane == 0, ids // RADIX, ids % RADIX)
    normed[:, width:] = facts.astype(wide).astype(low)


def enter(tokens, teacher, gain, shift, bias_a, bias_b, place, owner, owners):
    rows, width = tokens.shape
    whole = pl.BlockSpec(memory_space=pltpu.VMEM)
    return pl.pallas_call(
        functools.partial(enter_kernel, owners),
        in_specs=[pl.BlockSpec(memory_space=pltpu.SMEM)] + [whole] * 7,
        out_specs=[whole] * 2,
        out_shape=[
            jax.ShapeDtypeStruct((rows, width + LANES), low),
            jax.ShapeDtypeStruct((rows, width), wide),
        ],
        scratch_shapes=[pltpu.VMEM((rows, width), wide)] * 2,
        name="enter",
    )(
        owner[None],
        tokens,
        teacher,
        gain,
        shift,
        bias_a,
        bias_b,
        place,
    )


def column_of(row):
    size = row.shape[1]
    here = lax.broadcasted_iota(jnp.int32, (size, size), 0)
    there = lax.broadcasted_iota(jnp.int32, (size, size), 1)
    return jnp.sum(jnp.where(here == there, row.astype(wide), 0.0), axis=1, keepdims=True)


def grade_kernel(scale, branches, base, valid, grad, grad_low, sums):
    width = base.shape[1]
    lane = lax.broadcasted_iota(jnp.int32, (1, LANES), 1)
    weight = jnp.where(lane == 1, float(DIGIT), jnp.where(lane == 2, float(DIGIT * DIGIT), 1.0))
    digits = jnp.where(lane < 3, branches[:1, width:].astype(wide) * weight, 0.0)
    count = jnp.sum(digits, axis=1, keepdims=True)
    error = base[...] + branches[:, :width].astype(wide)
    weighted = column_of(valid[...]) * error
    squares = jnp.sum(jnp.sum(weighted * error, axis=0, keepdims=True), axis=1, keepdims=True)
    result = scale / count * weighted
    grad[...] = result
    grad_low[...] = result.astype(low)
    line = lax.broadcasted_iota(jnp.int32, sums.shape, 0)
    sums[...] = jnp.where(line == 0, squares, count)


def grade(branches, base, valid, scale):
    whole = pl.BlockSpec(memory_space=pltpu.VMEM)
    return pl.pallas_call(
        functools.partial(grade_kernel, scale),
        in_specs=[whole] * 3,
        out_specs=[whole] * 3,
        out_shape=[
            jax.ShapeDtypeStruct(base.shape, wide),
            jax.ShapeDtypeStruct(base.shape, low),
            jax.ShapeDtypeStruct((8, LANES), wide),
        ],
        cost_estimate=pl.CostEstimate(
            flops=4 * base.size, bytes_accessed=12 * base.size, transcendentals=0
        ),
        name="grade",
    )(branches, base, valid)


def leave_kernel(
    owners, owner, tokens, gain, summed, grad, bias, token_grad, gain_grad, shift_grad, bias_grad
):
    inputs = tokens[...].astype(wide)
    xhat, rstd = normalise(inputs)
    depth = inputs.shape[1] // owners
    for k in range(owners):
        theirs = pl.ds(pl.multiple_of((owner[0] ^ k) * depth, LANES), depth)
        token_grad[:, theirs] = summed[:, k * depth : (k + 1) * depth]
        bias_grad[:, theirs] = bias[:, k * depth : (k + 1) * depth]
    normed_grad = token_grad[...]
    gain_grad[...] = jnp.sum(normed_grad * xhat, axis=0, keepdims=True)
    shift_grad[...] = jnp.sum(normed_grad, axis=0, keepdims=True)
    scaled = normed_grad * gain[...].astype(wide)[None]
    token_grad[...] = rstd * (
        scaled
        - jnp.mean(scaled, axis=-1, keepdims=True)
        - xhat * jnp.mean(scaled * xhat, axis=-1, keepdims=True)
    )
    for k in range(owners):
        theirs = pl.ds(pl.multiple_of((owner[0] ^ k) * depth, LANES), depth)
        token_grad[:, theirs] += grad[:, k * depth : (k + 1) * depth]


def leave(tokens, gain, summed, grad, bias, owner, owners):
    rows, width = tokens.shape
    whole = pl.BlockSpec(memory_space=pltpu.VMEM)
    line = jax.ShapeDtypeStruct((1, width), wide)
    return pl.pallas_call(
        functools.partial(leave_kernel, owners),
        in_specs=[pl.BlockSpec(memory_space=pltpu.SMEM)] + [whole] * 5,
        out_specs=[whole] * 4,
        out_shape=[jax.ShapeDtypeStruct((rows, width), wide), line, line, line],
        name="leave",
    )(owner[None], tokens, gain, summed, grad, bias[None])


def pick_kernel(moves, part, counted, a, b, *refs):
    outs, arrived = refs[:2], refs[2]
    copies = []
    for which, source, half, target in moves:
        copies.append(
            pltpu.make_async_copy(
                (a, b)[which].at[source(part[0])],
                outs[half].at[target],
                arrived.at[len(copies)],
            )
        )
    for copy in copies:
        copy.start()
    tall = outs[0].shape[0]
    more = outs[1].shape[0] - tall
    if more:
        count = jnp.sum(counted[...].astype(wide), axis=1, keepdims=True)
        outs[1][tall:, :] = jnp.broadcast_to(count, (more, outs[1].shape[1])).astype(low)
    for copy in copies:
        copy.wait()


def pick(arrays, part, counted, moves, shapes):
    moved = 4 * sum(shape[0] * shape[1] for shape in shapes)
    return pl.pallas_call(
        functools.partial(pick_kernel, moves),
        in_specs=[
            pl.BlockSpec(memory_space=pltpu.SMEM),
            pl.BlockSpec(memory_space=pltpu.VMEM),
        ]
        + [pl.BlockSpec(memory_space=pl.ANY)] * 2,
        out_specs=[pl.BlockSpec(memory_space=pltpu.VMEM)] * 2,
        out_shape=[jax.ShapeDtypeStruct(shape, low) for shape in shapes],
        scratch_shapes=[pltpu.SemaphoreType.DMA((len(moves),))],
        cost_estimate=pl.CostEstimate(flops=0, bytes_accessed=moved, transcendentals=0),
        name="pick",
    )(part, counted, *arrays)


def gelu_parts(values):
    root = (2.0 / jnp.pi) ** 0.5
    square = values * values
    bent = jnp.tanh(root * (values + 0.044715 * (values * square)))
    factor = 0.5 * (1.0 + bent)
    slope = 0.5 * values * (1.0 - bent * bent) * (root * (1.0 + 3.0 * 0.044715 * square))
    return factor, factor + slope


def turn(values, cosine, sine):
    lane = lax.broadcasted_iota(jnp.int32, values.shape, 1) % HEAD_DIM
    half, width = ROTARY // 2, values.shape[1]
    partner = jnp.where(
        lane < half, pltpu.roll(values, width - half, 1), pltpu.roll(values, half, 1)
    )
    return values * cosine + partner * sine


def project_kernel(count, normed, cosine, sine, bias, *refs):
    weights, (qkv, hidden, stacked) = refs[:count], refs[count:]
    tile = pl.program_id(0)
    tall = normed.shape[1] // count
    total = bias[...]
    for k in range(count):
        block = normed[:, k * tall : (k + 1) * tall]
        total = total + jnp.dot(block, weights[k][...], preferred_element_type=wide)
    repeats = total.shape[1] // LANES

    @pl.when(tile < 2)
    def _():
        turned = turn(
            total,
            jnp.concatenate([cosine[...]] * repeats, axis=1),
            jnp.concatenate([sine[...]] * repeats, axis=1),
        )
        qkv[...] = turned.astype(low)

    @pl.when(tile == 2)
    def _():
        qkv[...] = total.astype(low)

    @pl.when(tile > 2)
    def _():
        hidden[...] = total
        stacked[...] = (total * gelu_parts(total)[0]).astype(low)


def project(normed, cosine, sine, bias, weights, tall, head_width):
    count = len(weights)
    length = normed.shape[0]
    inside = weights[0].shape[1]
    units = inside - 3 * head_width
    table = pl.BlockSpec((length, LANES), lambda t: (0, 0))
    return pl.pallas_call(
        functools.partial(project_kernel, count),
        grid=(inside // head_width,),
        in_specs=[
            pl.BlockSpec((length, count * tall), lambda t: (0, 0)),
            table,
            table,
            pl.BlockSpec((1, head_width), lambda t: (0, t)),
        ]
        + [pl.BlockSpec((tall, head_width), lambda t: (0, t))] * count,
        out_specs=[
            pl.BlockSpec((length, head_width), lambda t: (0, jnp.minimum(t, 2))),
            pl.BlockSpec((length, head_width), lambda t: (0, jnp.maximum(t - 3, 0))),
            pl.BlockSpec((length, head_width), lambda t: (0, jnp.maximum(t - 2, 1))),
        ],
        out_shape=[
            jax.ShapeDtypeStruct((length, 3 * head_width), low),
            jax.ShapeDtypeStruct((length, units), wide),
            jax.ShapeDtypeStruct((length, head_width + units), low),
        ],
        cost_estimate=pl.CostEstimate(
            flops=2 * length * count * tall * inside,
            bytes_accessed=2 * count * tall * (inside + length) + 8 * length * inside,
            transcendentals=length * units,
        ),
        name="project",
    )(normed, cosine, sine, bias, *weights)


def emit_kernel(owners, counts, stacked, *refs):
    counted, refs = refs[:counts], refs[counts:]
    weights, (out, slots, arrived) = refs[: 2 * owners], refs[-3:]
    middle, size = slots.shape[2:]
    step = pl.program_id(0)

    def fetch(n):
        columns = pl.ds(n % 2 * size, size)
        return [
            pltpu.make_async_copy(
                weights[n // 2 * 2 + half].at[:, columns],
                slots.at[n % 2, half],
                arrived.at[n % 2, half],
            )
            for half in range(2)
        ]

    @pl.when(step == 0)
    def _():
        for copy in fetch(0):
            copy.start()

    for n in range(2 * owners):

        @pl.when(step == n)
        def _(n=n):
            if n + 1 < 2 * owners:
                for copy in fetch(n + 1):
                    copy.start()
            for copy in fetch(n):
                copy.wait()

    @pl.when(step < 2 * owners)
    def _():
        slot = lax.rem(step, 2)
        total = jnp.dot(stacked[:, :middle], slots[slot, 0], preferred_element_type=wide)
        total = total + jnp.dot(stacked[:, middle:], slots[slot, 1], preferred_element_type=wide)
        out[...] = total.astype(low)

    if not counted:
        return

    @pl.when(step == 2 * owners)
    def _():
        count = counted[0][...].astype(wide)
        for ref in counted[1:]:
            count = count + ref[...].astype(wide)
        count = count[:1].astype(jnp.int32)
        lane = lax.broadcasted_iota(jnp.int32, count.shape, 1)
        digits = jnp.where(lane == 0, count, count // DIGIT)
        digits = jnp.where(lane == 2, count // (DIGIT * DIGIT), digits) % DIGIT
        out[:, :LANES] = jnp.broadcast_to(digits.astype(wide), (out.shape[0], LANES)).astype(low)


def emit(stacked, weights, counted, first, all_owners, into=None):
    owners = len(weights)
    length, behind = stacked.shape
    middle, depth = weights[0][0].shape
    size = depth // 2
    steps = 2 * owners + (first + owners == all_owners)

    row = size // SPARE
    operands = [stacked, *counted, *[item for pair in weights for item in pair]]
    in_specs = [pl.BlockSpec((length, behind), lambda t: (0, 0))]
    in_specs += [pl.BlockSpec((SPARE, LANES), lambda t: (row, 0))] * len(counted)
    in_specs += [pl.BlockSpec(memory_space=pl.ANY)] * (2 * owners)
    aliases = {}
    if into is not None:
        aliases = {len(operands): 0}
        operands.append(into)
        in_specs.append(pl.BlockSpec(memory_space=pl.ANY))
    return pl.pallas_call(
        functools.partial(emit_kernel, owners, len(counted)),
        grid=(steps,),
        in_specs=in_specs,
        out_specs=pl.BlockSpec((length, size), lambda t: (0, 2 * first + t)),
        out_shape=jax.ShapeDtypeStruct((length, all_owners * depth + LANES), low),
        input_output_aliases=aliases,
        scratch_shapes=[
            pltpu.VMEM((2, 2, middle, size), low),
            pltpu.SemaphoreType.DMA((2, 2)),
        ],
        cost_estimate=pl.CostEstimate(
            flops=2 * length * behind * owners * depth,
            bytes_accessed=2 * behind * (length + owners * depth) + 2 * length * steps * size,
            transcendentals=0,
        ),
        name="emit",
    )(*operands)


def scores_of(rows, keys, start):
    raw = lax.dot_general(rows, keys, (((1,), (1,)), ((), ())), preferred_element_type=wide)
    place = start + lax.broadcasted_iota(jnp.int32, raw.shape, 0)
    kept = lax.broadcasted_iota(jnp.int32, raw.shape, 1) <= place
    return jnp.where(kept, raw * HEAD_DIM ** (-0.5), masked_fill)


def by_blocks(length, head_width, step, body):
    pairs = head_width // LANES
    blocks = length // 2 // step
    for half in range(2):

        def one(n, carry, half=half):
            row = pl.multiple_of(half * (length // 2) + lax.rem(n, blocks) * step, step)
            body(row, pl.multiple_of(lax.div(n, blocks) * LANES, LANES), (half + 1) * length // 2)
            return carry

        lax.fori_loop(0, pairs * blocks, one, 0)


def attend_kernel(step, qkv, stacked, out, logsum):
    del stacked
    length, head_width = out.shape
    lane = lax.broadcasted_iota(jnp.int32, (step, LANES), 1)

    def body(row, at, last):
        rows = pl.ds(row, step)
        queries = qkv[rows, pl.ds(at, LANES)]
        keys = qkv[:last, pl.ds(head_width + at, LANES)]
        values = qkv[:last, pl.ds(2 * head_width + at, LANES)]
        sums = logsum[rows, :]
        outs = []
        for n, h in enumerate((slice(0, HEAD_DIM), slice(HEAD_DIM, LANES))):
            scores = scores_of(queries[:, h], keys[:, h], row)
            top = jnp.max(scores, axis=-1, keepdims=True)
            expd = jnp.exp(scores - top)
            total = jnp.sum(expd, axis=-1, keepdims=True)
            probs = (expd * (1.0 / total)).astype(low)
            outs.append(jnp.dot(probs, values[:, h], preferred_element_type=wide))
            sums = jnp.where(lane == at // HEAD_DIM + n, top + jnp.log(total), sums)
        out[rows, pl.ds(at, LANES)] = jnp.concatenate(outs, axis=1).astype(low)
        logsum[rows, :] = sums

    logsum[...] = jnp.zeros(logsum.shape, wide)
    by_blocks(length, head_width, step, body)


def attend(qkv, stacked):
    length, three = qkv.shape
    head_width = three // 3
    heads = head_width // HEAD_DIM
    whole = pl.BlockSpec(memory_space=pltpu.VMEM)
    return pl.pallas_call(
        functools.partial(attend_kernel, 256),
        grid=(1,),
        in_specs=[whole, pl.BlockSpec(memory_space=pl.ANY)],
        out_specs=[pl.BlockSpec((length, head_width), lambda n: (0, 0)), whole],
        out_shape=[
            jax.ShapeDtypeStruct(stacked.shape, low),
            jax.ShapeDtypeStruct((length, LANES), wide),
        ],
        input_output_aliases={1: 0},
        cost_estimate=pl.CostEstimate(
            flops=4 * heads * length * length * LANES,
            bytes_accessed=8 * length * three,
            transcendentals=heads * length * length,
        ),
        name="attend",
    )(qkv, stacked)


def attend_back_kernel(step, qkv, grad, logsum, cosine, sine, entered, out, gone):
    del entered
    length, head_width = grad.shape
    scale = HEAD_DIM ** (-0.5)
    over_rows = (((0,), (0,)), ((), ()))
    lane = lax.broadcasted_iota(jnp.int32, (step, LANES), 1)

    def body(row, at, last):
        rows = pl.ds(row, step)
        spots = [pl.ds(t * head_width + at, LANES) for t in range(3)]
        queries, keys, values = qkv[rows, spots[0]], qkv[:last, spots[1]], qkv[:last, spots[2]]
        upstreams = grad[rows, spots[0]]
        parts = [[], [], []]
        for n, h in enumerate((slice(0, HEAD_DIM), slice(HEAD_DIM, LANES))):
            sums = jnp.where(lane == at // HEAD_DIM + n, logsum[rows, :], 0.0)
            sums = jnp.sum(sums, axis=1, keepdims=True)
            probs = jnp.exp(scores_of(queries[:, h], keys[:, h], row) - sums)
            prob_grad = lax.dot_general(
                upstreams[:, h],
                values[:, h],
                (((1,), (1,)), ((), ())),
                preferred_element_type=wide,
            )
            inner = jnp.sum(probs * prob_grad, axis=-1, keepdims=True)
            score_grad = (probs * (prob_grad - inner)).astype(low)
            parts[0].append(jnp.dot(score_grad, keys[:, h], preferred_element_type=wide))
            parts[1].append(
                lax.dot_general(score_grad, queries[:, h], over_rows, preferred_element_type=wide)
            )
            parts[2].append(
                lax.dot_general(
                    probs.astype(low), upstreams[:, h], over_rows, preferred_element_type=wide
                )
            )
        parts = [jnp.concatenate(part, axis=1) for part in parts]
        gone[rows, spots[0]] = parts[0] * scale
        gone[:last, spots[1]] += parts[1] * scale
        gone[:last, spots[2]] += parts[2]

    gone[:, head_width:] = jnp.zeros((length, 2 * head_width), wide)
    by_blocks(length, head_width, step, body)

    def turn_back(n, carry):
        rows = pl.ds(pl.multiple_of(lax.rem(n, length // step) * step, step), step)
        at = pl.multiple_of(lax.div(n, length // step) * LANES, LANES)
        value = gone[rows, pl.ds(at, LANES)].astype(low).astype(wide)
        out[rows, pl.ds(at, LANES)] = turn(value, cosine[rows, :], -sine[rows, :]).astype(low)
        return carry

    lax.fori_loop(0, length // step * (2 * head_width // LANES), turn_back, 0)
    out[:, 2 * head_width :] = gone[:, 2 * head_width :].astype(low)


def attend_back(qkv, grad, logsum, cosine, sine, entered):
    length, three = qkv.shape
    head_width = three // 3
    heads = head_width // HEAD_DIM
    whole = pl.BlockSpec(memory_space=pltpu.VMEM)
    return pl.pallas_call(
        functools.partial(attend_back_kernel, 128),
        grid=(1,),
        in_specs=[whole] * 5 + [pl.BlockSpec(memory_space=pl.ANY)],
        out_specs=pl.BlockSpec((length, three), lambda n: (0, 0)),
        out_shape=jax.ShapeDtypeStruct(entered.shape, low),
        scratch_shapes=[
            pltpu.VMEM((length, three), wide),
        ],
        input_output_aliases={5: 0},
        cost_estimate=pl.CostEstimate(
            flops=10 * heads * length * length * LANES,
            bytes_accessed=8 * length * three,
            transcendentals=heads * length * length,
        ),
        name="attend_back",
    )(qkv, grad, logsum, cosine, sine, entered)


def reject_kernel(count, hidden, grads, *refs):
    weights, (head_grad, entered) = refs[:count], refs[count:]
    depth = weights[0].shape[1]
    over = (((1,), (1,)), ((), ()))
    total = lax.dot_general(grads[:, :depth], weights[0][...], over, preferred_element_type=wide)
    for k in range(1, count):
        total = total + lax.dot_general(
            grads[:, k * depth : (k + 1) * depth],
            weights[k][...],
            over,
            preferred_element_type=wide,
        )

    @pl.when(pl.program_id(0) == 0)
    def _():
        head_grad[...] = total.astype(low)

    @pl.when(pl.program_id(0) > 0)
    def _():
        entered[...] = (total * gelu_parts(hidden[...])[1]).astype(low)


def reject(grads, weights, hidden, head_width):
    count = len(weights)
    length = grads.shape[0]
    behind, depth = weights[0].shape
    inside = behind + 2 * head_width
    return pl.pallas_call(
        functools.partial(reject_kernel, count),
        grid=(behind // head_width,),
        in_specs=[pl.BlockSpec((length, head_width), lambda t: (0, jnp.maximum(t - 1, 0)))]
        + [pl.BlockSpec((length, count * depth), lambda t: (0, 0))]
        + [pl.BlockSpec((head_width, depth), lambda t: (t, 0))] * count,
        out_specs=[
            pl.BlockSpec((length, head_width), lambda t: (0, 0)),
            pl.BlockSpec((length, head_width), lambda t: (0, jnp.maximum(t + 2, 3))),
        ],
        out_shape=[
            jax.ShapeDtypeStruct((length, head_width), low),
            jax.ShapeDtypeStruct((length, inside), low),
        ],
        cost_estimate=pl.CostEstimate(
            flops=2 * length * count * depth * behind,
            bytes_accessed=2 * count * depth * (behind + length) + 8 * length * behind,
            transcendentals=length * behind,
        ),
        name="reject",
    )(hidden, grads, *weights)


def sort_blocks(held, part, chips, kept, sent):
    rows = kept.shape[0] // chips
    for k in range(chips):
        here = slice(k * rows, (k + 1) * rows)
        for core, out in enumerate((kept, sent)):
            block = part ^ (2 * k + core)
            source = pl.ds(pl.multiple_of(block * rows, rows), rows)
            out[here, :] = held[source, :].astype(out.dtype)


def outer_kernel(left, right, *outs):
    total = lax.dot_general(
        left[...], right[...], (((0,), (0,)), ((), ())), preferred_element_type=wide
    )
    for n, out in enumerate(outs):

        @pl.when(pl.program_id(0) == n)
        def _(out=out):
            out[...] = total.astype(out.dtype)


def outer(left, right, count, left_size, right_size):
    length = left.shape[0]
    left_step = int(left.shape[1] >= count * left_size)
    flops = 2 * length * count * left_size * right_size
    kinds = [wide] + [low] * (count - 1)
    results = pl.pallas_call(
        outer_kernel,
        grid=(count,),
        in_specs=[
            pl.BlockSpec((length, left_size), lambda k: (0, k * left_step)),
            pl.BlockSpec((length, right_size), lambda k: (0, k * (1 - left_step))),
        ],
        out_specs=[pl.BlockSpec((left_size, right_size), lambda k: (0, 0))] * count,
        out_shape=[jax.ShapeDtypeStruct((left_size, right_size), kind) for kind in kinds],
        cost_estimate=pl.CostEstimate(
            flops=flops, bytes_accessed=flops // length, transcendentals=0
        ),
        name="outer",
    )(left, right)
    return results[0], list(results[1:])


def answer_kernel(count, chips, part, entered, *refs):
    weights, (kept, sent, held, slots, arrived) = refs[:count], refs[count:]
    tall = slots.shape[1]
    step = pl.program_id(0)

    def fetch(n):
        return pltpu.make_async_copy(
            weights[n].at[pl.ds(0, tall)], slots.at[n % 2], arrived.at[n % 2]
        )

    @pl.when(step == 0)
    def _():
        fetch(0).start()

    for n in range(count):

        @pl.when(step == n)
        def _(n=n):
            if n + 1 < count:
                fetch(n + 1).start()
            fetch(n).wait()

    held[...] = lax.dot_general(
        entered[...],
        slots[lax.rem(step, 2)],
        (((1,), (1,)), ((), ())),
        preferred_element_type=wide,
    )
    sort_blocks(held, part[0], chips, kept, sent)


def answer(entered, pieces, part, chips, tall):
    count = len(pieces)
    length, inside = entered.shape
    half = length // 2
    return pl.pallas_call(
        functools.partial(answer_kernel, count, chips),
        grid=(count,),
        in_specs=[
            pl.BlockSpec(memory_space=pltpu.SMEM),
            pl.BlockSpec((length, inside), lambda t: (0, 0)),
        ]
        + [pl.BlockSpec(memory_space=pl.ANY)] * count,
        out_specs=[pl.BlockSpec((half, tall), lambda t: (0, t))] * 2,
        out_shape=[
            jax.ShapeDtypeStruct((half, count * tall), wide),
            jax.ShapeDtypeStruct((half, count * tall), low),
        ],
        scratch_shapes=[
            pltpu.VMEM((length, tall), wide),
            pltpu.VMEM((2, tall, inside), low),
            pltpu.SemaphoreType.DMA((2,)),
        ],
        cost_estimate=pl.CostEstimate(
            flops=2 * length * inside * count * tall,
            bytes_accessed=2 * inside * (length + count * tall) + 3 * length * count * tall,
            transcendentals=0,
        ),
        name="answer",
    )(part[None], entered, *pieces)


def widen_rows_kernel(head_width, a, b, down, out):
    cut = b.shape[1] - head_width
    out[...] = b[0, :head_width].astype(wide)
    down[:cut] = b[0, head_width:].astype(wide)
    down[cut:] = a[0].astype(wide)


def widen_rows(all_a, all_b, head_width, width):
    count, rest, depth = all_a.shape
    tall = all_b.shape[1]
    units = rest + tall - head_width
    return pl.pallas_call(
        functools.partial(widen_rows_kernel, head_width),
        grid=(count,),
        in_specs=[
            pl.BlockSpec((1, rest, depth), lambda j: (j, 0, 0)),
            pl.BlockSpec((1, tall, depth), lambda j: (j, 0, 0)),
        ],
        out_specs=[
            pl.BlockSpec((units, depth), lambda j: (j, 0)),
            pl.BlockSpec((head_width, depth), lambda j: (j, 0)),
        ],
        out_shape=[
            jax.ShapeDtypeStruct((count * units, depth), wide),
            jax.ShapeDtypeStruct((width, depth), wide),
        ],
        cost_estimate=pl.CostEstimate(
            flops=0, bytes_accessed=6 * count * depth * (rest + tall), transcendentals=0
        ),
        name="widen_rows",
    )(all_a, all_b)


def widen_columns_kernel(groups, gathered, out):
    count, _, columns = gathered.shape
    size = columns // groups
    for j in range(count):
        for g in range(groups):
            at = (g * count + j) * size
            out[:, at : at + size] = gathered[j, :, g * size : (g + 1) * size].astype(wide)


def widen_columns(gathered, rows, groups):
    count, _, columns = gathered.shape
    tall = min(128, rows)
    moved = 6 * count * rows * columns
    return pl.pallas_call(
        functools.partial(widen_columns_kernel, groups),
        grid=(rows // tall,),
        in_specs=[pl.BlockSpec((count, tall, columns), lambda r: (0, r, 0))],
        out_specs=pl.BlockSpec((tall, count * columns), lambda r: (r, 0)),
        out_shape=jax.ShapeDtypeStruct((rows, count * columns), wide),
        cost_estimate=pl.CostEstimate(flops=0, bytes_accessed=moved, transcendentals=0),
        name="widen_columns",
    )(gathered)


def local(
    tokens,
    teacher,
    valid,
    positions,
    norm_gain,
    norm_bias,
    qkv_weight,
    qkv_bias,
    out_weight,
    out_bias,
    up_weight,
    up_bias,
    down_weight,
    down_bias,
):
    rows_here, width = tokens.shape[1:]
    seq_count = lax.axis_size("seq")
    data_count = lax.axis_size("dp")
    part = lax.axis_index("seq")
    owner = lax.axis_index("dp")
    length = rows_here * seq_count
    head_width = HEADS // seq_count * HEAD_DIM
    three = 3 * head_width
    units = up_weight.shape[1] // seq_count
    inside = three + units
    depth = qkv_weight.shape[0]

    tall = depth // 2
    behind = head_width + units

    def span(start, size, unit):
        return pl.ds(start if isinstance(start, int) else pl.multiple_of(start, unit), size)

    def block_at(row, rows, column, columns):
        return span(row, rows, ROWS), span(column, columns, LANES)

    moves = []
    for half in range(2):
        for t in range(3):
            moves.append(
                (
                    0,
                    lambda part, t=t, half=half: block_at(
                        half * tall, tall, t * width + part * head_width, head_width
                    ),
                    half,
                    block_at(0, tall, t * head_width, head_width),
                )
            )
        moves.append(
            (
                1,
                lambda part, half=half: block_at(half * tall, tall, part * units, units),
                half,
                block_at(0, tall, three, units),
            )
        )
    w_in = pick(
        (qkv_weight, up_weight),
        part[None],
        valid,
        moves,
        [(tall, inside), (tall + SPARE, inside)],
    )
    normed_low, base = enter(
        tokens[0],
        teacher[0],
        norm_gain,
        norm_bias,
        out_bias,
        down_bias,
        positions,
        after(owner, *w_in),
        data_count,
    )

    rest = behind // 2 - head_width
    moves = [
        (
            0,
            lambda part: block_at(part * head_width, head_width, 0, depth),
            0,
            block_at(0, head_width, 0, depth),
        ),
        (
            1,
            lambda part: block_at(part * units, rest, 0, depth),
            0,
            block_at(head_width, rest, 0, depth),
        ),
        (
            1,
            lambda part: block_at(part * units + rest, units - rest, 0, depth),
            1,
            block_at(0, units - rest, 0, depth),
        ),
    ]
    w_back = pick(
        (out_weight, down_weight),
        after(part[None], normed_low),
        valid,
        moves,
        [(behind // 2, depth)] * 2,
    )
    if data_count == 4:
        sides = [tuple(swap(item, "dp", k) for item in w_in) for k in (1, 2)]
        last_in = swap(sides[0][0], "dp", 2), swap(sides[1][1], "dp", 1)
        first_in = [w_in, *sides]
        w_back = lax.optimization_barrier((*w_back, *last_in))[:2]
        back_sides = [tuple(swap(item, "dp", k) for item in w_back) for k in (1, 2)]
    else:
        w_in = [w_in] + [tuple(swap(item, "dp", k) for item in w_in) for k in range(1, data_count)]
        w_back = [w_back] + [
            tuple(swap(item, "dp", k) for item in w_back) for k in range(1, data_count)
        ]
        first_in, last_in = w_in[:-1], w_in[-1]
    normed_all = gather_seq(normed_low)
    facts = normed_all[:, width : width + 2].astype(jnp.int32)
    where = facts[:, 0] * RADIX + facts[:, 1]

    half = ROTARY // 2
    lane = jnp.arange(LANES, dtype=jnp.int32) % HEAD_DIM
    freqs = rope_base ** (-((lane % half).astype(wide) * 2.0) / ROTARY)
    angles = where.astype(wide)[:, None] * jnp.where(lane < ROTARY, freqs, 0.0)[None, :]
    cosine = jnp.cos(angles)
    sine = jnp.sin(angles) * jnp.where(lane < half, -1.0, 1.0)[None, :]

    b_in = jnp.concatenate(
        [
            lax.dynamic_slice_in_dim(qkv_bias, t * width + part * head_width, head_width, 0)
            for t in range(3)
        ]
        + [lax.dynamic_slice_in_dim(up_bias, part * units, units, 0)]
    ).astype(wide)[None]

    def piece(array, k):
        return array[:, k * depth : (k + 1) * depth]

    flat_in = [item for pair in (*first_in, last_in) for item in pair]
    qkv, hidden, stacked = project(normed_all, cosine, sine, b_in, flat_in, tall, head_width)
    stacked, logsum = attend(qkv, stacked)

    counted = [item[1] for item in (*first_in, last_in)]
    if data_count == 4:
        back_sides = [tuple(after(item, stacked) for item in pair) for pair in back_sides]
        w_back = [w_back, *back_sides]
        w_back.append((swap(back_sides[0][0], "dp", 2), swap(back_sides[1][1], "dp", 1)))
    branches = emit(stacked, w_back[:-1], [], 0, data_count)
    branches = emit(stacked, w_back[-1:], counted, data_count - 1, data_count, branches)
    w_back = [jnp.concatenate(pair, axis=0) for pair in w_back]
    branches, *w_back = lax.optimization_barrier((scatter_seq(branches), *w_back))
    grad_output, grad_low, sums = grade(branches, base, valid, float(length * data_count))
    squares, count = sums[0, 0], sums[1, 0]
    grad_all = gather_seq(grad_low)
    branch_bias_grad = jnp.sum(grad_all.astype(wide), axis=0)

    def owned(left, right):
        return dot(left, right, ((0,), (0,)))

    def gather(array):
        return lax.all_gather(array, "seq", axis=0, tiled=False)

    cut = units // 2 // LANES * LANES

    def of_stacked(first, last):
        return [owned(stacked[:, first:last], piece(grad_all, k)) for k in range(data_count)]

    def prepare(pieces):
        return pieces[0], [item.astype(low) for item in pieces[1:]]

    def send(sent, *meanwhile):
        got = [swap(item, "dp", k + 1) for k, item in enumerate(sent)]
        held = lax.optimization_barrier((*got, *jax.tree.leaves(meanwhile)))
        return held[: len(got)], jax.tree.unflatten(jax.tree.structure(meanwhile), held[len(got) :])

    def total(own, got):
        for item in got:
            own = own + item.astype(wide)
        return own.astype(low)

    own_a, sent_a = prepare(of_stacked(head_width + cut, head_width + units))
    own_b, sent_b = outer(stacked, grad_all, data_count, head_width + cut, depth)
    got, ((own_b, sent_b),) = send(sent_a, (own_b, sent_b))
    down_a = total(own_a, got)
    all_a = gather(down_a)
    head_grad, in_low = reject(after(grad_all, down_a), w_back, hidden, head_width)
    own_up, sent_up = outer(normed_all, in_low[:, three:], data_count, depth, units)
    got, (head_grad, in_low, (own_up, sent_up)) = send(
        sent_b, head_grad, in_low, (own_up, sent_up)
    )
    down_b = total(own_b, got)
    all_b = gather(down_b)
    head_grad = after(head_grad, down_b)
    in_low = attend_back(qkv, head_grad, logsum, cosine, sine, in_low)
    own_qkv, sent_qkv = outer(normed_all, after(in_low, *sent_up), data_count, depth, three)
    kept, sent = answer(in_low, flat_in, part, seq_count // 2, tall)
    got, ((own_qkv, sent_qkv), kept, all_a) = send(sent_up, (own_qkv, sent_qkv), kept, all_a)
    up_grad = total(own_up, got)
    all_up = gather(up_grad)
    summed = scatter_blocks(kept, sent)
    got, (summed, all_b) = send(sent_qkv, summed, all_b)
    qkv_grad = total(own_qkv, got)
    token_grad, gain_grad, shift_grad, branch_bias_grad = leave(
        tokens[0],
        norm_gain,
        summed,
        grad_output,
        branch_bias_grad,
        owner,
        data_count,
    )

    in_bias = jnp.sum(in_low.astype(wide), axis=0)
    small = jnp.concatenate(
        [in_bias, gain_grad[0], shift_grad[0], squares[None], branch_bias_grad[0]]
    )
    small = total_dp(small[None])[0]
    branch_bias_grad = small[-width:]
    small = small[:-width]
    lines = -(-small.size // three)
    lines += -lines % 8
    high = jnp.pad(small, (0, lines * three - small.size)).reshape(lines, three)
    first = lax.reduce_precision(high, 8, 7)
    beside = jnp.concatenate([qkv_grad, first.astype(low), (high - first).astype(low)])

    down_weight_grad, out_weight_grad = widen_rows(all_a, all_b, head_width, width)
    all_qkv = gather(after(beside, all_up))
    up_weight_grad = widen_columns(all_up, depth, 1)
    all_qkv = after(all_qkv, down_weight_grad, up_weight_grad)
    qkv_weight_grad = widen_columns(all_qkv, depth, 3)
    slots = all_qkv[:, depth:].astype(wide)
    slots = (slots[:, :lines] + slots[:, lines:]).reshape(seq_count, -1)
    norm_grads = jnp.sum(slots[:, inside : inside + 2 * width + 1], axis=0)
    qkv_bias_grad = slots[:, :three].reshape(seq_count, 3, head_width).transpose(1, 0, 2)
    up_bias_grad = slots[:, three:inside].reshape(-1)
    loss = norm_grads[-1] / (2.0 * width * count)
    return (
        loss,
        token_grad[None],
        norm_grads[:width],
        norm_grads[width : 2 * width],
        qkv_weight_grad,
        qkv_bias_grad.reshape(-1),
        out_weight_grad,
        branch_bias_grad,
        up_weight_grad,
        up_bias_grad,
        down_weight_grad,
        branch_bias_grad,
    )


def solution(mesh):
    placed = (
        P("dp", "seq", None),
        P("dp", "seq", None),
        P("dp", "seq"),
        P("dp", "seq"),
        P(),
        P(),
        P("dp", None),
        P(),
        P(None, "dp"),
        P(),
        P("dp", None),
        P(),
        P(None, "dp"),
        P(),
    )
    return jax.shard_map(
        local,
        mesh=mesh,
        in_specs=placed,
        out_specs=(
            P(),
            P("dp", "seq", None),
            P(),
            P(),
            P("dp", None),
            P(),
            P(None, "dp"),
            P(),
            P("dp", None),
            P(),
            P(None, "dp"),
            P(),
        ),
        check_vma=False,
    )
```

```python
import functools

import jax
import jax.numpy as jnp
from jax import lax
from jax.experimental import pallas as pl
from jax.experimental.pallas import tpu as pltpu
from jax.sharding import PartitionSpec as P

HEADS = 32
HEAD_DIM = 64
ROTARY = 32


norm_eps = 1e-05
rope_base = 10000.0
masked_fill = -1e30
LANES = 128
RADIX = 64
DIGIT = 16
SPARE = 16
ROWS = 64

low = jnp.bfloat16
wide = jnp.float32


def dot(a, b, dims):
    return lax.dot_general(a, b, (dims, ((), ())), preferred_element_type=wide)


def after(array, *earlier):
    return lax.optimization_barrier((array, *earlier))[0]


def swap(array, axis, bit):
    return lax.ppermute(array, axis, [(s, s ^ bit) for s in range(lax.axis_size(axis))])


def gather_seq(rows):
    return lax.all_gather(rows, "seq", axis=0, tiled=True)


def between(array, pairs):
    return lax.ppermute(
        array, "seq", [(2 * a + core, 2 * b + core) for a, b in pairs for core in range(2)]
    )


def scatter_chips(blocks):
    chips = len(blocks)
    if chips != 4:
        total = blocks[0]
        for k in range(1, chips):
            total = total + swap(blocks[k].astype(low), "seq", 2 * k).astype(wide)
        return total
    chip = lax.axis_index("seq") // 2
    far = between(blocks[3].astype(low), [(0, 1), (3, 2)])
    passed = (blocks[2] + far.astype(wide)).astype(low)
    upward = between(passed, [(0, 1), (1, 2)])
    downward = between(passed, [(3, 2), (2, 1)])
    upward = jnp.where(chip == 1, blocks[3], blocks[1]) + upward.astype(wide)
    downward = jnp.where(chip == 2, blocks[3], blocks[1]) + downward.astype(wide)
    upward = between(upward.astype(low), [(0, 1), (1, 2), (2, 3)])
    downward = between(downward.astype(low), [(3, 2), (2, 1), (1, 0)])
    return blocks[0] + upward.astype(wide) + downward.astype(wide)


def scatter_blocks(kept, sent):
    chips = lax.axis_size("seq") // 2
    rows = kept.shape[0] // chips
    chip = kept + swap(sent, "seq", 1).astype(wide)
    return scatter_chips([chip[k * rows : (k + 1) * rows] for k in range(chips)])


def scatter_seq(partial):
    return lax.psum_scatter(partial, "seq", scatter_dimension=0, tiled=True)


def total_dp(array):
    items = [array] + [swap(array, "dp", k) for k in range(1, lax.axis_size("dp"))]
    while len(items) > 1:
        items = [a + b for a, b in zip(items[::2], items[1::2])]
    return items[0]


def normalise(values):
    centre = values - jnp.mean(values, axis=-1, keepdims=True)
    spread = jnp.mean(centre * centre, axis=-1, keepdims=True)
    rstd = lax.rsqrt(spread + norm_eps)
    return centre * rstd, rstd


def enter_kernel(
    owners, owner, tokens, teacher, gain, shift, bias_a, bias_b, place, normed, base, held, kept
):
    inputs = tokens[...].astype(wide)
    xhat, _ = normalise(inputs)
    held[...] = xhat * gain[...].astype(wide)[None] + shift[...].astype(wide)[None]
    biases = (bias_a[...].astype(wide) + bias_b[...].astype(wide))[None]
    kept[...] = inputs + biases - teacher[...].astype(wide)
    width = inputs.shape[1]
    depth = width // owners
    for k in range(owners):
        theirs = pl.ds(pl.multiple_of((owner[0] ^ k) * depth, LANES), depth)
        normed[:, k * depth : (k + 1) * depth] = held[:, theirs].astype(low)
        base[:, k * depth : (k + 1) * depth] = kept[:, theirs]
    lane = lax.broadcasted_iota(jnp.int32, (inputs.shape[0], LANES), 1)
    ids = column_of(place[...]).astype(jnp.int32)
    facts = jnp.where(lane == 0, ids // RADIX, ids % RADIX)
    normed[:, width:] = facts.astype(wide).astype(low)


def enter(tokens, teacher, gain, shift, bias_a, bias_b, place, owner, owners):
    rows, width = tokens.shape
    whole = pl.BlockSpec(memory_space=pltpu.VMEM)
    return pl.pallas_call(
        functools.partial(enter_kernel, owners),
        in_specs=[pl.BlockSpec(memory_space=pltpu.SMEM)] + [whole] * 7,
        out_specs=[whole] * 2,
        out_shape=[
            jax.ShapeDtypeStruct((rows, width + LANES), low),
            jax.ShapeDtypeStruct((rows, width), wide),
        ],
        scratch_shapes=[pltpu.VMEM((rows, width), wide)] * 2,
        name="enter",
    )(
        owner[None],
        tokens,
        teacher,
        gain,
        shift,
        bias_a,
        bias_b,
        place,
    )


def column_of(row):
    size = row.shape[1]
    here = lax.broadcasted_iota(jnp.int32, (size, size), 0)
    there = lax.broadcasted_iota(jnp.int32, (size, size), 1)
    return jnp.sum(jnp.where(here == there, row.astype(wide), 0.0), axis=1, keepdims=True)


def grade_kernel(scale, branches, base, valid, grad, grad_low, sums):
    width = base.shape[1]
    lane = lax.broadcasted_iota(jnp.int32, (1, LANES), 1)
    weight = jnp.where(lane == 1, float(DIGIT), jnp.where(lane == 2, float(DIGIT * DIGIT), 1.0))
    digits = jnp.where(lane < 3, branches[:1, width:].astype(wide) * weight, 0.0)
    count = jnp.sum(digits, axis=1, keepdims=True)
    error = base[...] + branches[:, :width].astype(wide)
    weighted = column_of(valid[...]) * error
    squares = jnp.sum(jnp.sum(weighted * error, axis=0, keepdims=True), axis=1, keepdims=True)
    result = scale / count * weighted
    grad[...] = result
    grad_low[...] = result.astype(low)
    line = lax.broadcasted_iota(jnp.int32, sums.shape, 0)
    sums[...] = jnp.where(line == 0, squares, count)


def grade(branches, base, valid, scale):
    whole = pl.BlockSpec(memory_space=pltpu.VMEM)
    return pl.pallas_call(
        functools.partial(grade_kernel, scale),
        in_specs=[whole] * 3,
        out_specs=[whole] * 3,
        out_shape=[
            jax.ShapeDtypeStruct(base.shape, wide),
            jax.ShapeDtypeStruct(base.shape, low),
            jax.ShapeDtypeStruct((8, LANES), wide),
        ],
        cost_estimate=pl.CostEstimate(
            flops=4 * base.size, bytes_accessed=12 * base.size, transcendentals=0
        ),
        name="grade",
    )(branches, base, valid)


def leave_kernel(
    owners, owner, tokens, gain, summed, grad, bias, token_grad, gain_grad, shift_grad, bias_grad
):
    inputs = tokens[...].astype(wide)
    xhat, rstd = normalise(inputs)
    depth = inputs.shape[1] // owners
    for k in range(owners):
        theirs = pl.ds(pl.multiple_of((owner[0] ^ k) * depth, LANES), depth)
        token_grad[:, theirs] = summed[:, k * depth : (k + 1) * depth]
        bias_grad[:, theirs] = bias[:, k * depth : (k + 1) * depth]
    normed_grad = token_grad[...]
    gain_grad[...] = jnp.sum(normed_grad * xhat, axis=0, keepdims=True)
    shift_grad[...] = jnp.sum(normed_grad, axis=0, keepdims=True)
    scaled = normed_grad * gain[...].astype(wide)[None]
    token_grad[...] = rstd * (
        scaled
        - jnp.mean(scaled, axis=-1, keepdims=True)
        - xhat * jnp.mean(scaled * xhat, axis=-1, keepdims=True)
    )
    for k in range(owners):
        theirs = pl.ds(pl.multiple_of((owner[0] ^ k) * depth, LANES), depth)
        token_grad[:, theirs] += grad[:, k * depth : (k + 1) * depth]


def leave(tokens, gain, summed, grad, bias, owner, owners):
    rows, width = tokens.shape
    whole = pl.BlockSpec(memory_space=pltpu.VMEM)
    line = jax.ShapeDtypeStruct((1, width), wide)
    return pl.pallas_call(
        functools.partial(leave_kernel, owners),
        in_specs=[pl.BlockSpec(memory_space=pltpu.SMEM)] + [whole] * 5,
        out_specs=[whole] * 4,
        out_shape=[jax.ShapeDtypeStruct((rows, width), wide), line, line, line],
        name="leave",
    )(owner[None], tokens, gain, summed, grad, bias[None])


def pick_kernel(moves, part, counted, a, b, *refs):
    outs, arrived = refs[:2], refs[2]
    copies = []
    for which, source, half, target in moves:
        copies.append(
            pltpu.make_async_copy(
                (a, b)[which].at[source(part[0])],
                outs[half].at[target],
                arrived.at[len(copies)],
            )
        )
    for copy in copies:
        copy.start()
    tall = outs[0].shape[0]
    more = outs[1].shape[0] - tall
    if more:
        count = jnp.sum(counted[...].astype(wide), axis=1, keepdims=True)
        outs[1][tall:, :] = jnp.broadcast_to(count, (more, outs[1].shape[1])).astype(low)
    for copy in copies:
        copy.wait()


def pick(arrays, part, counted, moves, shapes):
    moved = 4 * sum(shape[0] * shape[1] for shape in shapes)
    return pl.pallas_call(
        functools.partial(pick_kernel, moves),
        in_specs=[
            pl.BlockSpec(memory_space=pltpu.SMEM),
            pl.BlockSpec(memory_space=pltpu.VMEM),
        ]
        + [pl.BlockSpec(memory_space=pl.ANY)] * 2,
        out_specs=[pl.BlockSpec(memory_space=pltpu.VMEM)] * 2,
        out_shape=[jax.ShapeDtypeStruct(shape, low) for shape in shapes],
        scratch_shapes=[pltpu.SemaphoreType.DMA((len(moves),))],
        cost_estimate=pl.CostEstimate(flops=0, bytes_accessed=moved, transcendentals=0),
        name="pick",
    )(part, counted, *arrays)


def gelu_parts(values):
    root = (2.0 / jnp.pi) ** 0.5
    square = values * values
    bent = jnp.tanh(root * (values + 0.044715 * (values * square)))
    factor = 0.5 * (1.0 + bent)
    slope = 0.5 * values * (1.0 - bent * bent) * (root * (1.0 + 3.0 * 0.044715 * square))
    return factor, factor + slope


def turn(values, cosine, sine):
    lane = lax.broadcasted_iota(jnp.int32, values.shape, 1) % HEAD_DIM
    half, width = ROTARY // 2, values.shape[1]
    partner = jnp.where(
        lane < half, pltpu.roll(values, width - half, 1), pltpu.roll(values, half, 1)
    )
    return values * cosine + partner * sine


def project_kernel(count, normed, cosine, sine, bias, *refs):
    weights, (qkv, hidden, stacked) = refs[:count], refs[count:]
    tile = pl.program_id(0)
    tall = normed.shape[1] // count
    total = bias[...]
    for k in range(count):
        block = normed[:, k * tall : (k + 1) * tall]
        total = total + jnp.dot(block, weights[k][...], preferred_element_type=wide)
    repeats = total.shape[1] // LANES

    @pl.when(tile < 2)
    def _():
        turned = turn(
            total,
            jnp.concatenate([cosine[...]] * repeats, axis=1),
            jnp.concatenate([sine[...]] * repeats, axis=1),
        )
        qkv[...] = turned.astype(low)

    @pl.when(tile == 2)
    def _():
        qkv[...] = total.astype(low)

    @pl.when(tile > 2)
    def _():
        hidden[...] = total
        stacked[...] = (total * gelu_parts(total)[0]).astype(low)


def project(normed, cosine, sine, bias, weights, tall, head_width):
    count = len(weights)
    length = normed.shape[0]
    inside = weights[0].shape[1]
    units = inside - 3 * head_width
    table = pl.BlockSpec((length, LANES), lambda t: (0, 0))
    return pl.pallas_call(
        functools.partial(project_kernel, count),
        grid=(inside // head_width,),
        in_specs=[
            pl.BlockSpec((length, count * tall), lambda t: (0, 0)),
            table,
            table,
            pl.BlockSpec((1, head_width), lambda t: (0, t)),
        ]
        + [pl.BlockSpec((tall, head_width), lambda t: (0, t))] * count,
        out_specs=[
            pl.BlockSpec((length, head_width), lambda t: (0, jnp.minimum(t, 2))),
            pl.BlockSpec((length, head_width), lambda t: (0, jnp.maximum(t - 3, 0))),
            pl.BlockSpec((length, head_width), lambda t: (0, jnp.maximum(t - 2, 1))),
        ],
        out_shape=[
            jax.ShapeDtypeStruct((length, 3 * head_width), low),
            jax.ShapeDtypeStruct((length, units), wide),
            jax.ShapeDtypeStruct((length, head_width + units), low),
        ],
        cost_estimate=pl.CostEstimate(
            flops=2 * length * count * tall * inside,
            bytes_accessed=2 * count * tall * (inside + length) + 8 * length * inside,
            transcendentals=length * units,
        ),
        name="project",
    )(normed, cosine, sine, bias, *weights)


def emit_kernel(owners, counts, stacked, *refs):
    counted, refs = refs[:counts], refs[counts:]
    weights, (out, slots, arrived) = refs[: 2 * owners], refs[-3:]
    middle, size = slots.shape[2:]
    step = pl.program_id(0)

    def fetch(n):
        columns = pl.ds(n % 2 * size, size)
        return [
            pltpu.make_async_copy(
                weights[n // 2 * 2 + half].at[:, columns],
                slots.at[n % 2, half],
                arrived.at[n % 2, half],
            )
            for half in range(2)
        ]

    @pl.when(step == 0)
    def _():
        for copy in fetch(0):
            copy.start()

    for n in range(2 * owners):

        @pl.when(step == n)
        def _(n=n):
            if n + 1 < 2 * owners:
                for copy in fetch(n + 1):
                    copy.start()
            for copy in fetch(n):
                copy.wait()

    @pl.when(step < 2 * owners)
    def _():
        slot = lax.rem(step, 2)
        total = jnp.dot(stacked[:, :middle], slots[slot, 0], preferred_element_type=wide)
        total = total + jnp.dot(stacked[:, middle:], slots[slot, 1], preferred_element_type=wide)
        out[...] = total.astype(low)

    if not counted:
        return

    @pl.when(step == 2 * owners)
    def _():
        count = counted[0][...].astype(wide)
        for ref in counted[1:]:
            count = count + ref[...].astype(wide)
        count = count[:1].astype(jnp.int32)
        lane = lax.broadcasted_iota(jnp.int32, count.shape, 1)
        digits = jnp.where(lane == 0, count, count // DIGIT)
        digits = jnp.where(lane == 2, count // (DIGIT * DIGIT), digits) % DIGIT
        out[:, :LANES] = jnp.broadcast_to(digits.astype(wide), (out.shape[0], LANES)).astype(low)


def emit(stacked, weights, counted, first, all_owners, into=None):
    owners = len(weights)
    length, behind = stacked.shape
    middle, depth = weights[0][0].shape
    size = depth // 2
    steps = 2 * owners + (first + owners == all_owners)

    row = size // SPARE
    operands = [stacked, *counted, *[item for pair in weights for item in pair]]
    in_specs = [pl.BlockSpec((length, behind), lambda t: (0, 0))]
    in_specs += [pl.BlockSpec((SPARE, LANES), lambda t: (row, 0))] * len(counted)
    in_specs += [pl.BlockSpec(memory_space=pl.ANY)] * (2 * owners)
    aliases = {}
    if into is not None:
        aliases = {len(operands): 0}
        operands.append(into)
        in_specs.append(pl.BlockSpec(memory_space=pl.ANY))
    return pl.pallas_call(
        functools.partial(emit_kernel, owners, len(counted)),
        grid=(steps,),
        in_specs=in_specs,
        out_specs=pl.BlockSpec((length, size), lambda t: (0, 2 * first + t)),
        out_shape=jax.ShapeDtypeStruct((length, all_owners * depth + LANES), low),
        input_output_aliases=aliases,
        scratch_shapes=[
            pltpu.VMEM((2, 2, middle, size), low),
            pltpu.SemaphoreType.DMA((2, 2)),
        ],
        cost_estimate=pl.CostEstimate(
            flops=2 * length * behind * owners * depth,
            bytes_accessed=2 * behind * (length + owners * depth) + 2 * length * steps * size,
            transcendentals=0,
        ),
        name="emit",
    )(*operands)


def scores_of(rows, keys, start):
    raw = lax.dot_general(rows, keys, (((1,), (1,)), ((), ())), preferred_element_type=wide)
    place = start + lax.broadcasted_iota(jnp.int32, raw.shape, 0)
    kept = lax.broadcasted_iota(jnp.int32, raw.shape, 1) <= place
    return jnp.where(kept, raw * HEAD_DIM ** (-0.5), masked_fill)


def by_blocks(length, head_width, step, body):
    pairs = head_width // LANES
    blocks = length // 2 // step
    for half in range(2):

        def one(n, carry, half=half):
            row = pl.multiple_of(half * (length // 2) + lax.rem(n, blocks) * step, step)
            body(row, pl.multiple_of(lax.div(n, blocks) * LANES, LANES), (half + 1) * length // 2)
            return carry

        lax.fori_loop(0, pairs * blocks, one, 0)


def attend_kernel(step, qkv, stacked, out, logsum):
    del stacked
    length, head_width = out.shape
    lane = lax.broadcasted_iota(jnp.int32, (step, LANES), 1)

    def body(row, at, last):
        rows = pl.ds(row, step)
        queries = qkv[rows, pl.ds(at, LANES)]
        keys = qkv[:last, pl.ds(head_width + at, LANES)]
        values = qkv[:last, pl.ds(2 * head_width + at, LANES)]
        sums = logsum[rows, :]
        outs = []
        for n, h in enumerate((slice(0, HEAD_DIM), slice(HEAD_DIM, LANES))):
            scores = scores_of(queries[:, h], keys[:, h], row)
            top = jnp.max(scores, axis=-1, keepdims=True)
            expd = jnp.exp(scores - top)
            total = jnp.sum(expd, axis=-1, keepdims=True)
            probs = (expd * (1.0 / total)).astype(low)
            outs.append(jnp.dot(probs, values[:, h], preferred_element_type=wide))
            sums = jnp.where(lane == at // HEAD_DIM + n, top + jnp.log(total), sums)
        out[rows, pl.ds(at, LANES)] = jnp.concatenate(outs, axis=1).astype(low)
        logsum[rows, :] = sums

    logsum[...] = jnp.zeros(logsum.shape, wide)
    by_blocks(length, head_width, step, body)


def attend(qkv, stacked):
    length, three = qkv.shape
    head_width = three // 3
    heads = head_width // HEAD_DIM
    whole = pl.BlockSpec(memory_space=pltpu.VMEM)
    return pl.pallas_call(
        functools.partial(attend_kernel, 256),
        grid=(1,),
        in_specs=[whole, pl.BlockSpec(memory_space=pl.ANY)],
        out_specs=[pl.BlockSpec((length, head_width), lambda n: (0, 0)), whole],
        out_shape=[
            jax.ShapeDtypeStruct(stacked.shape, low),
            jax.ShapeDtypeStruct((length, LANES), wide),
        ],
        input_output_aliases={1: 0},
        cost_estimate=pl.CostEstimate(
            flops=4 * heads * length * length * LANES,
            bytes_accessed=8 * length * three,
            transcendentals=heads * length * length,
        ),
        name="attend",
    )(qkv, stacked)


def attend_back_kernel(step, qkv, grad, logsum, cosine, sine, entered, out, gone):
    del entered
    length, head_width = grad.shape
    scale = HEAD_DIM ** (-0.5)
    over_rows = (((0,), (0,)), ((), ()))
    lane = lax.broadcasted_iota(jnp.int32, (step, LANES), 1)

    def body(row, at, last):
        rows = pl.ds(row, step)
        spots = [pl.ds(t * head_width + at, LANES) for t in range(3)]
        queries, keys, values = qkv[rows, spots[0]], qkv[:last, spots[1]], qkv[:last, spots[2]]
        upstreams = grad[rows, spots[0]]
        parts = [[], [], []]
        for n, h in enumerate((slice(0, HEAD_DIM), slice(HEAD_DIM, LANES))):
            sums = jnp.where(lane == at // HEAD_DIM + n, logsum[rows, :], 0.0)
            sums = jnp.sum(sums, axis=1, keepdims=True)
            probs = jnp.exp(scores_of(queries[:, h], keys[:, h], row) - sums)
            prob_grad = lax.dot_general(
                upstreams[:, h],
                values[:, h],
                (((1,), (1,)), ((), ())),
                preferred_element_type=wide,
            )
            inner = jnp.sum(probs * prob_grad, axis=-1, keepdims=True)
            score_grad = (probs * (prob_grad - inner)).astype(low)
            parts[0].append(jnp.dot(score_grad, keys[:, h], preferred_element_type=wide))
            parts[1].append(
                lax.dot_general(score_grad, queries[:, h], over_rows, preferred_element_type=wide)
            )
            parts[2].append(
                lax.dot_general(
                    probs.astype(low), upstreams[:, h], over_rows, preferred_element_type=wide
                )
            )
        parts = [jnp.concatenate(part, axis=1) for part in parts]
        gone[rows, spots[0]] = parts[0] * scale
        gone[:last, spots[1]] += parts[1] * scale
        gone[:last, spots[2]] += parts[2]

    gone[:, head_width:] = jnp.zeros((length, 2 * head_width), wide)
    by_blocks(length, head_width, step, body)

    def turn_back(n, carry):
        rows = pl.ds(pl.multiple_of(lax.rem(n, length // step) * step, step), step)
        at = pl.multiple_of(lax.div(n, length // step) * LANES, LANES)
        value = gone[rows, pl.ds(at, LANES)].astype(low).astype(wide)
        out[rows, pl.ds(at, LANES)] = turn(value, cosine[rows, :], -sine[rows, :]).astype(low)
        return carry

    lax.fori_loop(0, length // step * (2 * head_width // LANES), turn_back, 0)
    out[:, 2 * head_width :] = gone[:, 2 * head_width :].astype(low)


def attend_back(qkv, grad, logsum, cosine, sine, entered):
    length, three = qkv.shape
    head_width = three // 3
    heads = head_width // HEAD_DIM
    whole = pl.BlockSpec(memory_space=pltpu.VMEM)
    return pl.pallas_call(
        functools.partial(attend_back_kernel, 128),
        grid=(1,),
        in_specs=[whole] * 5 + [pl.BlockSpec(memory_space=pl.ANY)],
        out_specs=pl.BlockSpec((length, three), lambda n: (0, 0)),
        out_shape=jax.ShapeDtypeStruct(entered.shape, low),
        scratch_shapes=[
            pltpu.VMEM((length, three), wide),
        ],
        input_output_aliases={5: 0},
        cost_estimate=pl.CostEstimate(
            flops=10 * heads * length * length * LANES,
            bytes_accessed=8 * length * three,
            transcendentals=heads * length * length,
        ),
        name="attend_back",
    )(qkv, grad, logsum, cosine, sine, entered)


def reject_kernel(count, hidden, grads, *refs):
    weights, (head_grad, entered) = refs[:count], refs[count:]
    depth = weights[0].shape[1]
    over = (((1,), (1,)), ((), ()))
    total = lax.dot_general(grads[:, :depth], weights[0][...], over, preferred_element_type=wide)
    for k in range(1, count):
        total = total + lax.dot_general(
            grads[:, k * depth : (k + 1) * depth],
            weights[k][...],
            over,
            preferred_element_type=wide,
        )

    @pl.when(pl.program_id(0) == 0)
    def _():
        head_grad[...] = total.astype(low)

    @pl.when(pl.program_id(0) > 0)
    def _():
        entered[...] = (total * gelu_parts(hidden[...])[1]).astype(low)


def reject(grads, weights, hidden, head_width):
    count = len(weights)
    length = grads.shape[0]
    behind, depth = weights[0].shape
    inside = behind + 2 * head_width
    return pl.pallas_call(
        functools.partial(reject_kernel, count),
        grid=(behind // head_width,),
        in_specs=[pl.BlockSpec((length, head_width), lambda t: (0, jnp.maximum(t - 1, 0)))]
        + [pl.BlockSpec((length, count * depth), lambda t: (0, 0))]
        + [pl.BlockSpec((head_width, depth), lambda t: (t, 0))] * count,
        out_specs=[
            pl.BlockSpec((length, head_width), lambda t: (0, 0)),
            pl.BlockSpec((length, head_width), lambda t: (0, jnp.maximum(t + 2, 3))),
        ],
        out_shape=[
            jax.ShapeDtypeStruct((length, head_width), low),
            jax.ShapeDtypeStruct((length, inside), low),
        ],
        cost_estimate=pl.CostEstimate(
            flops=2 * length * count * depth * behind,
            bytes_accessed=2 * count * depth * (behind + length) + 8 * length * behind,
            transcendentals=length * behind,
        ),
        name="reject",
    )(hidden, grads, *weights)


def sort_blocks(held, part, chips, kept, sent):
    rows = kept.shape[0] // chips
    for k in range(chips):
        here = slice(k * rows, (k + 1) * rows)
        for core, out in enumerate((kept, sent)):
            block = part ^ (2 * k + core)
            source = pl.ds(pl.multiple_of(block * rows, rows), rows)
            out[here, :] = held[source, :].astype(out.dtype)


def outer_kernel(left, right, *outs):
    total = lax.dot_general(
        left[...], right[...], (((0,), (0,)), ((), ())), preferred_element_type=wide
    )
    for n, out in enumerate(outs):

        @pl.when(pl.program_id(0) == n)
        def _(out=out):
            out[...] = total.astype(out.dtype)


def outer(left, right, count, left_size, right_size):
    length = left.shape[0]
    left_step = int(left.shape[1] >= count * left_size)
    flops = 2 * length * count * left_size * right_size
    kinds = [wide] + [low] * (count - 1)
    results = pl.pallas_call(
        outer_kernel,
        grid=(count,),
        in_specs=[
            pl.BlockSpec((length, left_size), lambda k: (0, k * left_step)),
            pl.BlockSpec((length, right_size), lambda k: (0, k * (1 - left_step))),
        ],
        out_specs=[pl.BlockSpec((left_size, right_size), lambda k: (0, 0))] * count,
        out_shape=[jax.ShapeDtypeStruct((left_size, right_size), kind) for kind in kinds],
        cost_estimate=pl.CostEstimate(
            flops=flops, bytes_accessed=flops // length, transcendentals=0
        ),
        name="outer",
    )(left, right)
    return results[0], list(results[1:])


def answer_kernel(count, chips, part, entered, *refs):
    weights, (kept, sent, held, slots, arrived) = refs[:count], refs[count:]
    tall = slots.shape[1]
    step = pl.program_id(0)

    def fetch(n):
        return pltpu.make_async_copy(
            weights[n].at[pl.ds(0, tall)], slots.at[n % 2], arrived.at[n % 2]
        )

    @pl.when(step == 0)
    def _():
        fetch(0).start()

    for n in range(count):

        @pl.when(step == n)
        def _(n=n):
            if n + 1 < count:
                fetch(n + 1).start()
            fetch(n).wait()

    held[...] = lax.dot_general(
        entered[...],
        slots[lax.rem(step, 2)],
        (((1,), (1,)), ((), ())),
        preferred_element_type=wide,
    )
    sort_blocks(held, part[0], chips, kept, sent)


def answer(entered, pieces, part, chips, tall):
    count = len(pieces)
    length, inside = entered.shape
    half = length // 2
    return pl.pallas_call(
        functools.partial(answer_kernel, count, chips),
        grid=(count,),
        in_specs=[
            pl.BlockSpec(memory_space=pltpu.SMEM),
            pl.BlockSpec((length, inside), lambda t: (0, 0)),
        ]
        + [pl.BlockSpec(memory_space=pl.ANY)] * count,
        out_specs=[pl.BlockSpec((half, tall), lambda t: (0, t))] * 2,
        out_shape=[
            jax.ShapeDtypeStruct((half, count * tall), wide),
            jax.ShapeDtypeStruct((half, count * tall), low),
        ],
        scratch_shapes=[
            pltpu.VMEM((length, tall), wide),
            pltpu.VMEM((2, tall, inside), low),
            pltpu.SemaphoreType.DMA((2,)),
        ],
        cost_estimate=pl.CostEstimate(
            flops=2 * length * inside * count * tall,
            bytes_accessed=2 * inside * (length + count * tall) + 3 * length * count * tall,
            transcendentals=0,
        ),
        name="answer",
    )(part[None], entered, *pieces)


def widen_rows_kernel(head_width, a, b, down, out):
    cut = b.shape[1] - head_width
    out[...] = b[0, :head_width].astype(wide)
    down[:cut] = b[0, head_width:].astype(wide)
    down[cut:] = a[0].astype(wide)


def widen_rows(all_a, all_b, head_width, width):
    count, rest, depth = all_a.shape
    tall = all_b.shape[1]
    units = rest + tall - head_width
    return pl.pallas_call(
        functools.partial(widen_rows_kernel, head_width),
        grid=(count,),
        in_specs=[
            pl.BlockSpec((1, rest, depth), lambda j: (j, 0, 0)),
            pl.BlockSpec((1, tall, depth), lambda j: (j, 0, 0)),
        ],
        out_specs=[
            pl.BlockSpec((units, depth), lambda j: (j, 0)),
            pl.BlockSpec((head_width, depth), lambda j: (j, 0)),
        ],
        out_shape=[
            jax.ShapeDtypeStruct((count * units, depth), wide),
            jax.ShapeDtypeStruct((width, depth), wide),
        ],
        cost_estimate=pl.CostEstimate(
            flops=0, bytes_accessed=6 * count * depth * (rest + tall), transcendentals=0
        ),
        name="widen_rows",
    )(all_a, all_b)


def widen_columns_kernel(groups, gathered, out):
    count, _, columns = gathered.shape
    size = columns // groups
    for j in range(count):
        for g in range(groups):
            at = (g * count + j) * size
            out[:, at : at + size] = gathered[j, :, g * size : (g + 1) * size].astype(wide)


def widen_columns(gathered, rows, groups):
    count, _, columns = gathered.shape
    tall = min(128, rows)
    moved = 6 * count * rows * columns
    return pl.pallas_call(
        functools.partial(widen_columns_kernel, groups),
        grid=(rows // tall,),
        in_specs=[pl.BlockSpec((count, tall, columns), lambda r: (0, r, 0))],
        out_specs=pl.BlockSpec((tall, count * columns), lambda r: (r, 0)),
        out_shape=jax.ShapeDtypeStruct((rows, count * columns), wide),
        cost_estimate=pl.CostEstimate(flops=0, bytes_accessed=moved, transcendentals=0),
        name="widen_columns",
    )(gathered)


def local(
    tokens,
    teacher,
    valid,
    positions,
    norm_gain,
    norm_bias,
    qkv_weight,
    qkv_bias,
    out_weight,
    out_bias,
    up_weight,
    up_bias,
    down_weight,
    down_bias,
):
    rows_here, width = tokens.shape[1:]
    seq_count = lax.axis_size("seq")
    data_count = lax.axis_size("dp")
    part = lax.axis_index("seq")
    owner = lax.axis_index("dp")
    length = rows_here * seq_count
    head_width = HEADS // seq_count * HEAD_DIM
    three = 3 * head_width
    units = up_weight.shape[1] // seq_count
    inside = three + units
    depth = qkv_weight.shape[0]

    tall = depth // 2
    behind = head_width + units

    def span(start, size, unit):
        return pl.ds(start if isinstance(start, int) else pl.multiple_of(start, unit), size)

    def block_at(row, rows, column, columns):
        return span(row, rows, ROWS), span(column, columns, LANES)

    moves = []
    for half in range(2):
        for t in range(3):
            moves.append(
                (
                    0,
                    lambda part, t=t, half=half: block_at(
                        half * tall, tall, t * width + part * head_width, head_width
                    ),
                    half,
                    block_at(0, tall, t * head_width, head_width),
                )
            )
        moves.append(
            (
                1,
                lambda part, half=half: block_at(half * tall, tall, part * units, units),
                half,
                block_at(0, tall, three, units),
            )
        )
    w_in = pick(
        (qkv_weight, up_weight),
        part[None],
        valid,
        moves,
        [(tall, inside), (tall + SPARE, inside)],
    )
    normed_low, base = enter(
        tokens[0],
        teacher[0],
        norm_gain,
        norm_bias,
        out_bias,
        down_bias,
        positions,
        after(owner, *w_in),
        data_count,
    )

    rest = behind // 2 - head_width
    moves = [
        (
            0,
            lambda part: block_at(part * head_width, head_width, 0, depth),
            0,
            block_at(0, head_width, 0, depth),
        ),
        (
            1,
            lambda part: block_at(part * units, rest, 0, depth),
            0,
            block_at(head_width, rest, 0, depth),
        ),
        (
            1,
            lambda part: block_at(part * units + rest, units - rest, 0, depth),
            1,
            block_at(0, units - rest, 0, depth),
        ),
    ]
    w_back = pick(
        (out_weight, down_weight),
        after(part[None], normed_low),
        valid,
        moves,
        [(behind // 2, depth)] * 2,
    )
    if data_count == 4:
        sides = [tuple(swap(item, "dp", k) for item in w_in) for k in (1, 2)]
        last_in = swap(sides[0][0], "dp", 2), swap(sides[1][1], "dp", 1)
        first_in = [w_in, *sides]
        w_back = lax.optimization_barrier((*w_back, *last_in))[:2]
        back_sides = [tuple(swap(item, "dp", k) for item in w_back) for k in (1, 2)]
    else:
        w_in = [w_in] + [tuple(swap(item, "dp", k) for item in w_in) for k in range(1, data_count)]
        w_back = [w_back] + [
            tuple(swap(item, "dp", k) for item in w_back) for k in range(1, data_count)
        ]
        first_in, last_in = w_in[:-1], w_in[-1]
    normed_all = gather_seq(normed_low)
    facts = normed_all[:, width : width + 2].astype(jnp.int32)
    where = facts[:, 0] * RADIX + facts[:, 1]

    half = ROTARY // 2
    lane = jnp.arange(LANES, dtype=jnp.int32) % HEAD_DIM
    freqs = rope_base ** (-((lane % half).astype(wide) * 2.0) / ROTARY)
    angles = where.astype(wide)[:, None] * jnp.where(lane < ROTARY, freqs, 0.0)[None, :]
    cosine = jnp.cos(angles)
    sine = jnp.sin(angles) * jnp.where(lane < half, -1.0, 1.0)[None, :]

    b_in = jnp.concatenate(
        [
            lax.dynamic_slice_in_dim(qkv_bias, t * width + part * head_width, head_width, 0)
            for t in range(3)
        ]
        + [lax.dynamic_slice_in_dim(up_bias, part * units, units, 0)]
    ).astype(wide)[None]

    def piece(array, k):
        return array[:, k * depth : (k + 1) * depth]

    flat_in = [item for pair in (*first_in, last_in) for item in pair]
    qkv, hidden, stacked = project(normed_all, cosine, sine, b_in, flat_in, tall, head_width)
    stacked, logsum = attend(qkv, stacked)

    counted = [item[1] for item in (*first_in, last_in)]
    if data_count == 4:
        back_sides = [tuple(after(item, stacked) for item in pair) for pair in back_sides]
        w_back = [w_back, *back_sides]
        w_back.append((swap(back_sides[0][0], "dp", 2), swap(back_sides[1][1], "dp", 1)))
    branches = emit(stacked, w_back[:-1], [], 0, data_count)
    branches = emit(stacked, w_back[-1:], counted, data_count - 1, data_count, branches)
    w_back = [jnp.concatenate(pair, axis=0) for pair in w_back]
    branches, *w_back = lax.optimization_barrier((scatter_seq(branches), *w_back))
    grad_output, grad_low, sums = grade(branches, base, valid, float(length * data_count))
    squares, count = sums[0, 0], sums[1, 0]
    grad_all = gather_seq(grad_low)
    branch_bias_grad = jnp.sum(grad_all.astype(wide), axis=0)

    def owned(left, right):
        return dot(left, right, ((0,), (0,)))

    def gather(array):
        return lax.all_gather(array, "seq", axis=0, tiled=False)

    cut = units // 2 // LANES * LANES

    def of_stacked(first, last):
        return [owned(stacked[:, first:last], piece(grad_all, k)) for k in range(data_count)]

    def prepare(pieces):
        return pieces[0], [item.astype(low) for item in pieces[1:]]

    def send(sent, *meanwhile):
        got = [swap(item, "dp", k + 1) for k, item in enumerate(sent)]
        held = lax.optimization_barrier((*got, *jax.tree.leaves(meanwhile)))
        return held[: len(got)], jax.tree.unflatten(jax.tree.structure(meanwhile), held[len(got) :])

    def total(own, got):
        for item in got:
            own = own + item.astype(wide)
        return own.astype(low)

    own_a, sent_a = prepare(of_stacked(head_width + cut, head_width + units))
    own_b, sent_b = outer(stacked, grad_all, data_count, head_width + cut, depth)
    got, ((own_b, sent_b),) = send(sent_a, (own_b, sent_b))
    down_a = total(own_a, got)
    all_a = gather(down_a)
    head_grad, in_low = reject(after(grad_all, down_a), w_back, hidden, head_width)
    own_up, sent_up = outer(normed_all, in_low[:, three:], data_count, depth, units)
    got, (head_grad, in_low, (own_up, sent_up)) = send(
        sent_b, head_grad, in_low, (own_up, sent_up)
    )
    down_b = total(own_b, got)
    all_b = gather(down_b)
    head_grad = after(head_grad, down_b)
    in_low = attend_back(qkv, head_grad, logsum, cosine, sine, in_low)
    kept, sent = answer(in_low, flat_in, part, seq_count // 2, tall)
    got, (kept, all_a) = send(sent_up, kept, all_a)
    up_grad = total(own_up, got)
    own_qkv, sent_qkv = outer(normed_all, after(in_low, up_grad), data_count, depth, three)
    all_up = gather(up_grad)
    summed = scatter_blocks(kept, sent)
    got, (summed, all_b) = send(sent_qkv, summed, all_b)
    qkv_grad = total(own_qkv, got)
    token_grad, gain_grad, shift_grad, branch_bias_grad = leave(
        tokens[0],
        norm_gain,
        summed,
        grad_output,
        branch_bias_grad,
        owner,
        data_count,
    )

    in_bias = jnp.sum(in_low.astype(wide), axis=0)
    small = jnp.concatenate(
        [in_bias, gain_grad[0], shift_grad[0], squares[None], branch_bias_grad[0]]
    )
    small = total_dp(small[None])[0]
    branch_bias_grad = small[-width:]
    small = small[:-width]
    lines = -(-small.size // three)
    lines += -lines % 8
    high = jnp.pad(small, (0, lines * three - small.size)).reshape(lines, three)
    first = lax.reduce_precision(high, 8, 7)
    beside = jnp.concatenate([qkv_grad, first.astype(low), (high - first).astype(low)])

    down_weight_grad, out_weight_grad = widen_rows(all_a, all_b, head_width, width)
    all_qkv = gather(after(beside, all_up))
    up_weight_grad = widen_columns(all_up, depth, 1)
    all_qkv = after(all_qkv, down_weight_grad, up_weight_grad)
    qkv_weight_grad = widen_columns(all_qkv, depth, 3)
    slots = all_qkv[:, depth:].astype(wide)
    slots = (slots[:, :lines] + slots[:, lines:]).reshape(seq_count, -1)
    norm_grads = jnp.sum(slots[:, inside : inside + 2 * width + 1], axis=0)
    qkv_bias_grad = slots[:, :three].reshape(seq_count, 3, head_width).transpose(1, 0, 2)
    up_bias_grad = slots[:, three:inside].reshape(-1)
    loss = norm_grads[-1] / (2.0 * width * count)
    return (
        loss,
        token_grad[None],
        norm_grads[:width],
        norm_grads[width : 2 * width],
        qkv_weight_grad,
        qkv_bias_grad.reshape(-1),
        out_weight_grad,
        branch_bias_grad,
        up_weight_grad,
        up_bias_grad,
        down_weight_grad,
        branch_bias_grad,
    )


def solution(mesh):
    placed = (
        P("dp", "seq", None),
        P("dp", "seq", None),
        P("dp", "seq"),
        P("dp", "seq"),
        P(),
        P(),
        P("dp", None),
        P(),
        P(None, "dp"),
        P(),
        P("dp", None),
        P(),
        P(None, "dp"),
        P(),
    )
    return jax.shard_map(
        local,
        mesh=mesh,
        in_specs=placed,
        out_specs=(
            P(),
            P("dp", "seq", None),
            P(),
            P(),
            P("dp", None),
            P(),
            P(None, "dp"),
            P(),
            P("dp", None),
            P(),
            P(None, "dp"),
            P(),
        ),
        check_vma=False,
    )
```

```python
import functools

import jax
import jax.numpy as jnp
from jax import lax
from jax.experimental import pallas as pl
from jax.experimental.pallas import tpu as pltpu
from jax.sharding import PartitionSpec as P

HEADS = 32
HEAD_DIM = 64
ROTARY = 32


norm_eps = 1e-05
rope_base = 10000.0
masked_fill = -1e30
LANES = 128
RADIX = 64
DIGIT = 16
SPARE = 16
ROWS = 64

low = jnp.bfloat16
wide = jnp.float32


def dot(a, b, dims):
    return lax.dot_general(a, b, (dims, ((), ())), preferred_element_type=wide)


def after(array, *earlier):
    return lax.optimization_barrier((array, *earlier))[0]


def swap(array, axis, bit):
    return lax.ppermute(array, axis, [(s, s ^ bit) for s in range(lax.axis_size(axis))])


def gather_seq(rows):
    return lax.all_gather(rows, "seq", axis=0, tiled=True)


def between(array, pairs):
    return lax.ppermute(
        array, "seq", [(2 * a + core, 2 * b + core) for a, b in pairs for core in range(2)]
    )


def scatter_chips(blocks):
    chips = len(blocks)
    if chips != 4:
        total = blocks[0]
        for k in range(1, chips):
            total = total + swap(blocks[k].astype(low), "seq", 2 * k).astype(wide)
        return total
    chip = lax.axis_index("seq") // 2
    far = between(blocks[3].astype(low), [(0, 1), (3, 2)])
    passed = (blocks[2] + far.astype(wide)).astype(low)
    upward = between(passed, [(0, 1), (1, 2)])
    downward = between(passed, [(3, 2), (2, 1)])
    upward = jnp.where(chip == 1, blocks[3], blocks[1]) + upward.astype(wide)
    downward = jnp.where(chip == 2, blocks[3], blocks[1]) + downward.astype(wide)
    upward = between(upward.astype(low), [(0, 1), (1, 2), (2, 3)])
    downward = between(downward.astype(low), [(3, 2), (2, 1), (1, 0)])
    return blocks[0] + upward.astype(wide) + downward.astype(wide)


def scatter_blocks(kept, sent):
    chips = lax.axis_size("seq") // 2
    rows = kept.shape[0] // chips
    chip = kept + swap(sent, "seq", 1).astype(wide)
    return scatter_chips([chip[k * rows : (k + 1) * rows] for k in range(chips)])


def scatter_seq(partial):
    return lax.psum_scatter(partial, "seq", scatter_dimension=0, tiled=True)


def total_dp(array):
    items = [array] + [swap(array, "dp", k) for k in range(1, lax.axis_size("dp"))]
    while len(items) > 1:
        items = [a + b for a, b in zip(items[::2], items[1::2])]
    return items[0]


def normalise(values):
    centre = values - jnp.mean(values, axis=-1, keepdims=True)
    spread = jnp.mean(centre * centre, axis=-1, keepdims=True)
    rstd = lax.rsqrt(spread + norm_eps)
    return centre * rstd, rstd


def enter_kernel(
    owners, owner, tokens, teacher, gain, shift, bias_a, bias_b, place, normed, base, held, kept
):
    inputs = tokens[...].astype(wide)
    xhat, _ = normalise(inputs)
    held[...] = xhat * gain[...].astype(wide)[None] + shift[...].astype(wide)[None]
    biases = (bias_a[...].astype(wide) + bias_b[...].astype(wide))[None]
    kept[...] = inputs + biases - teacher[...].astype(wide)
    width = inputs.shape[1]
    depth = width // owners
    for k in range(owners):
        theirs = pl.ds(pl.multiple_of((owner[0] ^ k) * depth, LANES), depth)
        normed[:, k * depth : (k + 1) * depth] = held[:, theirs].astype(low)
        base[:, k * depth : (k + 1) * depth] = kept[:, theirs]
    lane = lax.broadcasted_iota(jnp.int32, (inputs.shape[0], LANES), 1)
    ids = column_of(place[...]).astype(jnp.int32)
    facts = jnp.where(lane == 0, ids // RADIX, ids % RADIX)
    normed[:, width:] = facts.astype(wide).astype(low)


def enter(tokens, teacher, gain, shift, bias_a, bias_b, place, owner, owners):
    rows, width = tokens.shape
    whole = pl.BlockSpec(memory_space=pltpu.VMEM)
    return pl.pallas_call(
        functools.partial(enter_kernel, owners),
        in_specs=[pl.BlockSpec(memory_space=pltpu.SMEM)] + [whole] * 7,
        out_specs=[whole] * 2,
        out_shape=[
            jax.ShapeDtypeStruct((rows, width + LANES), low),
            jax.ShapeDtypeStruct((rows, width), wide),
        ],
        scratch_shapes=[pltpu.VMEM((rows, width), wide)] * 2,
        name="enter",
    )(
        owner[None],
        tokens,
        teacher,
        gain,
        shift,
        bias_a,
        bias_b,
        place,
    )


def column_of(row):
    size = row.shape[1]
    here = lax.broadcasted_iota(jnp.int32, (size, size), 0)
    there = lax.broadcasted_iota(jnp.int32, (size, size), 1)
    return jnp.sum(jnp.where(here == there, row.astype(wide), 0.0), axis=1, keepdims=True)


def grade_kernel(scale, branches, base, valid, grad, grad_low, sums):
    width = base.shape[1]
    lane = lax.broadcasted_iota(jnp.int32, (1, LANES), 1)
    weight = jnp.where(lane == 1, float(DIGIT), jnp.where(lane == 2, float(DIGIT * DIGIT), 1.0))
    digits = jnp.where(lane < 3, branches[:1, width:].astype(wide) * weight, 0.0)
    count = jnp.sum(digits, axis=1, keepdims=True)
    error = base[...] + branches[:, :width].astype(wide)
    weighted = column_of(valid[...]) * error
    squares = jnp.sum(jnp.sum(weighted * error, axis=0, keepdims=True), axis=1, keepdims=True)
    result = scale / count * weighted
    grad[...] = result
    grad_low[...] = result.astype(low)
    line = lax.broadcasted_iota(jnp.int32, sums.shape, 0)
    sums[...] = jnp.where(line == 0, squares, count)


def grade(branches, base, valid, scale):
    whole = pl.BlockSpec(memory_space=pltpu.VMEM)
    return pl.pallas_call(
        functools.partial(grade_kernel, scale),
        in_specs=[whole] * 3,
        out_specs=[whole] * 3,
        out_shape=[
            jax.ShapeDtypeStruct(base.shape, wide),
            jax.ShapeDtypeStruct(base.shape, low),
            jax.ShapeDtypeStruct((8, LANES), wide),
        ],
        cost_estimate=pl.CostEstimate(
            flops=4 * base.size, bytes_accessed=12 * base.size, transcendentals=0
        ),
        name="grade",
    )(branches, base, valid)


def leave_kernel(
    owners, owner, tokens, gain, summed, grad, bias, token_grad, gain_grad, shift_grad, bias_grad
):
    inputs = tokens[...].astype(wide)
    xhat, rstd = normalise(inputs)
    depth = inputs.shape[1] // owners
    for k in range(owners):
        theirs = pl.ds(pl.multiple_of((owner[0] ^ k) * depth, LANES), depth)
        token_grad[:, theirs] = summed[:, k * depth : (k + 1) * depth]
        bias_grad[:, theirs] = bias[:, k * depth : (k + 1) * depth]
    normed_grad = token_grad[...]
    gain_grad[...] = jnp.sum(normed_grad * xhat, axis=0, keepdims=True)
    shift_grad[...] = jnp.sum(normed_grad, axis=0, keepdims=True)
    scaled = normed_grad * gain[...].astype(wide)[None]
    token_grad[...] = rstd * (
        scaled
        - jnp.mean(scaled, axis=-1, keepdims=True)
        - xhat * jnp.mean(scaled * xhat, axis=-1, keepdims=True)
    )
    for k in range(owners):
        theirs = pl.ds(pl.multiple_of((owner[0] ^ k) * depth, LANES), depth)
        token_grad[:, theirs] += grad[:, k * depth : (k + 1) * depth]


def leave(tokens, gain, summed, grad, bias, owner, owners):
    rows, width = tokens.shape
    whole = pl.BlockSpec(memory_space=pltpu.VMEM)
    line = jax.ShapeDtypeStruct((1, width), wide)
    return pl.pallas_call(
        functools.partial(leave_kernel, owners),
        in_specs=[pl.BlockSpec(memory_space=pltpu.SMEM)] + [whole] * 5,
        out_specs=[whole] * 4,
        out_shape=[jax.ShapeDtypeStruct((rows, width), wide), line, line, line],
        name="leave",
    )(owner[None], tokens, gain, summed, grad, bias[None])


def pick_kernel(moves, part, counted, a, b, *refs):
    outs, arrived = refs[:2], refs[2]
    copies = []
    for which, source, half, target in moves:
        copies.append(
            pltpu.make_async_copy(
                (a, b)[which].at[source(part[0])],
                outs[half].at[target],
                arrived.at[len(copies)],
            )
        )
    for copy in copies:
        copy.start()
    tall = outs[0].shape[0]
    more = outs[1].shape[0] - tall
    if more:
        count = jnp.sum(counted[...].astype(wide), axis=1, keepdims=True)
        outs[1][tall:, :] = jnp.broadcast_to(count, (more, outs[1].shape[1])).astype(low)
    for copy in copies:
        copy.wait()


def pick(arrays, part, counted, moves, shapes):
    moved = 4 * sum(shape[0] * shape[1] for shape in shapes)
    return pl.pallas_call(
        functools.partial(pick_kernel, moves),
        in_specs=[
            pl.BlockSpec(memory_space=pltpu.SMEM),
            pl.BlockSpec(memory_space=pltpu.VMEM),
        ]
        + [pl.BlockSpec(memory_space=pl.ANY)] * 2,
        out_specs=[pl.BlockSpec(memory_space=pltpu.VMEM)] * 2,
        out_shape=[jax.ShapeDtypeStruct(shape, low) for shape in shapes],
        scratch_shapes=[pltpu.SemaphoreType.DMA((len(moves),))],
        cost_estimate=pl.CostEstimate(flops=0, bytes_accessed=moved, transcendentals=0),
        name="pick",
    )(part, counted, *arrays)


def gelu_parts(values):
    root = (2.0 / jnp.pi) ** 0.5
    square = values * values
    bent = jnp.tanh(root * (values + 0.044715 * (values * square)))
    factor = 0.5 * (1.0 + bent)
    slope = 0.5 * values * (1.0 - bent * bent) * (root * (1.0 + 3.0 * 0.044715 * square))
    return factor, factor + slope


def turn(values, cosine, sine):
    lane = lax.broadcasted_iota(jnp.int32, values.shape, 1) % HEAD_DIM
    half, width = ROTARY // 2, values.shape[1]
    partner = jnp.where(
        lane < half, pltpu.roll(values, width - half, 1), pltpu.roll(values, half, 1)
    )
    return values * cosine + partner * sine


def project_kernel(count, normed, cosine, sine, bias, *refs):
    weights, (qkv, hidden, stacked) = refs[:count], refs[count:]
    tile = pl.program_id(0)
    tall = normed.shape[1] // count
    total = bias[...]
    for k in range(count):
        block = normed[:, k * tall : (k + 1) * tall]
        total = total + jnp.dot(block, weights[k][...], preferred_element_type=wide)
    repeats = total.shape[1] // LANES

    @pl.when(tile < 2)
    def _():
        turned = turn(
            total,
            jnp.concatenate([cosine[...]] * repeats, axis=1),
            jnp.concatenate([sine[...]] * repeats, axis=1),
        )
        qkv[...] = turned.astype(low)

    @pl.when(tile == 2)
    def _():
        qkv[...] = total.astype(low)

    @pl.when(tile > 2)
    def _():
        hidden[...] = total
        stacked[...] = (total * gelu_parts(total)[0]).astype(low)


def project(normed, cosine, sine, bias, weights, tall, head_width):
    count = len(weights)
    length = normed.shape[0]
    inside = weights[0].shape[1]
    units = inside - 3 * head_width
    table = pl.BlockSpec((length, LANES), lambda t: (0, 0))
    return pl.pallas_call(
        functools.partial(project_kernel, count),
        grid=(inside // head_width,),
        in_specs=[
            pl.BlockSpec((length, count * tall), lambda t: (0, 0)),
            table,
            table,
            pl.BlockSpec((1, head_width), lambda t: (0, t)),
        ]
        + [pl.BlockSpec((tall, head_width), lambda t: (0, t))] * count,
        out_specs=[
            pl.BlockSpec((length, head_width), lambda t: (0, jnp.minimum(t, 2))),
            pl.BlockSpec((length, head_width), lambda t: (0, jnp.maximum(t - 3, 0))),
            pl.BlockSpec((length, head_width), lambda t: (0, jnp.maximum(t - 2, 1))),
        ],
        out_shape=[
            jax.ShapeDtypeStruct((length, 3 * head_width), low),
            jax.ShapeDtypeStruct((length, units), wide),
            jax.ShapeDtypeStruct((length, head_width + units), low),
        ],
        cost_estimate=pl.CostEstimate(
            flops=2 * length * count * tall * inside,
            bytes_accessed=2 * count * tall * (inside + length) + 8 * length * inside,
            transcendentals=length * units,
        ),
        name="project",
    )(normed, cosine, sine, bias, *weights)


def emit_kernel(owners, counts, stacked, *refs):
    counted, refs = refs[:counts], refs[counts:]
    weights, (out, slots, arrived) = refs[: 2 * owners], refs[-3:]
    middle, size = slots.shape[2:]
    step = pl.program_id(0)

    def fetch(n):
        columns = pl.ds(n % 2 * size, size)
        return [
            pltpu.make_async_copy(
                weights[n // 2 * 2 + half].at[:, columns],
                slots.at[n % 2, half],
                arrived.at[n % 2, half],
            )
            for half in range(2)
        ]

    @pl.when(step == 0)
    def _():
        for copy in fetch(0):
            copy.start()

    for n in range(2 * owners):

        @pl.when(step == n)
        def _(n=n):
            if n + 1 < 2 * owners:
                for copy in fetch(n + 1):
                    copy.start()
            for copy in fetch(n):
                copy.wait()

    @pl.when(step < 2 * owners)
    def _():
        slot = lax.rem(step, 2)
        total = jnp.dot(stacked[:, :middle], slots[slot, 0], preferred_element_type=wide)
        total = total + jnp.dot(stacked[:, middle:], slots[slot, 1], preferred_element_type=wide)
        out[...] = total.astype(low)

    if not counted:
        return

    @pl.when(step == 2 * owners)
    def _():
        count = counted[0][...].astype(wide)
        for ref in counted[1:]:
            count = count + ref[...].astype(wide)
        count = count[:1].astype(jnp.int32)
        lane = lax.broadcasted_iota(jnp.int32, count.shape, 1)
        digits = jnp.where(lane == 0, count, count // DIGIT)
        digits = jnp.where(lane == 2, count // (DIGIT * DIGIT), digits) % DIGIT
        out[:, :LANES] = jnp.broadcast_to(digits.astype(wide), (out.shape[0], LANES)).astype(low)


def emit(stacked, weights, counted, first, all_owners, into=None):
    owners = len(weights)
    length, behind = stacked.shape
    middle, depth = weights[0][0].shape
    size = depth // 2
    steps = 2 * owners + (first + owners == all_owners)

    row = size // SPARE
    operands = [stacked, *counted, *[item for pair in weights for item in pair]]
    in_specs = [pl.BlockSpec((length, behind), lambda t: (0, 0))]
    in_specs += [pl.BlockSpec((SPARE, LANES), lambda t: (row, 0))] * len(counted)
    in_specs += [pl.BlockSpec(memory_space=pl.ANY)] * (2 * owners)
    aliases = {}
    if into is not None:
        aliases = {len(operands): 0}
        operands.append(into)
        in_specs.append(pl.BlockSpec(memory_space=pl.ANY))
    return pl.pallas_call(
        functools.partial(emit_kernel, owners, len(counted)),
        grid=(steps,),
        in_specs=in_specs,
        out_specs=pl.BlockSpec((length, size), lambda t: (0, 2 * first + t)),
        out_shape=jax.ShapeDtypeStruct((length, all_owners * depth + LANES), low),
        input_output_aliases=aliases,
        scratch_shapes=[
            pltpu.VMEM((2, 2, middle, size), low),
            pltpu.SemaphoreType.DMA((2, 2)),
        ],
        cost_estimate=pl.CostEstimate(
            flops=2 * length * behind * owners * depth,
            bytes_accessed=2 * behind * (length + owners * depth) + 2 * length * steps * size,
            transcendentals=0,
        ),
        name="emit",
    )(*operands)


def scores_of(rows, keys, start):
    raw = lax.dot_general(rows, keys, (((1,), (1,)), ((), ())), preferred_element_type=wide)
    place = start + lax.broadcasted_iota(jnp.int32, raw.shape, 0)
    kept = lax.broadcasted_iota(jnp.int32, raw.shape, 1) <= place
    return jnp.where(kept, raw * HEAD_DIM ** (-0.5), masked_fill)


def by_blocks(length, head_width, step, body):
    pairs = head_width // LANES
    blocks = length // 2 // step
    for half in range(2):

        def one(n, carry, half=half):
            row = pl.multiple_of(half * (length // 2) + lax.rem(n, blocks) * step, step)
            body(row, pl.multiple_of(lax.div(n, blocks) * LANES, LANES), (half + 1) * length // 2)
            return carry

        lax.fori_loop(0, pairs * blocks, one, 0)


def attend_kernel(step, qkv, stacked, out, logsum):
    del stacked
    length, head_width = out.shape
    lane = lax.broadcasted_iota(jnp.int32, (step, LANES), 1)

    def body(row, at, last):
        rows = pl.ds(row, step)
        queries = qkv[rows, pl.ds(at, LANES)]
        keys = qkv[:last, pl.ds(head_width + at, LANES)]
        values = qkv[:last, pl.ds(2 * head_width + at, LANES)]
        sums = logsum[rows, :]
        outs = []
        for n, h in enumerate((slice(0, HEAD_DIM), slice(HEAD_DIM, LANES))):
            scores = scores_of(queries[:, h], keys[:, h], row)
            top = jnp.max(scores, axis=-1, keepdims=True)
            expd = jnp.exp(scores - top)
            total = jnp.sum(expd, axis=-1, keepdims=True)
            probs = (expd * (1.0 / total)).astype(low)
            outs.append(jnp.dot(probs, values[:, h], preferred_element_type=wide))
            sums = jnp.where(lane == at // HEAD_DIM + n, top + jnp.log(total), sums)
        out[rows, pl.ds(at, LANES)] = jnp.concatenate(outs, axis=1).astype(low)
        logsum[rows, :] = sums

    logsum[...] = jnp.zeros(logsum.shape, wide)
    by_blocks(length, head_width, step, body)


def attend(qkv, stacked):
    length, three = qkv.shape
    head_width = three // 3
    heads = head_width // HEAD_DIM
    whole = pl.BlockSpec(memory_space=pltpu.VMEM)
    return pl.pallas_call(
        functools.partial(attend_kernel, 256),
        grid=(1,),
        in_specs=[whole, pl.BlockSpec(memory_space=pl.ANY)],
        out_specs=[pl.BlockSpec((length, head_width), lambda n: (0, 0)), whole],
        out_shape=[
            jax.ShapeDtypeStruct(stacked.shape, low),
            jax.ShapeDtypeStruct((length, LANES), wide),
        ],
        input_output_aliases={1: 0},
        cost_estimate=pl.CostEstimate(
            flops=4 * heads * length * length * LANES,
            bytes_accessed=8 * length * three,
            transcendentals=heads * length * length,
        ),
        name="attend",
    )(qkv, stacked)


def attend_back_kernel(step, qkv, grad, logsum, cosine, sine, entered, out, gone):
    del entered
    length, head_width = grad.shape
    scale = HEAD_DIM ** (-0.5)
    over_rows = (((0,), (0,)), ((), ()))
    lane = lax.broadcasted_iota(jnp.int32, (step, LANES), 1)

    def body(row, at, last):
        rows = pl.ds(row, step)
        spots = [pl.ds(t * head_width + at, LANES) for t in range(3)]
        queries, keys, values = qkv[rows, spots[0]], qkv[:last, spots[1]], qkv[:last, spots[2]]
        upstreams = grad[rows, spots[0]]
        parts = [[], [], []]
        for n, h in enumerate((slice(0, HEAD_DIM), slice(HEAD_DIM, LANES))):
            sums = jnp.where(lane == at // HEAD_DIM + n, logsum[rows, :], 0.0)
            sums = jnp.sum(sums, axis=1, keepdims=True)
            probs = jnp.exp(scores_of(queries[:, h], keys[:, h], row) - sums)
            prob_grad = lax.dot_general(
                upstreams[:, h],
                values[:, h],
                (((1,), (1,)), ((), ())),
                preferred_element_type=wide,
            )
            inner = jnp.sum(probs * prob_grad, axis=-1, keepdims=True)
            score_grad = (probs * (prob_grad - inner)).astype(low)
            parts[0].append(jnp.dot(score_grad, keys[:, h], preferred_element_type=wide))
            parts[1].append(
                lax.dot_general(score_grad, queries[:, h], over_rows, preferred_element_type=wide)
            )
            parts[2].append(
                lax.dot_general(
                    probs.astype(low), upstreams[:, h], over_rows, preferred_element_type=wide
                )
            )
        parts = [jnp.concatenate(part, axis=1) for part in parts]
        gone[rows, spots[0]] = parts[0] * scale
        gone[:last, spots[1]] += parts[1] * scale
        gone[:last, spots[2]] += parts[2]

    gone[:, head_width:] = jnp.zeros((length, 2 * head_width), wide)
    by_blocks(length, head_width, step, body)

    def turn_back(n, carry):
        rows = pl.ds(pl.multiple_of(lax.rem(n, length // step) * step, step), step)
        at = pl.multiple_of(lax.div(n, length // step) * LANES, LANES)
        value = gone[rows, pl.ds(at, LANES)].astype(low).astype(wide)
        out[rows, pl.ds(at, LANES)] = turn(value, cosine[rows, :], -sine[rows, :]).astype(low)
        return carry

    lax.fori_loop(0, length // step * (2 * head_width // LANES), turn_back, 0)
    out[:, 2 * head_width :] = gone[:, 2 * head_width :].astype(low)


def attend_back(qkv, grad, logsum, cosine, sine, entered):
    length, three = qkv.shape
    head_width = three // 3
    heads = head_width // HEAD_DIM
    whole = pl.BlockSpec(memory_space=pltpu.VMEM)
    return pl.pallas_call(
        functools.partial(attend_back_kernel, 128),
        grid=(1,),
        in_specs=[whole] * 5 + [pl.BlockSpec(memory_space=pl.ANY)],
        out_specs=pl.BlockSpec((length, three), lambda n: (0, 0)),
        out_shape=jax.ShapeDtypeStruct(entered.shape, low),
        scratch_shapes=[
            pltpu.VMEM((length, three), wide),
        ],
        input_output_aliases={5: 0},
        cost_estimate=pl.CostEstimate(
            flops=10 * heads * length * length * LANES,
            bytes_accessed=8 * length * three,
            transcendentals=heads * length * length,
        ),
        name="attend_back",
    )(qkv, grad, logsum, cosine, sine, entered)


def reject_kernel(count, hidden, grads, *refs):
    weights, (head_grad, entered) = refs[:count], refs[count:]
    depth = weights[0].shape[1]
    over = (((1,), (1,)), ((), ()))
    total = lax.dot_general(grads[:, :depth], weights[0][...], over, preferred_element_type=wide)
    for k in range(1, count):
        total = total + lax.dot_general(
            grads[:, k * depth : (k + 1) * depth],
            weights[k][...],
            over,
            preferred_element_type=wide,
        )

    @pl.when(pl.program_id(0) == 0)
    def _():
        head_grad[...] = total.astype(low)

    @pl.when(pl.program_id(0) > 0)
    def _():
        entered[...] = (total * gelu_parts(hidden[...])[1]).astype(low)


def reject(grads, weights, hidden, head_width):
    count = len(weights)
    length = grads.shape[0]
    behind, depth = weights[0].shape
    inside = behind + 2 * head_width
    return pl.pallas_call(
        functools.partial(reject_kernel, count),
        grid=(behind // head_width,),
        in_specs=[pl.BlockSpec((length, head_width), lambda t: (0, jnp.maximum(t - 1, 0)))]
        + [pl.BlockSpec((length, count * depth), lambda t: (0, 0))]
        + [pl.BlockSpec((head_width, depth), lambda t: (t, 0))] * count,
        out_specs=[
            pl.BlockSpec((length, head_width), lambda t: (0, 0)),
            pl.BlockSpec((length, head_width), lambda t: (0, jnp.maximum(t + 2, 3))),
        ],
        out_shape=[
            jax.ShapeDtypeStruct((length, head_width), low),
            jax.ShapeDtypeStruct((length, inside), low),
        ],
        cost_estimate=pl.CostEstimate(
            flops=2 * length * count * depth * behind,
            bytes_accessed=2 * count * depth * (behind + length) + 8 * length * behind,
            transcendentals=length * behind,
        ),
        name="reject",
    )(hidden, grads, *weights)


def sort_blocks(held, part, chips, kept, sent):
    rows = kept.shape[0] // chips
    for k in range(chips):
        here = slice(k * rows, (k + 1) * rows)
        for core, out in enumerate((kept, sent)):
            block = part ^ (2 * k + core)
            source = pl.ds(pl.multiple_of(block * rows, rows), rows)
            out[here, :] = held[source, :].astype(out.dtype)


def outer_kernel(left, right, *outs):
    total = lax.dot_general(
        left[...], right[...], (((0,), (0,)), ((), ())), preferred_element_type=wide
    )
    for n, out in enumerate(outs):

        @pl.when(pl.program_id(0) == n)
        def _(out=out):
            out[...] = total.astype(out.dtype)


def outer(left, right, count, left_size, right_size):
    length = left.shape[0]
    left_step = int(left.shape[1] >= count * left_size)
    flops = 2 * length * count * left_size * right_size
    kinds = [wide] + [low] * (count - 1)
    results = pl.pallas_call(
        outer_kernel,
        grid=(count,),
        in_specs=[
            pl.BlockSpec((length, left_size), lambda k: (0, k * left_step)),
            pl.BlockSpec((length, right_size), lambda k: (0, k * (1 - left_step))),
        ],
        out_specs=[pl.BlockSpec((left_size, right_size), lambda k: (0, 0))] * count,
        out_shape=[jax.ShapeDtypeStruct((left_size, right_size), kind) for kind in kinds],
        cost_estimate=pl.CostEstimate(
            flops=flops, bytes_accessed=flops // length, transcendentals=0
        ),
        name="outer",
    )(left, right)
    return results[0], list(results[1:])


def answer_kernel(count, chips, part, entered, *refs):
    weights, (kept, sent, held, slots, arrived) = refs[:count], refs[count:]
    tall = slots.shape[1]
    step = pl.program_id(0)

    def fetch(n):
        return pltpu.make_async_copy(
            weights[n].at[pl.ds(0, tall)], slots.at[n % 2], arrived.at[n % 2]
        )

    @pl.when(step == 0)
    def _():
        fetch(0).start()

    for n in range(count):

        @pl.when(step == n)
        def _(n=n):
            if n + 1 < count:
                fetch(n + 1).start()
            fetch(n).wait()

    held[...] = lax.dot_general(
        entered[...],
        slots[lax.rem(step, 2)],
        (((1,), (1,)), ((), ())),
        preferred_element_type=wide,
    )
    sort_blocks(held, part[0], chips, kept, sent)


def answer(entered, pieces, part, chips, tall):
    count = len(pieces)
    length, inside = entered.shape
    half = length // 2
    return pl.pallas_call(
        functools.partial(answer_kernel, count, chips),
        grid=(count,),
        in_specs=[
            pl.BlockSpec(memory_space=pltpu.SMEM),
            pl.BlockSpec((length, inside), lambda t: (0, 0)),
        ]
        + [pl.BlockSpec(memory_space=pl.ANY)] * count,
        out_specs=[pl.BlockSpec((half, tall), lambda t: (0, t))] * 2,
        out_shape=[
            jax.ShapeDtypeStruct((half, count * tall), wide),
            jax.ShapeDtypeStruct((half, count * tall), low),
        ],
        scratch_shapes=[
            pltpu.VMEM((length, tall), wide),
            pltpu.VMEM((2, tall, inside), low),
            pltpu.SemaphoreType.DMA((2,)),
        ],
        cost_estimate=pl.CostEstimate(
            flops=2 * length * inside * count * tall,
            bytes_accessed=2 * inside * (length + count * tall) + 3 * length * count * tall,
            transcendentals=0,
        ),
        name="answer",
    )(part[None], entered, *pieces)


def widen_rows_kernel(head_width, a, b, down, out):
    cut = b.shape[1] - head_width
    out[...] = b[0, :head_width].astype(wide)
    down[:cut] = b[0, head_width:].astype(wide)
    down[cut:] = a[0].astype(wide)


def widen_rows(all_a, all_b, head_width, width):
    count, rest, depth = all_a.shape
    tall = all_b.shape[1]
    units = rest + tall - head_width
    return pl.pallas_call(
        functools.partial(widen_rows_kernel, head_width),
        grid=(count,),
        in_specs=[
            pl.BlockSpec((1, rest, depth), lambda j: (j, 0, 0)),
            pl.BlockSpec((1, tall, depth), lambda j: (j, 0, 0)),
        ],
        out_specs=[
            pl.BlockSpec((units, depth), lambda j: (j, 0)),
            pl.BlockSpec((head_width, depth), lambda j: (j, 0)),
        ],
        out_shape=[
            jax.ShapeDtypeStruct((count * units, depth), wide),
            jax.ShapeDtypeStruct((width, depth), wide),
        ],
        cost_estimate=pl.CostEstimate(
            flops=0, bytes_accessed=6 * count * depth * (rest + tall), transcendentals=0
        ),
        name="widen_rows",
    )(all_a, all_b)


def widen_columns_kernel(groups, gathered, out):
    count, _, columns = gathered.shape
    size = columns // groups
    for j in range(count):
        for g in range(groups):
            at = (g * count + j) * size
            out[:, at : at + size] = gathered[j, :, g * size : (g + 1) * size].astype(wide)


def widen_columns(gathered, rows, groups):
    count, _, columns = gathered.shape
    tall = min(128, rows)
    moved = 6 * count * rows * columns
    return pl.pallas_call(
        functools.partial(widen_columns_kernel, groups),
        grid=(rows // tall,),
        in_specs=[pl.BlockSpec((count, tall, columns), lambda r: (0, r, 0))],
        out_specs=pl.BlockSpec((tall, count * columns), lambda r: (r, 0)),
        out_shape=jax.ShapeDtypeStruct((rows, count * columns), wide),
        cost_estimate=pl.CostEstimate(flops=0, bytes_accessed=moved, transcendentals=0),
        name="widen_columns",
    )(gathered)


def local(
    tokens,
    teacher,
    valid,
    positions,
    norm_gain,
    norm_bias,
    qkv_weight,
    qkv_bias,
    out_weight,
    out_bias,
    up_weight,
    up_bias,
    down_weight,
    down_bias,
):
    rows_here, width = tokens.shape[1:]
    seq_count = lax.axis_size("seq")
    data_count = lax.axis_size("dp")
    part = lax.axis_index("seq")
    owner = lax.axis_index("dp")
    length = rows_here * seq_count
    head_width = HEADS // seq_count * HEAD_DIM
    three = 3 * head_width
    units = up_weight.shape[1] // seq_count
    inside = three + units
    depth = qkv_weight.shape[0]

    tall = depth // 2
    behind = head_width + units

    def span(start, size, unit):
        return pl.ds(start if isinstance(start, int) else pl.multiple_of(start, unit), size)

    def block_at(row, rows, column, columns):
        return span(row, rows, ROWS), span(column, columns, LANES)

    moves = []
    for half in range(2):
        for t in range(3):
            moves.append(
                (
                    0,
                    lambda part, t=t, half=half: block_at(
                        half * tall, tall, t * width + part * head_width, head_width
                    ),
                    half,
                    block_at(0, tall, t * head_width, head_width),
                )
            )
        moves.append(
            (
                1,
                lambda part, half=half: block_at(half * tall, tall, part * units, units),
                half,
                block_at(0, tall, three, units),
            )
        )
    w_in = pick(
        (qkv_weight, up_weight),
        part[None],
        valid,
        moves,
        [(tall, inside), (tall + SPARE, inside)],
    )
    normed_low, base = enter(
        tokens[0],
        teacher[0],
        norm_gain,
        norm_bias,
        out_bias,
        down_bias,
        positions,
        after(owner, *w_in),
        data_count,
    )

    rest = behind // 2 - head_width
    moves = [
        (
            0,
            lambda part: block_at(part * head_width, head_width, 0, depth),
            0,
            block_at(0, head_width, 0, depth),
        ),
        (
            1,
            lambda part: block_at(part * units, rest, 0, depth),
            0,
            block_at(head_width, rest, 0, depth),
        ),
        (
            1,
            lambda part: block_at(part * units + rest, units - rest, 0, depth),
            1,
            block_at(0, units - rest, 0, depth),
        ),
    ]
    w_back = pick(
        (out_weight, down_weight),
        after(part[None], normed_low),
        valid,
        moves,
        [(behind // 2, depth)] * 2,
    )
    if data_count == 4:
        sides = [tuple(swap(item, "dp", k) for item in w_in) for k in (1, 2)]
        last_in = swap(sides[0][0], "dp", 2), swap(sides[1][1], "dp", 1)
        first_in = [w_in, *sides]
        w_back = lax.optimization_barrier((*w_back, *last_in))[:2]
        back_sides = [tuple(swap(item, "dp", k) for item in w_back) for k in (1, 2)]
    else:
        w_in = [w_in] + [tuple(swap(item, "dp", k) for item in w_in) for k in range(1, data_count)]
        w_back = [w_back] + [
            tuple(swap(item, "dp", k) for item in w_back) for k in range(1, data_count)
        ]
        first_in, last_in = w_in[:-1], w_in[-1]
    normed_all = gather_seq(normed_low)
    facts = normed_all[:, width : width + 2].astype(jnp.int32)
    where = facts[:, 0] * RADIX + facts[:, 1]

    half = ROTARY // 2
    lane = jnp.arange(LANES, dtype=jnp.int32) % HEAD_DIM
    freqs = rope_base ** (-((lane % half).astype(wide) * 2.0) / ROTARY)
    angles = where.astype(wide)[:, None] * jnp.where(lane < ROTARY, freqs, 0.0)[None, :]
    cosine = jnp.cos(angles)
    sine = jnp.sin(angles) * jnp.where(lane < half, -1.0, 1.0)[None, :]

    b_in = jnp.concatenate(
        [
            lax.dynamic_slice_in_dim(qkv_bias, t * width + part * head_width, head_width, 0)
            for t in range(3)
        ]
        + [lax.dynamic_slice_in_dim(up_bias, part * units, units, 0)]
    ).astype(wide)[None]

    def piece(array, k):
        return array[:, k * depth : (k + 1) * depth]

    flat_in = [item for pair in (*first_in, last_in) for item in pair]
    qkv, hidden, stacked = project(normed_all, cosine, sine, b_in, flat_in, tall, head_width)
    stacked, logsum = attend(qkv, stacked)

    counted = [item[1] for item in (*first_in, last_in)]
    if data_count == 4:
        back_sides = [tuple(after(item, stacked) for item in pair) for pair in back_sides]
        w_back = [w_back, *back_sides]
        w_back.append((swap(back_sides[0][0], "dp", 2), swap(back_sides[1][1], "dp", 1)))
    branches = emit(stacked, w_back[:-1], [], 0, data_count)
    branches = emit(stacked, w_back[-1:], counted, data_count - 1, data_count, branches)
    w_back = [jnp.concatenate(pair, axis=0) for pair in w_back]
    branches, *w_back = lax.optimization_barrier((scatter_seq(branches), *w_back))
    grad_output, grad_low, sums = grade(branches, base, valid, float(length * data_count))
    squares, count = sums[0, 0], sums[1, 0]
    grad_all = gather_seq(grad_low)
    branch_bias_grad = jnp.sum(grad_all.astype(wide), axis=0)

    def owned(left, right):
        return dot(left, right, ((0,), (0,)))

    def gather(array):
        return lax.all_gather(array, "seq", axis=0, tiled=False)

    cut = units // 2 // LANES * LANES

    def of_stacked(first, last):
        return [owned(stacked[:, first:last], piece(grad_all, k)) for k in range(data_count)]

    def prepare(pieces):
        return pieces[0], [item.astype(low) for item in pieces[1:]]

    def send(sent, *meanwhile):
        got = [swap(item, "dp", k + 1) for k, item in enumerate(sent)]
        held = lax.optimization_barrier((*got, *jax.tree.leaves(meanwhile)))
        return held[: len(got)], jax.tree.unflatten(jax.tree.structure(meanwhile), held[len(got) :])

    def total(own, got):
        for item in got:
            own = own + item.astype(wide)
        return own.astype(low)

    own_a, sent_a = prepare(of_stacked(head_width + cut, head_width + units))
    own_b, sent_b = outer(stacked, grad_all, data_count, head_width + cut, depth)
    got, ((own_b, sent_b),) = send(sent_a, (own_b, sent_b))
    down_a = total(own_a, got)
    all_a = gather(down_a)
    head_grad, in_low = reject(after(grad_all, down_a), w_back, hidden, head_width)
    own_up, sent_up = outer(normed_all, in_low[:, three:], data_count, depth, units)
    got, (head_grad, in_low, (own_up, sent_up)) = send(
        sent_b, head_grad, in_low, (own_up, sent_up)
    )
    down_b = total(own_b, got)
    all_b = gather(down_b)
    head_grad = after(head_grad, down_b)
    in_low = attend_back(qkv, head_grad, logsum, cosine, sine, in_low)
    kept, sent = answer(in_low, flat_in, part, seq_count // 2, tall)
    got, (kept, all_a) = send(sent_up, kept, all_a)
    up_grad = total(own_up, got)
    own_qkv, sent_qkv = outer(normed_all, after(in_low, up_grad), data_count, depth, three)
    all_up = gather(up_grad)
    summed = scatter_blocks(kept, sent)
    got, (summed, all_b) = send(sent_qkv, summed, all_b)
    qkv_grad = total(own_qkv, got)
    token_grad, gain_grad, shift_grad, branch_bias_grad = leave(
        tokens[0],
        norm_gain,
        summed,
        grad_output,
        branch_bias_grad,
        owner,
        data_count,
    )

    in_bias = jnp.sum(in_low.astype(wide), axis=0)
    small = jnp.concatenate(
        [in_bias, gain_grad[0], shift_grad[0], squares[None], branch_bias_grad[0]]
    )
    small = total_dp(small[None])[0]
    branch_bias_grad = small[-width:]
    small = small[:-width]
    lines = -(-small.size // three)
    lines += -lines % 8
    high = jnp.pad(small, (0, lines * three - small.size)).reshape(lines, three)
    first = lax.reduce_precision(high, 8, 7)
    beside = jnp.concatenate([qkv_grad, first.astype(low), (high - first).astype(low)])

    down_weight_grad, out_weight_grad = widen_rows(all_a, all_b, head_width, width)
    all_qkv = gather(beside)
    up_weight_grad = widen_columns(all_up, depth, 1)
    all_qkv = after(all_qkv, down_weight_grad, up_weight_grad)
    qkv_weight_grad = widen_columns(all_qkv, depth, 3)
    slots = all_qkv[:, depth:].astype(wide)
    slots = (slots[:, :lines] + slots[:, lines:]).reshape(seq_count, -1)
    norm_grads = jnp.sum(slots[:, inside : inside + 2 * width + 1], axis=0)
    qkv_bias_grad = slots[:, :three].reshape(seq_count, 3, head_width).transpose(1, 0, 2)
    up_bias_grad = slots[:, three:inside].reshape(-1)
    loss = norm_grads[-1] / (2.0 * width * count)
    return (
        loss,
        token_grad[None],
        norm_grads[:width],
        norm_grads[width : 2 * width],
        qkv_weight_grad,
        qkv_bias_grad.reshape(-1),
        out_weight_grad,
        branch_bias_grad,
        up_weight_grad,
        up_bias_grad,
        down_weight_grad,
        branch_bias_grad,
    )


def solution(mesh):
    placed = (
        P("dp", "seq", None),
        P("dp", "seq", None),
        P("dp", "seq"),
        P("dp", "seq"),
        P(),
        P(),
        P("dp", None),
        P(),
        P(None, "dp"),
        P(),
        P("dp", None),
        P(),
        P(None, "dp"),
        P(),
    )
    return jax.shard_map(
        local,
        mesh=mesh,
        in_specs=placed,
        out_specs=(
            P(),
            P("dp", "seq", None),
            P(),
            P(),
            P("dp", None),
            P(),
            P(None, "dp"),
            P(),
            P("dp", None),
            P(),
            P(None, "dp"),
            P(),
        ),
        check_vma=False,
    )
```
